32 devices in a mesh: ctx: 8 (over y, x, core), tp: 4 (over z).
Axes of the slice: x: 2, y: 2, z: 4, core: 2. Of those that a mesh axis runs over, the one named last changes fastest.
Arguments:
- tokens: bfloat16 [4096, 2048], P(('ctx', 'tp')), may hold values from -8 to 8
- projection: bfloat16 [2048, 640], P(None, 'tp'), may hold values from -0.125 to 0.125
- conv_weight: float32 [4, 640], P(None, 'tp'), may hold values from -2.5 to 2.5
Outputs:
- attended: bfloat16 [4096, 512], P('ctx', 'tp')
The draws below stay inside these ranges and needn't reach their ends.
All inputs are finite; a program needn't handle non-finite values.
Results may differ from the reference program's by a relative error of at most 0.0032.
The reference program's roundings to bfloat16 on the way (of `projected` and `values`) count: a program that leaves them out, or rounds other values in their place, can miss the bound.
Values may be sent and summed in bfloat16 or wider, within the bound.
No kernel may reach another device: no remote copies, remote signals or barrier semaphores. Data moves between devices by JAX's collectives and lax.ppermute only.
A program may use at most 64 MiB of HBM per device.

```python
import math
import jax
import jax.numpy as jnp
from jax import lax

D = 2048
FEAT = 16
VW = 128
KERNEL = 4
HEADS = 4
PHI = 273
BLOCK = 512
TOKENS = 4096


def draw_tokens(key, part):
    key_noise, key_segment, key_common = jax.random.split(jax.random.fold_in(key, 7), 3)
    seg_len = 16
    noise = jnp.clip(jax.random.normal(key_noise, (TOKENS, D), jnp.float32), -4.0, 4.0)
    segment_mean = 0.8 * jnp.clip(jax.random.normal(key_segment, (TOKENS // seg_len, D), jnp.float32), -3.0, 3.0)
    common_mean = 0.5 * jnp.clip(jax.random.normal(key_common, (1, D), jnp.float32), -2.0, 2.0)
    values = noise + jnp.repeat(segment_mean, seg_len, axis=0) + common_mean
    return jnp.clip(values, -8.0, 8.0).astype(jnp.bfloat16)


def level_of(own_key, extent, shards, low, top_value):
    def one(position, blocks):
        steps = jax.random.uniform(jax.random.fold_in(jax.random.fold_in(own_key, 6), position), (blocks,), jnp.float32, low / len(shards), top_value / len(shards))
        return jnp.repeat(jnp.exp(steps), extent[position] // blocks).reshape((-1,) + (1,) * (len(extent) - position - 1))

    gain = one(*shards[0])
    for cut in shards[1:]:
        gain = gain * one(*cut)
    return gain


def gaussian(own_key, extent, scale, limit, cuts=(), dtype=jnp.bfloat16):
    array = scale * jax.random.normal(own_key, extent, jnp.float32)
    if cuts:
        array = array * level_of(own_key, extent, cuts, -0.22, 0.18)
    return jnp.clip(array, -limit, limit).astype(dtype)


def setup_inputs(seed: int = 0) -> dict:
    streams_of = jax.random.split(jax.random.key(seed), 4)
    tokens = draw_tokens(jax.random.fold_in(streams_of[3], 71), 0)
    projection = gaussian(streams_of[1], (D, HEADS * (2 * FEAT + VW)), D ** -0.5, 0.125, ((1, 4),))
    conv_weight = gaussian(streams_of[2], (KERNEL, HEADS * (2 * FEAT + VW)), 0.5, 2.5, ((1, 4),), jnp.float32)
    return dict(tokens=tokens, projection=projection, conv_weight=conv_weight)


def taylor(raw_vals):
    width_feat = raw_vals.shape[-1]
    linear = raw_vals * width_feat ** (-0.25)
    quadratic = raw_vals[..., :, None] * raw_vals[..., None, :]
    quadratic = quadratic.reshape(raw_vals.shape[:-1] + (width_feat * width_feat,))
    quadratic = quadratic * (1.0 / (math.sqrt(2.0) * math.sqrt(width_feat)))
    ones_col = jnp.ones(raw_vals.shape[:-1] + (1,), jnp.float32)
    return jnp.concatenate([ones_col, linear, quadratic], axis=-1).astype(jnp.bfloat16)

def reference(tokens, projection, conv_weight):
    row_width = 2 * FEAT + VW
    conv_lag = KERNEL - 1
    num_blocks = TOKENS // BLOCK
    token_blocks = tokens.reshape(num_blocks, BLOCK, D)
    causal = jnp.arange(BLOCK)[:, None] >= jnp.arange(BLOCK)[None, :]
    highest = lax.Precision.HIGHEST

    def block_step(carried, block_rows):
        tail_rows, run_state, run_total = carried
        projected = jnp.dot(block_rows, projection, preferred_element_type=jnp.float32).astype(jnp.bfloat16)
        padded = jnp.concatenate([tail_rows, projected], axis=0).astype(jnp.float32)
        convolved = jnp.zeros((BLOCK, HEADS * row_width), jnp.float32)
        for offset in range(KERNEL):
            convolved = convolved + conv_weight[offset] * padded[conv_lag - offset:conv_lag - offset + BLOCK]
        convolved = convolved.reshape(BLOCK, HEADS, row_width)
        feat_query = taylor(convolved[:, :, :FEAT]).astype(jnp.float32)
        feat_key = taylor(convolved[:, :, FEAT:2 * FEAT]).astype(jnp.float32)
        values = convolved[:, :, 2 * FEAT:].astype(jnp.bfloat16).astype(jnp.float32)
        scores = jnp.einsum('ihp,jhp->hij', feat_query, feat_key, precision=highest)
        scores = jnp.where(causal[None], scores, jnp.float32(0.0))
        rounded = lax.optimization_barrier(scores.astype(jnp.bfloat16)).astype(jnp.float32)
        numerator = jnp.einsum('hij,jhv->ihv', rounded, values, precision=highest)
        denominator = jnp.transpose(lax.optimization_barrier(jnp.sum(scores, axis=2)))
        numerator = numerator + jnp.einsum('ihp,hpv->ihv', feat_query, run_state, precision=highest)
        denominator = denominator + jnp.einsum('ihp,hp->ih', feat_query, run_total, precision=highest)
        run_state = run_state + jnp.einsum('jhp,jhv->hpv', feat_key, values, precision=highest)
        run_total = run_total + lax.optimization_barrier(jnp.sum(feat_key, axis=0))
        attended = (numerator / denominator[:, :, None]).astype(jnp.bfloat16).reshape(BLOCK, HEADS * VW)
        return ((projected[BLOCK - conv_lag:], run_state, run_total), attended)
    initial = (jnp.zeros((conv_lag, HEADS * row_width), jnp.bfloat16), jnp.zeros((HEADS, PHI, VW), jnp.float32), jnp.zeros((HEADS, PHI), jnp.float32))
    _, outputs = lax.scan(block_step, initial, token_blocks)
    return outputs.reshape(TOKENS, HEADS * VW)
```

```python
import functools
import math

import jax
import jax.numpy as jnp
from jax import lax
from jax.experimental import pallas as pl
from jax.experimental.pallas import tpu as pltpu
from jax.sharding import PartitionSpec as P

FEAT = 16
QUAD = 4
HALO = 8
QUAD_FEATS = FEAT * (FEAT + 1) // 2
NUM_FEAT = QUAD_FEATS + FEAT + 8
STATE_ROWS = NUM_FEAT + 8
BLOCK = 512
F32 = jnp.float32
BF16 = jnp.bfloat16
VMEM = pl.BlockSpec(memory_space=pltpu.VMEM)
SMEM = pl.BlockSpec(memory_space=pltpu.SMEM)


def cost(flops, moved):
    return pl.CostEstimate(flops=flops, bytes_accessed=moved, transcendentals=0)


def project_kernel(half_ref, own, core, along, corner, near, far, *outs):
    depth = near.shape[0]
    first = pl.multiple_of(half_ref[0] * depth, depth)
    second = pl.multiple_of(depth - half_ref[0] * depth, depth)
    for rows, out in zip((own, core, along, corner), outs):
        total = jnp.dot(rows[:, pl.ds(first, depth)], near[...], preferred_element_type=F32)
        total += jnp.dot(rows[:, pl.ds(second, depth)], far[...], preferred_element_type=F32)
        out[...] = total.astype(BF16)


def features(raw, weighted):
    scale = 1.0 / (math.sqrt(2.0) * math.sqrt(FEAT))
    parts = []
    for shift in range(FEAT // 2 + 1):
        pair = raw * (pltpu.roll(raw, shift, 0) if shift else raw) * scale
        if shift == FEAT // 2:
            pair = pair[: FEAT // 2]
        pair = pair.astype(BF16).astype(F32)
        parts.append(pair * 2.0 if weighted and shift else pair)
    parts.append(raw * FEAT ** (-0.25))
    row = lax.broadcasted_iota(jnp.int32, (8, raw.shape[1]), 0)
    parts.append(jnp.where(row == 0, 1.0, 0.0).astype(F32))
    return jnp.concatenate(parts, axis=0).astype(BF16)


def feature_kernel(place_ref, conv_ref, *refs):
    count = place_ref.shape[0]
    blocks = refs[:count]
    query_ref, key_ref, value_ref, state_ref, wide = refs[count:]
    rows = blocks[0].shape[0] - HALO
    kernel_len = conv_ref.shape[0]
    local_rows = rows * count
    for index, block in enumerate(blocks):
        place = place_ref[index]
        start = pl.multiple_of(HALO + place * rows, 8)
        wide[pl.ds(start, rows), :] = block[HALO:, :].astype(F32)

        @pl.when(place == 0)
        def _():
            wide[:HALO, :] = block[:HALO, :].astype(F32)

    convolved = jnp.zeros((local_rows, wide.shape[1]), F32)
    for offset in range(kernel_len):
        convolved += conv_ref[offset : offset + 1, :] * wide[HALO - offset : HALO - offset + local_rows, :]
    value = convolved[:, 2 * FEAT :].astype(BF16)
    value_ref[...] = value
    raw = convolved[:, : 2 * FEAT].T
    query = features(raw[:FEAT], False)
    query_ref[...] = query.T
    key = features(raw[FEAT:], True)
    key_ref[...] = key
    state_ref[:NUM_FEAT, :] = jnp.dot(key, value, preferred_element_type=F32)
    ones = jnp.ones((8, local_rows), BF16)
    total = lax.dot_general(ones, key, (((1,), (1,)), ((), ())), preferred_element_type=F32)
    width = state_ref.shape[1]
    rest = NUM_FEAT - width
    padded = jnp.concatenate([total[1:2, width:], jnp.zeros((1, width - rest), F32)], axis=1)
    row = lax.broadcasted_iota(jnp.int32, (8, width), 0)
    state_ref[NUM_FEAT:, :] = jnp.where(row == 0, total[:, :width], jnp.where(row == 1, padded, 0.0))


def inner_kernel(query_ref, key_ref, value_ref, numerator_ref, denominator_ref):
    local_rows = query_ref.shape[0]
    width = value_ref.shape[1]
    step = 128
    for start in range(0, local_rows, step):
        size = start + step
        scores = jnp.dot(query_ref[start:size, :], key_ref[:, :size], preferred_element_type=F32)
        row = lax.broadcasted_iota(jnp.int32, (step, size), 0) + start
        column = lax.broadcasted_iota(jnp.int32, (step, size), 1)
        scores = jnp.where(row >= column, scores, 0.0)
        numerator_ref[start:size, :] = jnp.dot(
            scores.astype(BF16), value_ref[:size, :], preferred_element_type=F32
        )
        denominator_ref[start:size, :] = jnp.broadcast_to(
            jnp.sum(scores, axis=1, keepdims=True), (step, width)
        )


def finish_kernel(query_ref, numerator_ref, denominator_ref, *refs):
    states, out_ref = refs[:-1], refs[-1]
    state = states[0][...]
    for other in states[1:]:
        state += other[...]
    width = numerator_ref.shape[1]
    query = query_ref[...]
    rest = state[:NUM_FEAT, :]
    numerator = numerator_ref[...]
    for _ in range(3):
        part = rest.astype(BF16)
        rest = rest - part.astype(F32)
        numerator += jnp.dot(query, part, preferred_element_type=F32)
    totals = jnp.concatenate(
        [state[NUM_FEAT : NUM_FEAT + 1, :], state[NUM_FEAT + 1 : NUM_FEAT + 2, : NUM_FEAT - width]], axis=1
    )
    denominator = denominator_ref[:, :1] + jnp.sum(query.astype(F32) * totals, axis=1, keepdims=True)
    out_ref[...] = (numerator / denominator).astype(BF16)


def head_at(tp, z, offset):
    return z ^ offset if tp & (tp - 1) == 0 else (z + offset) % tp


def plane_of(tp, head, offset):
    return head ^ offset if tp & (tp - 1) == 0 else (head - offset) % tp


def offset_of(place, turn):
    return ((place & 1) << 1 | (place >> 1 & 1)) + QUAD * turn


def per_device(ctx, tp, tokens, projection, conv_weight):
    both = ("ctx", "tp")
    rows, depth = tokens.shape
    half = depth // 2
    row_width = projection.shape[1]
    val_width = row_width - 2 * FEAT
    turns = tp // QUAD
    me = lax.axis_index("ctx")
    head = lax.axis_index("tp")
    upper = me // QUAD % 2

    def swap(array, bit):
        return lax.ppermute(array, "ctx", [(i, i ^ bit) for i in range(ctx)])

    tail = lax.ppermute(
        tokens[rows - HALO :], both, [((c - 1) * tp + tp - 1, c * tp) for c in range(1, ctx)]
    )
    mine = lax.dynamic_slice(projection, (upper * half, 0), (half, row_width))
    near = []
    for turn in range(turns):
        pairs = []
        for c in range(ctx):
            for z in range(tp):
                pairs.append((c * tp + head_at(tp, z, offset_of(c % QUAD, turn)), c * tp + z))
        near.append(lax.ppermute(mine, both, pairs))
    own = jnp.concatenate([tail, tokens], axis=0)
    along = swap(own, 2)
    core = swap(own, 1)
    far = [swap(part, QUAD) for part in near]
    corner = swap(along, 1)
    side = upper.astype(jnp.int32).reshape(1)
    blocks, places = [], []
    for turn in range(turns):
        projected = pl.pallas_call(
            project_kernel,
            out_shape=[jax.ShapeDtypeStruct((rows + HALO, row_width), BF16)] * QUAD,
            in_specs=[SMEM] + [VMEM] * 6,
            out_specs=[VMEM] * QUAD,
            cost_estimate=cost(2 * QUAD * rows * depth * row_width, QUAD * rows * depth * 2 + depth * row_width * 2),
        )(side, own, core, along, corner, near[turn], far[turn])
        for shift in range(QUAD):
            pairs = []
            for c in range(ctx):
                for z in range(tp):
                    pairs.append((c * tp + z, (c ^ shift) * tp + head_at(tp, z, offset_of(c % QUAD, turn))))
            blocks.append(lax.ppermute(projected[shift], both, pairs))
            source = (me ^ shift) % QUAD
            places.append(plane_of(tp, head, offset_of(source, turn)))
    place = jnp.stack(places).astype(jnp.int32)
    local_rows = rows * tp
    query, key, value, state = pl.pallas_call(
        feature_kernel,
        out_shape=[
            jax.ShapeDtypeStruct((local_rows, NUM_FEAT), BF16),
            jax.ShapeDtypeStruct((NUM_FEAT, local_rows), BF16),
            jax.ShapeDtypeStruct((local_rows, val_width), BF16),
            jax.ShapeDtypeStruct((STATE_ROWS, val_width), F32),
        ],
        in_specs=[SMEM] + [VMEM] * (1 + len(blocks)),
        out_specs=[VMEM] * 4,
        scratch_shapes=[pltpu.VMEM((HALO + local_rows, row_width), F32)],
        cost_estimate=cost(2 * local_rows * NUM_FEAT * val_width, local_rows * 1000),
    )(place, conv_weight, *blocks)
    numerator, denominator = pl.pallas_call(
        inner_kernel,
        out_shape=[jax.ShapeDtypeStruct((local_rows, val_width), F32)] * 2,
        in_specs=[VMEM] * 3,
        out_specs=[VMEM] * 2,
        cost_estimate=cost(2 * local_rows * local_rows * (NUM_FEAT + val_width), local_rows * 1000),
    )(query, key, value)

    neighbour = swap(state, 1)
    terms = [jnp.where(me % 2 == 1, neighbour, 0.0)]
    total = state + neighbour
    chips = ctx // 2
    chip = me // 2
    stride = 1
    while stride < chips:
        radix = min(QUAD, chips // stride)
        last = stride * radix >= chips
        digit = chip // stride % radix
        received = []
        for delta in range(1, radix):
            pairs = []
            for c in range(ctx):
                d = c // 2 // stride % radix
                if d + delta < radix:
                    pairs.append((c, c + 2 * stride * delta))
                elif not last:
                    pairs.append((c, c + 2 * stride * (delta - radix)))
            received.append(lax.ppermute(total, "ctx", pairs))
            terms.append(received[-1] if last else jnp.where(digit >= delta, received[-1], 0.0))
        if not last:
            total = functools.reduce(jnp.add, received, total)
        stride *= radix
    return pl.pallas_call(
        finish_kernel,
        out_shape=jax.ShapeDtypeStruct((local_rows, val_width), BF16),
        in_specs=[VMEM] * (3 + len(terms)),
        out_specs=VMEM,
        cost_estimate=cost(6 * local_rows * NUM_FEAT * val_width, local_rows * 1500),
    )(query, numerator, denominator, *terms)


def solution(mesh):
    ctx, tp = mesh.shape["ctx"], mesh.shape["tp"]
    if tp % QUAD or ctx % (2 * QUAD) or ctx & (ctx - 1):
        raise ValueError("unsupported mesh")
    return jax.shard_map(
        functools.partial(per_device, ctx, tp),
        mesh=mesh,
        in_specs=(P(("ctx", "tp"), None), P(None, "tp"), P(None, "tp")),
        out_specs=P("ctx", "tp"),
        check_vma=False,
    )
```

```python
import functools
import math

import jax
import jax.numpy as jnp
from jax import lax
from jax.experimental import pallas as pl
from jax.experimental.pallas import tpu as pltpu
from jax.sharding import PartitionSpec as P

FEAT = 16
HALO = 8
LANES = 128
QUAD_FEATS = FEAT * (FEAT + 1) // 2
NUM_FEAT = QUAD_FEATS + FEAT + 8
STATE_ROWS = NUM_FEAT + 8
F32 = jnp.float32
BF16 = jnp.bfloat16
VMEM = pl.BlockSpec(memory_space=pltpu.VMEM)
SMEM = pl.BlockSpec(memory_space=pltpu.SMEM)
LAST = (((1,), (1,)), ((), ()))


def call(kernel, outs, operands, scalars=0, scratch=(), flops=1 << 20, moved=1 << 20):
    return pl.pallas_call(
        kernel,
        out_shape=outs,
        in_specs=[SMEM] * scalars + [VMEM] * (len(operands) - scalars),
        out_specs=[VMEM] * len(outs),
        scratch_shapes=list(scratch),
        compiler_params=pltpu.CompilerParams(vmem_limit_bytes=16 << 20),
        cost_estimate=pl.CostEstimate(flops=flops, bytes_accessed=moved, transcendentals=0),
    )(*operands)


def dot_last(left, right):
    return lax.dot_general(left, right, LAST, preferred_element_type=F32)


def own_kernel(tail_ref, tokens_ref, weight_ref, halo_ref, own_ref):
    rows, depth = tokens_ref.shape
    weight = weight_ref[...]
    own_ref[...] = dot_last(weight, tokens_ref[...]).astype(BF16)
    padded = jnp.concatenate([jnp.zeros((rows - HALO, depth), BF16), tail_ref[...]], axis=0)
    halo_ref[...] = dot_last(weight, padded).astype(BF16)


def gathered(quarter, tokens_ref, pieces):
    depth = pieces[0].shape[1]
    total = None
    for index, piece in zip((0, 2, 1, 3), pieces):
        start = pl.multiple_of((quarter ^ index) * depth, depth)
        part = dot_last(piece[...], tokens_ref[:, pl.ds(start, depth)])
        total = part if total is None else total + part
    return total.astype(BF16)


def early_kernel(quarter_ref, tokens_ref, *refs):
    quarter = quarter_ref[0]
    count = len(refs) // 5
    for turn in range(count):
        refs[4 * count + turn][...] = gathered(quarter, tokens_ref, refs[4 * turn : 4 * turn + 4])


def late_kernel(quarter_ref, tokens_ref, weight_ref, *refs):
    quarter = quarter_ref[0]
    count = len(refs) // 5
    for turn in range(count):
        refs[4 * count + turn][...] = gathered(quarter, tokens_ref, refs[4 * turn : 4 * turn + 4])
    refs[-1][...] = dot_last(weight_ref[...], tokens_ref[...]).astype(BF16)


def features(raw, weighted):
    scale = 1.0 / (math.sqrt(2.0) * math.sqrt(FEAT))
    parts = []
    for shift in range(FEAT // 2 + 1):
        pair = raw * (pltpu.roll(raw, shift, 0) if shift else raw) * scale
        if shift == FEAT // 2:
            pair = pair[: FEAT // 2]
        pair = pair.astype(BF16).astype(F32)
        parts.append(pair * 2.0 if weighted and shift else pair)
    parts.append(raw * FEAT ** (-0.25))
    row = lax.broadcasted_iota(jnp.int32, (8, raw.shape[1]), 0)
    parts.append(jnp.where(row == 0, 1.0, 0.0).astype(F32))
    return jnp.concatenate(parts, axis=0).astype(BF16)


def feature_kernel(place_ref, conv_ref, halo_ref, *refs):
    count = place_ref.shape[0]
    blocks = refs[:count]
    query_ref, key_ref, value_ref, state_ref, wide = refs[count:]
    width = halo_ref.shape[1]
    local_rows = width * count
    wide[:, :width] = halo_ref[...].astype(F32)
    for index, block in enumerate(blocks):
        start = pl.multiple_of((place_ref[index] + 1) * width, LANES)
        wide[:, pl.ds(start, width)] = block[...].astype(F32)
    padded = wide[...]
    convolved = jnp.zeros((padded.shape[0], local_rows), F32)
    for offset in range(conv_ref.shape[1]):
        moved = pltpu.roll(padded, offset, 1) if offset else padded
        convolved += conv_ref[:, offset : offset + 1] * moved[:, width:]
    value = convolved[2 * FEAT :].astype(BF16)
    value_ref[...] = value
    query = features(convolved[:FEAT], False)
    query_ref[...] = query.T
    key = features(convolved[FEAT : 2 * FEAT], True)
    key_ref[...] = key
    state_ref[:NUM_FEAT, :] = dot_last(key, value)
    total = dot_last(jnp.ones((8, local_rows), BF16), key)
    lanes = state_ref.shape[1]
    rest = NUM_FEAT - lanes
    more = jnp.concatenate([total[:, lanes:], jnp.zeros((8, lanes - rest), F32)], axis=1)
    row = lax.broadcasted_iota(jnp.int32, (8, lanes), 0)
    state_ref[NUM_FEAT:, :] = jnp.where(row == 0, total[:, :lanes], jnp.where(row == 1, more, 0.0))


def inner_kernel(query_ref, key_ref, value_ref, numerator_ref, denominator_ref):
    local_rows = query_ref.shape[0]
    width = value_ref.shape[0]
    step = LANES
    for start in range(0, local_rows, step):
        size = start + step
        scores = jnp.dot(query_ref[start:size, :], key_ref[:, :size], preferred_element_type=F32)
        row = lax.broadcasted_iota(jnp.int32, (step, size), 0) + start
        column = lax.broadcasted_iota(jnp.int32, (step, size), 1)
        scores = jnp.where(row >= column, scores, 0.0)
        numerator_ref[start:size, :] = dot_last(scores.astype(BF16), value_ref[:, :size])
        denominator_ref[start:size, :] = jnp.broadcast_to(
            jnp.sum(scores, axis=1, keepdims=True), (step, width)
        )


def finish_kernel(query_ref, numerator_ref, denominator_ref, *refs):
    states, out_ref = refs[:-1], refs[-1]
    state = states[0][...]
    for other in states[1:]:
        state += other[...]
    width = numerator_ref.shape[1]
    query = query_ref[...]
    rest = state[:NUM_FEAT, :]
    numerator = numerator_ref[...]
    for _ in range(3):
        part = rest.astype(BF16)
        rest = rest - part.astype(F32)
        numerator += jnp.dot(query, part, preferred_element_type=F32)
    totals = jnp.concatenate(
        [state[NUM_FEAT : NUM_FEAT + 1, :], state[NUM_FEAT + 1 : NUM_FEAT + 2, : NUM_FEAT - width]], axis=1
    )
    denominator = denominator_ref[:, :1] + jnp.sum(query.astype(F32) * totals, axis=1, keepdims=True)
    out_ref[...] = (numerator / denominator).astype(BF16)


def per_device(ctx, tp, tokens, projection, conv_weight):
    both = ("ctx", "tp")
    rows, depth = tokens.shape
    row_width = projection.shape[1]
    val_width = row_width - 2 * FEAT
    local_rows = rows * tp
    turns = range(1, tp // 2)
    me = lax.axis_index("ctx")
    head = lax.axis_index("tp")
    weight = projection.T
    piece = depth // 4
    quarter = (me & 1) + 2 * (me >> 2 & 1)

    def swap(array, bit):
        return lax.ppermute(array, "ctx", [(i, i ^ bit) for i in range(ctx)])

    mine = lax.dynamic_slice(weight, (0, quarter * piece), (row_width, piece))
    pieces = []
    for turn in turns:
        first = lax.ppermute(mine, "tp", [((z + 2 * turn) % tp, z) for z in range(tp)])
        second = swap(first, 4)
        pieces += [first, second, swap(first, 1), swap(second, 1)]
    paired = lax.ppermute(tokens, "tp", [(z, z ^ 1) for z in range(tp)])

    tail = lax.ppermute(
        tokens[rows - HALO :], both, [((c - 1) * tp + tp - 1, c * tp + tp - 1) for c in range(1, ctx)]
    )
    have = [tp - 1]
    reach = 1 << (tp - 1).bit_length() - 1
    while reach:
        pairs = [(z, z - reach) for z in have if z >= reach]
        tail = tail + lax.ppermute(tail, "tp", pairs)
        have += [z for _, z in pairs]
        reach //= 2

    shape = jax.ShapeDtypeStruct((row_width, rows), BF16)
    work = 2 * rows * depth * row_width
    side = quarter.astype(jnp.int32).reshape(1)
    halo, own = call(own_kernel, [shape] * 2, [tail, tokens, weight], flops=2 * work)
    early = call(early_kernel, [shape] * len(turns), [side, tokens] + pieces, 1, flops=work)
    *late, other = call(
        late_kernel, [shape] * (len(turns) + 1), [side, paired, weight] + pieces, 1, flops=2 * work
    )
    blocks, places = [own, other], [head, head ^ 1]
    for turn, one, two in zip(turns, early, late):
        pairs = [(z, (z + 2 * turn) % tp) for z in range(tp)]
        source = (head + tp - 2 * turn) % tp
        blocks += [lax.ppermute(one, "tp", pairs), lax.ppermute(two, "tp", pairs)]
        places += [source, source ^ 1]
    place = jnp.stack(places).astype(jnp.int32)
    query, key, value, state = call(
        feature_kernel,
        [
            jax.ShapeDtypeStruct((local_rows, NUM_FEAT), BF16),
            jax.ShapeDtypeStruct((NUM_FEAT, local_rows), BF16),
            jax.ShapeDtypeStruct((val_width, local_rows), BF16),
            jax.ShapeDtypeStruct((STATE_ROWS, val_width), F32),
        ],
        [place, conv_weight.T, halo] + blocks,
        1,
        [pltpu.VMEM((row_width, rows + local_rows), F32)],
    )
    numerator, denominator = call(
        inner_kernel,
        [jax.ShapeDtypeStruct((local_rows, val_width), F32)] * 2,
        [query, key, value],
        flops=2 * local_rows * local_rows * (NUM_FEAT + val_width),
    )
    total, terms = state, []
    bit = 1
    while bit < ctx:
        if 2 * bit < ctx:
            received = swap(total, bit)
            terms.append(jnp.where(me & bit != 0, received, 0.0))
            total = total + received
        else:
            terms.append(lax.ppermute(total, "ctx", [(c, c + bit) for c in range(bit)]))
        bit *= 2
    return call(
        finish_kernel,
        [jax.ShapeDtypeStruct((local_rows, val_width), BF16)],
        [query, numerator, denominator] + terms,
        flops=6 * local_rows * NUM_FEAT * val_width,
    )[0]


def solution(mesh):
    ctx, tp = mesh.shape["ctx"], mesh.shape["tp"]
    if tp % 2 or tp < 4 or ctx < 8 or ctx & (ctx - 1):
        raise ValueError("unsupported mesh")
    return jax.shard_map(
        functools.partial(per_device, ctx, tp),
        mesh=mesh,
        in_specs=(P(("ctx", "tp"), None), P(None, "tp"), P(None, "tp")),
        out_specs=P("ctx", "tp"),
        check_vma=False,
    )
```

```python
import functools
import math

import jax
import jax.numpy as jnp
from jax import lax
from jax.experimental import pallas as pl
from jax.experimental.pallas import tpu as pltpu
from jax.sharding import PartitionSpec as P


FEAT = 16
HALO = 8
LANES = 128
QUAD_FEATS = FEAT * (FEAT + 1) // 2
NUM_FEAT = QUAD_FEATS + FEAT + 8
STATE_ROWS = NUM_FEAT + 8
F32 = jnp.float32
BF16 = jnp.bfloat16
VMEM = pl.BlockSpec(memory_space=pltpu.VMEM)
SMEM = pl.BlockSpec(memory_space=pltpu.SMEM)
LAST = (((1,), (1,)), ((), ()))


def call(kernel, outs, operands, scalars=0, scratch=(), flops=1 << 20, moved=1 << 20):
    return pl.pallas_call(
        kernel,
        out_shape=outs,
        in_specs=[SMEM] * scalars + [VMEM] * (len(operands) - scalars),
        out_specs=[VMEM] * len(outs),
        scratch_shapes=list(scratch),
        compiler_params=pltpu.CompilerParams(vmem_limit_bytes=16 << 20),
        cost_estimate=pl.CostEstimate(flops=flops, bytes_accessed=moved, transcendentals=0),
    )(*operands)


def dot_last(left, right):
    return lax.dot_general(left, right, LAST, preferred_element_type=F32)


def own_kernel(tail_ref, tokens_ref, weight_ref, halo_ref, own_ref):
    rows, depth = tokens_ref.shape
    weight = weight_ref[...]
    own_ref[...] = dot_last(weight, tokens_ref[...]).astype(BF16)
    padded = jnp.concatenate([jnp.zeros((rows - HALO, depth), BF16), tail_ref[...]], axis=0)
    halo_ref[...] = dot_last(weight, padded).astype(BF16)


def gathered(quarter, tokens_ref, pieces):
    depth = pieces[0].shape[1]
    total = None
    for index, piece in zip((0, 2, 1, 3), pieces):
        start = pl.multiple_of((quarter ^ index) * depth, depth)
        part = dot_last(piece[...], tokens_ref[:, pl.ds(start, depth)])
        total = part if total is None else total + part
    return total.astype(BF16)


def early_kernel(quarter_ref, tokens_ref, *refs):
    quarter = quarter_ref[0]
    count = len(refs) // 5
    for turn in range(count):
        refs[4 * count + turn][...] = gathered(quarter, tokens_ref, refs[4 * turn : 4 * turn + 4])


def late_kernel(quarter_ref, tokens_ref, weight_ref, *refs):
    quarter = quarter_ref[0]
    count = len(refs) // 5
    for turn in range(count):
        refs[4 * count + turn][...] = gathered(quarter, tokens_ref, refs[4 * turn : 4 * turn + 4])
    refs[-1][...] = dot_last(weight_ref[...], tokens_ref[...]).astype(BF16)


def features(raw, weighted):
    scale = 1.0 / (math.sqrt(2.0) * math.sqrt(FEAT))
    parts = []
    for shift in range(FEAT // 2 + 1):
        pair = raw * (pltpu.roll(raw, shift, 0) if shift else raw) * scale
        if shift == FEAT // 2:
            pair = pair[: FEAT // 2]
        pair = pair.astype(BF16).astype(F32)
        parts.append(pair * 2.0 if weighted and shift else pair)
    parts.append(raw * FEAT ** (-0.25))
    row = lax.broadcasted_iota(jnp.int32, (8, raw.shape[1]), 0)
    parts.append(jnp.where(row == 0, 1.0, 0.0).astype(F32))
    return jnp.concatenate(parts, axis=0).astype(BF16)


def feature_kernel(place_ref, conv_ref, halo_ref, *refs):
    count = place_ref.shape[0]
    blocks = refs[:count]
    query_ref, key_ref, value_ref, state_ref, wide = refs[count:]
    width = halo_ref.shape[1]
    local_rows = width * count
    wide[:, :width] = halo_ref[...].astype(F32)
    for index, block in enumerate(blocks):
        start = pl.multiple_of((place_ref[index] + 1) * width, LANES)
        wide[:, pl.ds(start, width)] = block[...].astype(F32)
    padded = wide[...]
    convolved = jnp.zeros((padded.shape[0], local_rows), F32)
    for offset in range(conv_ref.shape[1]):
        moved = pltpu.roll(padded, offset, 1) if offset else padded
        convolved += conv_ref[:, offset : offset + 1] * moved[:, width:]
    value = convolved[2 * FEAT :].astype(BF16)
    value_ref[...] = value
    query = features(convolved[:FEAT], False)
    query_ref[...] = query.T
    key = features(convolved[FEAT : 2 * FEAT], True)
    key_ref[...] = key
    state_ref[:NUM_FEAT, :] = dot_last(key, value)
    total = dot_last(jnp.ones((8, local_rows), BF16), key)
    lanes = state_ref.shape[1]
    rest = NUM_FEAT - lanes
    more = jnp.concatenate([total[:, lanes:], jnp.zeros((8, lanes - rest), F32)], axis=1)
    row = lax.broadcasted_iota(jnp.int32, (8, lanes), 0)
    state_ref[NUM_FEAT:, :] = jnp.where(row == 0, total[:, :lanes], jnp.where(row == 1, more, 0.0))


def inner_kernel(query_ref, key_ref, value_ref, numerator_ref, denominator_ref):
    local_rows = query_ref.shape[0]
    width = value_ref.shape[0]
    step = LANES
    for start in range(0, local_rows, step):
        size = start + step
        scores = jnp.dot(query_ref[start:size, :], key_ref[:, :size], preferred_element_type=F32)
        row = lax.broadcasted_iota(jnp.int32, (step, size), 0) + start
        column = lax.broadcasted_iota(jnp.int32, (step, size), 1)
        scores = jnp.where(row >= column, scores, 0.0)
        numerator_ref[start:size, :] = dot_last(scores.astype(BF16), value_ref[:, :size])
        denominator_ref[start:size, :] = jnp.broadcast_to(
            jnp.sum(scores, axis=1, keepdims=True), (step, width)
        )


def finish_kernel(query_ref, numerator_ref, denominator_ref, *refs):
    states, out_ref = refs[:-1], refs[-1]
    state = states[0][...]
    for other in states[1:]:
        state += other[...]
    width = numerator_ref.shape[1]
    query = query_ref[...]
    rest = state[:NUM_FEAT, :]
    numerator = numerator_ref[...]
    for _ in range(3):
        part = rest.astype(BF16)
        rest = rest - part.astype(F32)
        numerator += jnp.dot(query, part, preferred_element_type=F32)
    totals = jnp.concatenate(
        [state[NUM_FEAT : NUM_FEAT + 1, :], state[NUM_FEAT + 1 : NUM_FEAT + 2, : NUM_FEAT - width]], axis=1
    )
    denominator = denominator_ref[:, :1] + jnp.sum(query.astype(F32) * totals, axis=1, keepdims=True)
    out_ref[...] = (numerator / denominator).astype(BF16)


def per_device(ctx, tp, tokens, projection, conv_weight):
    both = ("ctx", "tp")
    rows, depth = tokens.shape
    row_width = projection.shape[1]
    val_width = row_width - 2 * FEAT
    local_rows = rows * tp
    turns = range(1, tp // 2)
    me = lax.axis_index("ctx")
    head = lax.axis_index("tp")
    weight = projection.T
    piece = depth // 4
    quarter = (me & 1) + 2 * (me >> 2 & 1)

    def swap(array, bit):
        return lax.ppermute(array, "ctx", [(i, i ^ bit) for i in range(ctx)])

    mine = lax.dynamic_slice(weight, (0, quarter * piece), (row_width, piece))
    pieces = []
    for turn in turns:
        first = lax.ppermute(mine, "tp", [((z + 2 * turn) % tp, z) for z in range(tp)])
        second = swap(first, 4)
        pieces += [first, second, swap(first, 1), swap(second, 1)]
    paired = lax.ppermute(tokens, "tp", [(z, z ^ 1) for z in range(tp)])

    tail = lax.ppermute(
        tokens[rows - HALO :],
        both,
        [((c - 1) * tp + tp - 1, c * tp + tp - 1) for c in range(1, ctx)],
    )
    have = [tp - 1]
    reach = 1 << (tp - 1).bit_length() - 1
    while reach:
        pairs = [(z, z - reach) for z in have if z >= reach]
        tail = tail + lax.ppermute(tail, "tp", pairs)
        have += [z for _, z in pairs]
        reach //= 2

    shape = jax.ShapeDtypeStruct((row_width, rows), BF16)
    work = 2 * rows * depth * row_width
    side = quarter.astype(jnp.int32).reshape(1)
    halo, own = call(own_kernel, [shape] * 2, [tail, tokens, weight], flops=2 * work)
    early = call(early_kernel, [shape] * len(turns), [side, tokens] + pieces, 1, flops=work)
    *late, other = call(
        late_kernel, [shape] * (len(turns) + 1), [side, paired, weight] + pieces, 1, flops=2 * work
    )
    blocks, places = [own, other], [head, head ^ 1]
    for turn, one, two in zip(turns, early, late):
        pairs = [(z, (z + 2 * turn) % tp) for z in range(tp)]
        source = (head + tp - 2 * turn) % tp
        blocks += [lax.ppermute(one, "tp", pairs), lax.ppermute(two, "tp", pairs)]
        places += [source, source ^ 1]
    place = jnp.stack(places).astype(jnp.int32)
    query, key, value, state = call(
        feature_kernel,
        [
            jax.ShapeDtypeStruct((local_rows, NUM_FEAT), BF16),
            jax.ShapeDtypeStruct((NUM_FEAT, local_rows), BF16),
            jax.ShapeDtypeStruct((val_width, local_rows), BF16),
            jax.ShapeDtypeStruct((STATE_ROWS, val_width), F32),
        ],
        [place, conv_weight.T, halo] + blocks,
        1,
        [pltpu.VMEM((row_width, rows + local_rows), F32)],
    )
    numerator, denominator = call(
        inner_kernel,
        [jax.ShapeDtypeStruct((local_rows, val_width), F32)] * 2,
        [query, key, value],
        flops=2 * local_rows * local_rows * (NUM_FEAT + val_width),
    )
    received = swap(state, 1)
    terms = [jnp.where(me % 2 == 1, received, 0.0)]
    total = state + received
    bit = 2
    while bit < ctx:
        radix = min(4, ctx // bit)
        last = bit * radix >= ctx
        digit = me // bit % radix
        parts = []
        for delta in range(1, radix):
            pairs = [(c, c ^ delta * bit) for c in range(ctx)]
            if last:
                pairs = [(c, d) for c, d in pairs if c < d]
            parts.append(lax.ppermute(total, "ctx", pairs))
            terms.append(parts[-1] if last else jnp.where(digit > digit ^ delta, parts[-1], 0.0))
        if not last:
            total = functools.reduce(jnp.add, parts, total)
        bit *= radix
    return call(
        finish_kernel,
        [jax.ShapeDtypeStruct((local_rows, val_width), BF16)],
        [query, numerator, denominator] + terms,
        flops=6 * local_rows * NUM_FEAT * val_width,
    )[0]


def solution(mesh):
    ctx, tp = mesh.shape["ctx"], mesh.shape["tp"]
    if tp % 2 or tp < 4 or ctx < 8 or ctx & (ctx - 1):
        raise ValueError("unsupported mesh")

    def body(*arrays):
        return per_device(ctx, tp, *arrays)

    return jax.shard_map(
        body,
        mesh=mesh,
        in_specs=(P(("ctx", "tp"), None), P(None, "tp"), P(None, "tp")),
        out_specs=P("ctx", "tp"),
        check_vma=False,
    )
```

```python
import functools
import math

import jax
import jax.numpy as jnp
from jax import lax
from jax.experimental import pallas as pl
from jax.experimental.pallas import tpu as pltpu
from jax.sharding import PartitionSpec as P


FEAT = 16
HALO = 8
LANES = 128
QUAD_FEATS = FEAT * (FEAT + 1) // 2
NUM_FEAT = QUAD_FEATS + FEAT + 8
STATE_ROWS = NUM_FEAT + 8
F32 = jnp.float32
BF16 = jnp.bfloat16
VMEM = pl.BlockSpec(memory_space=pltpu.VMEM)
SMEM = pl.BlockSpec(memory_space=pltpu.SMEM)
LAST = (((1,), (1,)), ((), ()))


def call(kernel, outs, operands, scalars=0, scratch=(), flops=1 << 20, moved=1 << 20):
    return pl.pallas_call(
        kernel,
        out_shape=outs,
        in_specs=[SMEM] * scalars + [VMEM] * (len(operands) - scalars),
        out_specs=[VMEM] * len(outs),
        scratch_shapes=list(scratch),
        compiler_params=pltpu.CompilerParams(vmem_limit_bytes=16 << 20),
        cost_estimate=pl.CostEstimate(flops=flops, bytes_accessed=moved, transcendentals=0),
    )(*operands)


def dot_last(left, right):
    return lax.dot_general(left, right, LAST, preferred_element_type=F32)


def own_kernel(tail_ref, tokens_ref, weight_ref, halo_ref, own_ref):
    rows, depth = tokens_ref.shape
    weight = weight_ref[...]
    own_ref[...] = dot_last(weight, tokens_ref[...]).astype(BF16)
    padded = jnp.concatenate([jnp.zeros((rows - HALO, depth), BF16), tail_ref[...]], axis=0)
    halo_ref[...] = dot_last(weight, padded).astype(BF16)


def gathered(quarter, tokens_ref, pieces):
    depth = pieces[0].shape[1]
    total = None
    for index, piece in zip((0, 2, 1, 3), pieces):
        start = pl.multiple_of((quarter ^ index) * depth, depth)
        part = dot_last(piece[...], tokens_ref[:, pl.ds(start, depth)])
        total = part if total is None else total + part
    return total.astype(BF16)


def early_kernel(quarter_ref, tokens_ref, *refs):
    quarter = quarter_ref[0]
    count = len(refs) // 5
    for turn in range(count):
        refs[4 * count + turn][...] = gathered(quarter, tokens_ref, refs[4 * turn : 4 * turn + 4])


def late_kernel(quarter_ref, tokens_ref, weight_ref, *refs):
    quarter = quarter_ref[0]
    count = len(refs) // 5
    for turn in range(count):
        refs[4 * count + turn][...] = gathered(quarter, tokens_ref, refs[4 * turn : 4 * turn + 4])
    refs[-1][...] = dot_last(weight_ref[...], tokens_ref[...]).astype(BF16)


def features(raw, weighted):
    scale = 1.0 / (math.sqrt(2.0) * math.sqrt(FEAT))
    parts = []
    for shift in range(FEAT // 2 + 1):
        pair = raw * (pltpu.roll(raw, shift, 0) if shift else raw) * scale
        if shift == FEAT // 2:
            pair = pair[: FEAT // 2]
        pair = pair.astype(BF16).astype(F32)
        parts.append(pair * 2.0 if weighted and shift else pair)
    parts.append(raw * FEAT ** (-0.25))
    row = lax.broadcasted_iota(jnp.int32, (8, raw.shape[1]), 0)
    parts.append(jnp.where(row == 0, 1.0, 0.0).astype(F32))
    return jnp.concatenate(parts, axis=0).astype(BF16)


def feature_kernel(place_ref, conv_ref, halo_ref, *refs):
    count = place_ref.shape[0]
    blocks = refs[:count]
    query_ref, key_ref, value_ref, state_ref, wide = refs[count:]
    width = halo_ref.shape[1]
    local_rows = width * count
    wide[:, :width] = halo_ref[...].astype(F32)
    for index, block in enumerate(blocks):
        start = pl.multiple_of((place_ref[index] + 1) * width, LANES)
        wide[:, pl.ds(start, width)] = block[...].astype(F32)
    padded = wide[...]
    convolved = jnp.zeros((padded.shape[0], local_rows), F32)
    for offset in range(conv_ref.shape[1]):
        moved = pltpu.roll(padded, offset, 1) if offset else padded
        convolved += conv_ref[:, offset : offset + 1] * moved[:, width:]
    value = convolved[2 * FEAT :].astype(BF16)
    value_ref[...] = value
    query = features(convolved[:FEAT], False)
    query_ref[...] = query.T
    key = features(convolved[FEAT : 2 * FEAT], True)
    key_ref[...] = key
    state_ref[:NUM_FEAT, :] = dot_last(key, value)
    total = dot_last(jnp.ones((8, local_rows), BF16), key)
    lanes = state_ref.shape[1]
    rest = NUM_FEAT - lanes
    more = jnp.concatenate([total[:, lanes:], jnp.zeros((8, lanes - rest), F32)], axis=1)
    row = lax.broadcasted_iota(jnp.int32, (8, lanes), 0)
    state_ref[NUM_FEAT:, :] = jnp.where(row == 0, total[:, :lanes], jnp.where(row == 1, more, 0.0))


def inner_kernel(query_ref, key_ref, value_ref, numerator_ref, denominator_ref):
    local_rows = query_ref.shape[0]
    width = value_ref.shape[0]
    step = LANES
    for start in range(0, local_rows, step):
        size = start + step
        scores = jnp.dot(query_ref[start:size, :], key_ref[:, :size], preferred_element_type=F32)
        row = lax.broadcasted_iota(jnp.int32, (step, size), 0) + start
        column = lax.broadcasted_iota(jnp.int32, (step, size), 1)
        scores = jnp.where(row >= column, scores, 0.0)
        numerator_ref[start:size, :] = dot_last(scores.astype(BF16), value_ref[:, :size])
        denominator_ref[start:size, :] = jnp.broadcast_to(
            jnp.sum(scores, axis=1, keepdims=True), (step, width)
        )


def finish_kernel(query_ref, numerator_ref, denominator_ref, *refs):
    states, out_ref = refs[:-1], refs[-1]
    state = states[0][...]
    for other in states[1:]:
        state += other[...]
    width = numerator_ref.shape[1]
    query = query_ref[...]
    rest = state[:NUM_FEAT, :]
    numerator = numerator_ref[...]
    for _ in range(3):
        part = rest.astype(BF16)
        rest = rest - part.astype(F32)
        numerator += jnp.dot(query, part, preferred_element_type=F32)
    totals = jnp.concatenate(
        [state[NUM_FEAT : NUM_FEAT + 1, :], state[NUM_FEAT + 1 : NUM_FEAT + 2, : NUM_FEAT - width]], axis=1
    )
    denominator = denominator_ref[:, :1] + jnp.sum(query.astype(F32) * totals, axis=1, keepdims=True)
    out_ref[...] = (numerator / denominator).astype(BF16)


def per_device(ctx, tp, tokens, projection, conv_weight):
    both = ("ctx", "tp")
    rows, depth = tokens.shape
    row_width = projection.shape[1]
    val_width = row_width - 2 * FEAT
    local_rows = rows * tp
    turns = range(1, tp // 2)
    me = lax.axis_index("ctx")
    head = lax.axis_index("tp")
    weight = projection.T
    piece = depth // 4
    quarter = (me & 1) + 2 * (me >> 2 & 1)

    def swap(array, bit):
        return lax.ppermute(array, "ctx", [(i, i ^ bit) for i in range(ctx)])

    mine = lax.dynamic_slice(weight, (0, quarter * piece), (row_width, piece))
    pieces = []
    for turn in turns:
        first = lax.ppermute(mine, "tp", [((z + 2 * turn) % tp, z) for z in range(tp)])
        second = swap(first, 4)
        pieces += [first, second, swap(first, 1), swap(second, 1)]
    paired = lax.ppermute(tokens, "tp", [(z, z ^ 1) for z in range(tp)])

    last_rows = tokens[rows - HALO :]
    tail = None
    for z in range(tp):
        pairs = [((c - 1) * tp + tp - 1, c * tp + z) for c in range(1, ctx)]
        part = lax.ppermute(last_rows, both, pairs)
        tail = part if tail is None else tail + part

    shape = jax.ShapeDtypeStruct((row_width, rows), BF16)
    work = 2 * rows * depth * row_width
    side = quarter.astype(jnp.int32).reshape(1)
    halo, own = call(own_kernel, [shape] * 2, [tail, tokens, weight], flops=2 * work)
    early = call(early_kernel, [shape] * len(turns), [side, tokens] + pieces, 1, flops=work)
    *late, other = call(
        late_kernel, [shape] * (len(turns) + 1), [side, paired, weight] + pieces, 1, flops=2 * work
    )
    blocks, places = [own, other], [head, head ^ 1]
    for turn, one, two in zip(turns, early, late):
        pairs = [(z, (z + 2 * turn) % tp) for z in range(tp)]
        source = (head + tp - 2 * turn) % tp
        blocks += [lax.ppermute(one, "tp", pairs), lax.ppermute(two, "tp", pairs)]
        places += [source, source ^ 1]
    place = jnp.stack(places).astype(jnp.int32)
    query, key, value, state = call(
        feature_kernel,
        [
            jax.ShapeDtypeStruct((local_rows, NUM_FEAT), BF16),
            jax.ShapeDtypeStruct((NUM_FEAT, local_rows), BF16),
            jax.ShapeDtypeStruct((val_width, local_rows), BF16),
            jax.ShapeDtypeStruct((STATE_ROWS, val_width), F32),
        ],
        [place, conv_weight.T, halo] + blocks,
        1,
        [pltpu.VMEM((row_width, rows + local_rows), F32)],
    )
    numerator, denominator = call(
        inner_kernel,
        [jax.ShapeDtypeStruct((local_rows, val_width), F32)] * 2,
        [query, key, value],
        flops=2 * local_rows * local_rows * (NUM_FEAT + val_width),
    )
    received = swap(state, 1)
    terms = [jnp.where(me % 2 == 1, received, 0.0)]
    total = state + received
    bit = 2
    while bit < ctx:
        radix = min(4, ctx // bit)
        last = bit * radix >= ctx
        digit = me // bit % radix
        parts = []
        for delta in range(1, radix):
            pairs = [(c, c ^ delta * bit) for c in range(ctx)]
            parts.append(lax.ppermute(total, "ctx", pairs))
            terms.append(jnp.where(digit > digit ^ delta, parts[-1], 0.0))
        if not last:
            total = functools.reduce(jnp.add, parts, total)
        bit *= radix
    return call(
        finish_kernel,
        [jax.ShapeDtypeStruct((local_rows, val_width), BF16)],
        [query, numerator, denominator] + terms,
        flops=6 * local_rows * NUM_FEAT * val_width,
    )[0]


def solution(mesh):
    ctx, tp = mesh.shape["ctx"], mesh.shape["tp"]
    if tp % 2 or tp < 4 or ctx < 8 or ctx & (ctx - 1):
        raise ValueError("unsupported mesh")

    def body(*arrays):
        return per_device(ctx, tp, *arrays)

    return jax.shard_map(
        body,
        mesh=mesh,
        in_specs=(P(("ctx", "tp"), None), P(None, "tp"), P(None, "tp")),
        out_specs=P("ctx", "tp"),
        check_vma=False,
    )
```

```python
import functools
import math

import jax
import jax.numpy as jnp
from jax import lax
from jax.experimental import pallas as pl
from jax.experimental.pallas import tpu as pltpu
from jax.sharding import PartitionSpec as P


FEAT = 16
HALO = 8
PIECES = 8
LANES = 128
QUAD_FEATS = FEAT * (FEAT + 1) // 2
NUM_FEAT = QUAD_FEATS + FEAT + 8
STATE_ROWS = NUM_FEAT + 8
F32 = jnp.float32
BF16 = jnp.bfloat16
VMEM = pl.BlockSpec(memory_space=pltpu.VMEM)
SMEM = pl.BlockSpec(memory_space=pltpu.SMEM)
LAST = (((1,), (1,)), ((), ()))


def call(kernel, outs, operands, scalars=0, scratch=(), flops=1 << 20, moved=1 << 20):
    return pl.pallas_call(
        kernel,
        out_shape=outs,
        in_specs=[SMEM] * scalars + [VMEM] * (len(operands) - scalars),
        out_specs=[VMEM] * len(outs),
        scratch_shapes=list(scratch),
        compiler_params=pltpu.CompilerParams(vmem_limit_bytes=16 << 20),
        cost_estimate=pl.CostEstimate(flops=flops, bytes_accessed=moved, transcendentals=0),
    )(*operands)


def dot_last(left, right):
    return lax.dot_general(left, right, LAST, preferred_element_type=F32)


def own_kernel(tokens_ref, weight_ref, own_ref):
    own_ref[...] = dot_last(weight_ref[...], tokens_ref[...]).astype(BF16)


def halo_kernel(tail_ref, weight_ref, halo_ref):
    padded = jnp.concatenate(
        [jnp.zeros((halo_ref.shape[1] - HALO, tail_ref.shape[1]), BF16), tail_ref[...]], axis=0
    )
    halo_ref[...] = dot_last(weight_ref[...], padded).astype(BF16)


def gathered(share, tokens_ref, pieces):
    depth = pieces[0].shape[1]
    total = None
    for index, piece in zip((0, 2, 4, 6, 1, 3, 5, 7), pieces):
        start = pl.multiple_of((share ^ index) * depth, depth)
        part = dot_last(piece[...], tokens_ref[:, pl.ds(start, depth)])
        total = part if total is None else total + part
    return total.astype(BF16)


def early_kernel(share_ref, tokens_ref, *refs):
    share = share_ref[0]
    count = len(refs) // (PIECES + 1)
    for turn in range(count):
        refs[PIECES * count + turn][...] = gathered(
            share, tokens_ref, refs[PIECES * turn : PIECES * turn + PIECES]
        )


def late_kernel(share_ref, tokens_ref, weight_ref, *refs):
    share = share_ref[0]
    count = len(refs) // (PIECES + 1)
    for turn in range(count):
        refs[PIECES * count + turn][...] = gathered(
            share, tokens_ref, refs[PIECES * turn : PIECES * turn + PIECES]
        )
    refs[-1][...] = dot_last(weight_ref[...], tokens_ref[...]).astype(BF16)


def features(raw, weighted):
    scale = 1.0 / (math.sqrt(2.0) * math.sqrt(FEAT))
    parts = []
    for shift in range(FEAT // 2 + 1):
        pair = raw * (pltpu.roll(raw, shift, 0) if shift else raw) * scale
        if shift == FEAT // 2:
            pair = pair[: FEAT // 2]
        pair = pair.astype(BF16).astype(F32)
        parts.append(pair * 2.0 if weighted and shift else pair)
    parts.append(raw * FEAT ** (-0.25))
    row = lax.broadcasted_iota(jnp.int32, (8, raw.shape[1]), 0)
    parts.append(jnp.where(row == 0, 1.0, 0.0).astype(F32))
    return jnp.concatenate(parts, axis=0).astype(BF16)


def feature_kernel(place_ref, conv_ref, halo_ref, *refs):
    count = place_ref.shape[0]
    blocks = refs[:count]
    query_ref, key_ref, value_ref, state_ref, wide = refs[count:]
    width = halo_ref.shape[1]
    local_rows = width * count
    wide[:, :width] = halo_ref[...].astype(F32)
    for index, block in enumerate(blocks):
        start = pl.multiple_of((place_ref[index] + 1) * width, LANES)
        wide[:, pl.ds(start, width)] = block[...].astype(F32)
    padded = wide[...]
    convolved = jnp.zeros((padded.shape[0], local_rows), F32)
    for offset in range(conv_ref.shape[1]):
        moved = pltpu.roll(padded, offset, 1) if offset else padded
        convolved += conv_ref[:, offset : offset + 1] * moved[:, width:]
    value = convolved[2 * FEAT :].astype(BF16)
    value_ref[...] = value
    query = features(convolved[:FEAT], False)
    query_ref[...] = query.T
    key = features(convolved[FEAT : 2 * FEAT], True)
    key_ref[...] = key
    state_ref[:NUM_FEAT, :] = dot_last(key, value)
    total = dot_last(jnp.ones((8, local_rows), BF16), key)
    lanes = state_ref.shape[1]
    rest = NUM_FEAT - lanes
    more = jnp.concatenate([total[:, lanes:], jnp.zeros((8, lanes - rest), F32)], axis=1)
    row = lax.broadcasted_iota(jnp.int32, (8, lanes), 0)
    state_ref[NUM_FEAT:, :] = jnp.where(row == 0, total[:, :lanes], jnp.where(row == 1, more, 0.0))


def inner_kernel(query_ref, key_ref, value_ref, numerator_ref, denominator_ref):
    local_rows = query_ref.shape[0]
    width = value_ref.shape[0]
    step = LANES
    for start in range(0, local_rows, step):
        size = start + step
        scores = jnp.dot(query_ref[start:size, :], key_ref[:, :size], preferred_element_type=F32)
        row = lax.broadcasted_iota(jnp.int32, (step, size), 0) + start
        column = lax.broadcasted_iota(jnp.int32, (step, size), 1)
        scores = jnp.where(row >= column, scores, 0.0)
        numerator_ref[start:size, :] = dot_last(scores.astype(BF16), value_ref[:, :size])
        denominator_ref[start:size, :] = jnp.broadcast_to(
            jnp.sum(scores, axis=1, keepdims=True), (step, width)
        )


def finish_kernel(query_ref, numerator_ref, denominator_ref, *refs):
    states, out_ref = refs[:-1], refs[-1]
    state = states[0][...]
    for other in states[1:]:
        state += other[...]
    width = numerator_ref.shape[1]
    query = query_ref[...]
    rest = state[:NUM_FEAT, :]
    numerator = numerator_ref[...]
    for _ in range(3):
        part = rest.astype(BF16)
        rest = rest - part.astype(F32)
        numerator += jnp.dot(query, part, preferred_element_type=F32)
    totals = jnp.concatenate(
        [state[NUM_FEAT : NUM_FEAT + 1, :], state[NUM_FEAT + 1 : NUM_FEAT + 2, : NUM_FEAT - width]], axis=1
    )
    denominator = denominator_ref[:, :1] + jnp.sum(query.astype(F32) * totals, axis=1, keepdims=True)
    out_ref[...] = (numerator / denominator).astype(BF16)


def per_device(ctx, tp, tokens, projection, conv_weight):
    both = ("ctx", "tp")
    rows, depth = tokens.shape
    row_width = projection.shape[1]
    val_width = row_width - 2 * FEAT
    local_rows = rows * tp
    turns = range(1, tp // 2)
    me = lax.axis_index("ctx")
    head = lax.axis_index("tp")
    weight = projection.T
    piece = depth // PIECES
    share = me & PIECES - 1

    def swap(array, bit):
        return lax.ppermute(array, "ctx", [(i, i ^ bit) for i in range(ctx)])

    mine = lax.dynamic_slice(weight, (0, share * piece), (row_width, piece))
    pieces = []
    for turn in turns:
        first = lax.ppermute(mine, "tp", [((z + 2 * turn) % tp, z) for z in range(tp)])
        parts = [first] + [swap(first, bits) for bits in (2, 4, 6)]
        pieces += parts + [swap(part, 1) for part in parts]
    paired = lax.ppermute(tokens, "tp", [(z, z ^ 1) for z in range(tp)])

    last_rows = tokens[rows - HALO :]
    tail = None
    for z in range(tp):
        pairs = [((c - 1) * tp + tp - 1, c * tp + z) for c in range(1, ctx)]
        part = lax.ppermute(last_rows, both, pairs)
        tail = part if tail is None else tail + part

    shape = jax.ShapeDtypeStruct((row_width, rows), BF16)
    work = 2 * rows * depth * row_width
    side = share.astype(jnp.int32).reshape(1)
    own = call(own_kernel, [shape], [tokens, weight], flops=work)[0]
    halo = call(halo_kernel, [shape], [tail, weight], flops=work)[0]
    early = call(early_kernel, [shape] * len(turns), [side, tokens] + pieces, 1, flops=work)
    *late, other = call(
        late_kernel, [shape] * (len(turns) + 1), [side, paired, weight] + pieces, 1, flops=2 * work
    )
    blocks, places = [own, other], [head, head ^ 1]
    for turn, one, two in zip(turns, early, late):
        pairs = [(z, (z + 2 * turn) % tp) for z in range(tp)]
        source = (head + tp - 2 * turn) % tp
        blocks += [lax.ppermute(one, "tp", pairs), lax.ppermute(two, "tp", pairs)]
        places += [source, source ^ 1]
    place = jnp.stack(places).astype(jnp.int32)
    query, key, value, state = call(
        feature_kernel,
        [
            jax.ShapeDtypeStruct((local_rows, NUM_FEAT), BF16),
            jax.ShapeDtypeStruct((NUM_FEAT, local_rows), BF16),
            jax.ShapeDtypeStruct((val_width, local_rows), BF16),
            jax.ShapeDtypeStruct((STATE_ROWS, val_width), F32),
        ],
        [place, conv_weight.T, halo] + blocks,
        1,
        [pltpu.VMEM((row_width, rows + local_rows), F32)],
    )
    numerator, denominator = call(
        inner_kernel,
        [jax.ShapeDtypeStruct((local_rows, val_width), F32)] * 2,
        [query, key, value],
        flops=2 * local_rows * local_rows * (NUM_FEAT + val_width),
    )
    received = swap(state, 1)
    terms = [jnp.where(me % 2 == 1, received, 0.0)]
    total = state + received
    bit = 2
    while bit < ctx:
        radix = min(4, ctx // bit)
        last = bit * radix >= ctx
        digit = me // bit % radix
        parts = []
        for delta in range(1, radix):
            pairs = [(c, c ^ delta * bit) for c in range(ctx)]
            parts.append(lax.ppermute(total, "ctx", pairs))
            terms.append(jnp.where(digit > digit ^ delta, parts[-1], 0.0))
        if not last:
            total = functools.reduce(jnp.add, parts, total)
        bit *= radix
    return call(
        finish_kernel,
        [jax.ShapeDtypeStruct((local_rows, val_width), BF16)],
        [query, numerator, denominator] + terms,
        flops=6 * local_rows * NUM_FEAT * val_width,
    )[0]


def solution(mesh):
    ctx, tp = mesh.shape["ctx"], mesh.shape["tp"]
    if tp % 2 or tp < 4 or ctx < 8 or ctx & (ctx - 1):
        raise ValueError("unsupported mesh")

    def body(*arrays):
        return per_device(ctx, tp, *arrays)

    return jax.shard_map(
        body,
        mesh=mesh,
        in_specs=(P(("ctx", "tp"), None), P(None, "tp"), P(None, "tp")),
        out_specs=P("ctx", "tp"),
        check_vma=False,
    )
```

```python
import functools
import math

import jax
import jax.numpy as jnp
from jax import lax
from jax.experimental import pallas as pl
from jax.experimental.pallas import tpu as pltpu
from jax.sharding import PartitionSpec as P


FEAT = 16
HALO = 8
PIECES = 8
LANES = 128
QUAD_FEATS = FEAT * (FEAT + 1) // 2
NUM_FEAT = QUAD_FEATS + FEAT + 8
STATE_ROWS = NUM_FEAT + 8
F32 = jnp.float32
BF16 = jnp.bfloat16
HBM = pl.BlockSpec(memory_space=pltpu.HBM)
VMEM = pl.BlockSpec(memory_space=pltpu.VMEM)
SMEM = pl.BlockSpec(memory_space=pltpu.SMEM)
LAST = (((1,), (1,)), ((), ()))


def call(kernel, outs, operands, scalars=0, scratch=(), flops=1 << 20, moved=1 << 20, space=VMEM):
    return pl.pallas_call(
        kernel,
        out_shape=outs,
        in_specs=[SMEM] * scalars + [space] * (len(operands) - scalars),
        out_specs=[VMEM] * len(outs),
        scratch_shapes=list(scratch),
        compiler_params=pltpu.CompilerParams(vmem_limit_bytes=16 << 20),
        cost_estimate=pl.CostEstimate(flops=flops, bytes_accessed=moved, transcendentals=0),
    )(*operands)


def dot_last(left, right):
    return lax.dot_general(left, right, LAST, preferred_element_type=F32)


def fetch_kernel(tokens_ref, all_ref, last_ref, sems):
    rows = tokens_ref.shape[0]
    last = pltpu.make_async_copy(tokens_ref.at[rows - HALO :, :], last_ref, sems.at[0])
    whole = pltpu.make_async_copy(tokens_ref, all_ref, sems.at[1])
    last.start()
    whole.start()
    last.wait()
    whole.wait()


def own_kernel(tail_ref, tokens_ref, weight_ref, halo_ref, own_ref):
    weight = weight_ref[...]
    own_ref[...] = dot_last(weight, tokens_ref[...]).astype(BF16)
    padded = jnp.concatenate(
        [jnp.zeros((halo_ref.shape[1] - HALO, tail_ref.shape[1]), BF16), tail_ref[...]], axis=0
    )
    halo_ref[...] = dot_last(weight, padded).astype(BF16)


def gathered(share, tokens_ref, pieces):
    depth = pieces[0].shape[1]
    total = None
    for index, piece in zip((0, 2, 4, 6, 1, 3, 5, 7), pieces):
        start = pl.multiple_of((share ^ index) * depth, depth)
        part = dot_last(piece[...], tokens_ref[:, pl.ds(start, depth)])
        total = part if total is None else total + part
    return total.astype(BF16)


def early_kernel(share_ref, tokens_ref, *refs):
    share = share_ref[0]
    count = len(refs) // (PIECES + 1)
    for turn in range(count):
        refs[PIECES * count + turn][...] = gathered(
            share, tokens_ref, refs[PIECES * turn : PIECES * turn + PIECES]
        )


def late_kernel(share_ref, tokens_ref, weight_ref, *refs):
    share = share_ref[0]
    count = len(refs) // (PIECES + 1)
    for turn in range(count):
        refs[PIECES * count + turn][...] = gathered(
            share, tokens_ref, refs[PIECES * turn : PIECES * turn + PIECES]
        )
    refs[-1][...] = dot_last(weight_ref[...], tokens_ref[...]).astype(BF16)


def features(raw, weighted):
    scale = 1.0 / (math.sqrt(2.0) * math.sqrt(FEAT))
    parts = []
    for shift in range(FEAT // 2 + 1):
        pair = raw * (pltpu.roll(raw, shift, 0) if shift else raw) * scale
        if shift == FEAT // 2:
            pair = pair[: FEAT // 2]
        pair = pair.astype(BF16).astype(F32)
        parts.append(pair * 2.0 if weighted and shift else pair)
    parts.append(raw * FEAT ** (-0.25))
    row = lax.broadcasted_iota(jnp.int32, (8, raw.shape[1]), 0)
    parts.append(jnp.where(row == 0, 1.0, 0.0).astype(F32))
    return jnp.concatenate(parts, axis=0).astype(BF16)


def feature_kernel(place_ref, conv_ref, halo_ref, *refs):
    count = place_ref.shape[0]
    blocks = refs[:count]
    query_ref, key_ref, value_ref, state_ref, wide = refs[count:]
    width = halo_ref.shape[1]
    local_rows = width * count
    wide[:, :width] = halo_ref[...].astype(F32)
    for index, block in enumerate(blocks):
        start = pl.multiple_of((place_ref[index] + 1) * width, LANES)
        wide[:, pl.ds(start, width)] = block[...].astype(F32)
    padded = wide[...]
    convolved = jnp.zeros((padded.shape[0], local_rows), F32)
    taps = conv_ref[...].T
    for offset in range(taps.shape[1]):
        moved = pltpu.roll(padded, offset, 1) if offset else padded
        convolved += taps[:, offset : offset + 1] * moved[:, width:]
    value = convolved[2 * FEAT :].astype(BF16)
    value_ref[...] = value
    query = features(convolved[:FEAT], False)
    query_ref[...] = query.T
    key = features(convolved[FEAT : 2 * FEAT], True)
    key_ref[...] = key
    state_ref[:NUM_FEAT, :] = dot_last(key, value)
    total = dot_last(jnp.ones((8, local_rows), BF16), key)
    lanes = state_ref.shape[1]
    rest = NUM_FEAT - lanes
    more = jnp.concatenate([total[:, lanes:], jnp.zeros((8, lanes - rest), F32)], axis=1)
    row = lax.broadcasted_iota(jnp.int32, (8, lanes), 0)
    state_ref[NUM_FEAT:, :] = jnp.where(row == 0, total[:, :lanes], jnp.where(row == 1, more, 0.0))


def inner_kernel(query_ref, key_ref, value_ref, numerator_ref, denominator_ref):
    local_rows = query_ref.shape[0]
    width = value_ref.shape[0]
    step = LANES
    for start in range(0, local_rows, step):
        size = start + step
        scores = jnp.dot(query_ref[start:size, :], key_ref[:, :size], preferred_element_type=F32)
        row = lax.broadcasted_iota(jnp.int32, (step, size), 0) + start
        column = lax.broadcasted_iota(jnp.int32, (step, size), 1)
        scores = jnp.where(row >= column, scores, 0.0)
        numerator_ref[start:size, :] = dot_last(scores.astype(BF16), value_ref[:, :size])
        denominator_ref[start:size, :] = jnp.broadcast_to(
            jnp.sum(scores, axis=1, keepdims=True), (step, width)
        )


def finish_kernel(query_ref, numerator_ref, denominator_ref, *refs):
    states, out_ref = refs[:-1], refs[-1]
    state = states[0][...]
    for other in states[1:]:
        state += other[...]
    width = numerator_ref.shape[1]
    query = query_ref[...]
    rest = state[:NUM_FEAT, :]
    numerator = numerator_ref[...]
    for _ in range(3):
        part = rest.astype(BF16)
        rest = rest - part.astype(F32)
        numerator += jnp.dot(query, part, preferred_element_type=F32)
    totals = jnp.concatenate(
        [state[NUM_FEAT : NUM_FEAT + 1, :], state[NUM_FEAT + 1 : NUM_FEAT + 2, : NUM_FEAT - width]], axis=1
    )
    denominator = denominator_ref[:, :1] + jnp.sum(query.astype(F32) * totals, axis=1, keepdims=True)
    out_ref[...] = (numerator / denominator).astype(BF16)


def per_device(ctx, tp, tokens, projection, conv_weight):
    both = ("ctx", "tp")
    rows, depth = tokens.shape
    row_width = projection.shape[1]
    val_width = row_width - 2 * FEAT
    local_rows = rows * tp
    turns = range(1, tp // 2)
    me = lax.axis_index("ctx")
    head = lax.axis_index("tp")
    weight = projection.T
    piece = depth // PIECES
    share = me & PIECES - 1

    def swap(array, bit):
        return lax.ppermute(array, "ctx", [(i, i ^ bit) for i in range(ctx)])

    side = share.astype(jnp.int32).reshape(1)
    mine = lax.dynamic_slice(weight, (0, share * piece), (row_width, piece))
    pieces = []
    for turn in turns:
        first = lax.ppermute(mine, "tp", [((z + 2 * turn) % tp, z) for z in range(tp)])
        parts = [first] + [swap(first, bits) for bits in (2, 4, 6)]
        pieces += parts + [swap(part, 1) for part in parts]
    paired = lax.ppermute(tokens, "tp", [(z, z ^ 1) for z in range(tp)])

    held, last_rows = call(
        fetch_kernel,
        [tokens, jax.ShapeDtypeStruct((HALO, depth), BF16)],
        [tokens],
        0,
        [pltpu.SemaphoreType.DMA((2,))],
        space=HBM,
    )
    tail = None
    for z in range(tp):
        pairs = [((c - 1) * tp + tp - 1, c * tp + z) for c in range(1, ctx)]
        part = lax.ppermute(last_rows, both, pairs)
        tail = part if tail is None else tail + part

    shape = jax.ShapeDtypeStruct((row_width, rows), BF16)
    work = 2 * rows * depth * row_width
    halo, own = call(own_kernel, [shape] * 2, [tail, held, weight], flops=2 * work)
    early = call(early_kernel, [shape] * len(turns), [side, held] + pieces, 1, flops=work)
    *late, other = call(
        late_kernel, [shape] * (len(turns) + 1), [side, paired, weight] + pieces, 1, flops=2 * work
    )
    blocks, places = [own, other], [head, head ^ 1]
    for turn, one, two in zip(turns, early, late):
        pairs = [(z, (z + 2 * turn) % tp) for z in range(tp)]
        source = (head + tp - 2 * turn) % tp
        blocks += [lax.ppermute(one, "tp", pairs), lax.ppermute(two, "tp", pairs)]
        places += [source, source ^ 1]
    place = jnp.stack(places).astype(jnp.int32)
    query, key, value, state = call(
        feature_kernel,
        [
            jax.ShapeDtypeStruct((local_rows, NUM_FEAT), BF16),
            jax.ShapeDtypeStruct((NUM_FEAT, local_rows), BF16),
            jax.ShapeDtypeStruct((val_width, local_rows), BF16),
            jax.ShapeDtypeStruct((STATE_ROWS, val_width), F32),
        ],
        [place, conv_weight, halo] + blocks,
        1,
        [pltpu.VMEM((row_width, rows + local_rows), F32)],
    )
    numerator, denominator = call(
        inner_kernel,
        [jax.ShapeDtypeStruct((local_rows, val_width), F32)] * 2,
        [query, key, value],
        flops=2 * local_rows * local_rows * (NUM_FEAT + val_width),
    )
    received = swap(state, 1)
    terms = [jnp.where(me % 2 == 1, received, 0.0)]
    total = state + received
    bit = 2
    while bit < ctx:
        radix = min(4, ctx // bit)
        last = bit * radix >= ctx
        digit = me // bit % radix
        parts = []
        for delta in range(1, radix):
            pairs = [(c, c ^ delta * bit) for c in range(ctx)]
            parts.append(lax.ppermute(total, "ctx", pairs))
            terms.append(jnp.where(digit > digit ^ delta, parts[-1], 0.0))
        if not last:
            total = functools.reduce(jnp.add, parts, total)
        bit *= radix
    return call(
        finish_kernel,
        [jax.ShapeDtypeStruct((local_rows, val_width), BF16)],
        [query, numerator, denominator] + terms,
        flops=6 * local_rows * NUM_FEAT * val_width,
    )[0]


def solution(mesh):
    ctx, tp = mesh.shape["ctx"], mesh.shape["tp"]
    if tp % 2 or tp < 4 or ctx < 8 or ctx & (ctx - 1):
        raise ValueError("unsupported mesh")

    def body(*arrays):
        return per_device(ctx, tp, *arrays)

    return jax.shard_map(
        body,
        mesh=mesh,
        in_specs=(P(("ctx", "tp"), None), P(None, "tp"), P(None, "tp")),
        out_specs=P("ctx", "tp"),
        check_vma=False,
    )
```

```python
import functools
import math

import jax
import jax.numpy as jnp
from jax import lax
from jax.experimental import pallas as pl
from jax.experimental.pallas import tpu as pltpu
from jax.sharding import PartitionSpec as P


FEAT = 16
HALO = 8
PIECES = 8
LANES = 128
QUAD_FEATS = FEAT * (FEAT + 1) // 2
NUM_FEAT = QUAD_FEATS + FEAT + 8
STATE_ROWS = NUM_FEAT + 8
F32 = jnp.float32
BF16 = jnp.bfloat16
HBM = pl.BlockSpec(memory_space=pltpu.HBM)
VMEM = pl.BlockSpec(memory_space=pltpu.VMEM)
SMEM = pl.BlockSpec(memory_space=pltpu.SMEM)
LAST = (((1,), (1,)), ((), ()))


def call(kernel, outs, operands, scalars=0, scratch=(), flops=1 << 20, moved=1 << 20, space=VMEM):
    return pl.pallas_call(
        kernel,
        out_shape=outs,
        in_specs=[SMEM] * scalars + [space] * (len(operands) - scalars),
        out_specs=[VMEM] * len(outs),
        scratch_shapes=list(scratch),
        compiler_params=pltpu.CompilerParams(vmem_limit_bytes=16 << 20),
        cost_estimate=pl.CostEstimate(flops=flops, bytes_accessed=moved, transcendentals=0),
    )(*operands)


def hbm(array):
    return pltpu.with_memory_space_constraint(array, pltpu.HBM)


def dot_last(left, right):
    return lax.dot_general(left, right, LAST, preferred_element_type=F32)


def pack_kernel(share_ref, weight_ref, tokens_ref, sent_ref, tail_ref, last_ref, sems):
    height, width = weight_ref.shape[0], sent_ref.shape[1]
    start = pl.multiple_of(share_ref[0] * width, LANES)
    weight_copy = pltpu.make_async_copy(
        weight_ref.at[:, pl.ds(start, width)], sent_ref.at[:height, :], sems.at[0]
    )
    tokens_copy = pltpu.make_async_copy(
        tokens_ref.at[tokens_ref.shape[0] - HALO :, :], last_ref, sems.at[1]
    )
    tokens_copy.start()
    weight_copy.start()
    tokens_copy.wait()
    lag = tail_ref.shape[0] // PIECES
    rows = last_ref[...].astype(F32)
    cuts = []
    for row in range(HALO - lag, HALO):
        cuts += [rows[row : row + 1, index * width : index * width + width] for index in range(PIECES)]
    tail = jnp.concatenate(cuts, axis=0).astype(BF16)
    sent_ref[height:, :] = tail
    tail_ref[...] = tail
    weight_copy.wait()


def own_kernel(tail_ref, tokens_ref, weight_ref, halo_ref, own_ref):
    weight = weight_ref[...]
    depth = weight.shape[1]
    own_ref[...] = dot_last(weight, tokens_ref[...]).astype(BF16)
    cuts = tail_ref[...].astype(F32)
    lag = cuts.shape[0] // PIECES
    rows = [jnp.zeros((halo_ref.shape[1] - lag, depth), F32)]
    for row in range(lag):
        first = row * PIECES
        rows.append(
            jnp.concatenate([cuts[first + i : first + i + 1, :] for i in range(PIECES)], axis=1)
        )
    padded = jnp.concatenate(rows, axis=0).astype(BF16)
    halo_ref[...] = dot_last(weight, padded).astype(BF16)


def gathered(share, tokens_ref, pieces):
    depth = pieces[0].shape[1]
    total = None
    for index, piece in zip((0, 2, 4, 6, 1, 3, 5, 7), pieces):
        start = pl.multiple_of((share ^ index) * depth, depth)
        part = dot_last(piece[...], tokens_ref[:, pl.ds(start, depth)])
        total = part if total is None else total + part
    return total.astype(BF16)


def early_kernel(share_ref, tokens_ref, *refs):
    share = share_ref[0]
    count = len(refs) // (PIECES + 1)
    for turn in range(count):
        refs[PIECES * count + turn][...] = gathered(
            share, tokens_ref, refs[PIECES * turn : PIECES * turn + PIECES]
        )


def late_kernel(share_ref, tokens_ref, weight_ref, *refs):
    share = share_ref[0]
    count = len(refs) // (PIECES + 1)
    for turn in range(count):
        refs[PIECES * count + turn][...] = gathered(
            share, tokens_ref, refs[PIECES * turn : PIECES * turn + PIECES]
        )
    refs[-1][...] = dot_last(weight_ref[...], tokens_ref[...]).astype(BF16)


def features(raw, weighted):
    scale = 1.0 / (math.sqrt(2.0) * math.sqrt(FEAT))
    parts = []
    for shift in range(FEAT // 2 + 1):
        pair = raw * (pltpu.roll(raw, shift, 0) if shift else raw) * scale
        if shift == FEAT // 2:
            pair = pair[: FEAT // 2]
        pair = pair.astype(BF16).astype(F32)
        parts.append(pair * 2.0 if weighted and shift else pair)
    parts.append(raw * FEAT ** (-0.25))
    row = lax.broadcasted_iota(jnp.int32, (8, raw.shape[1]), 0)
    parts.append(jnp.where(row == 0, 1.0, 0.0).astype(F32))
    return jnp.concatenate(parts, axis=0).astype(BF16)


def feature_kernel(place_ref, conv_ref, halo_ref, *refs):
    count = place_ref.shape[0]
    blocks = refs[:count]
    query_ref, key_ref, value_ref, state_ref, wide = refs[count:]
    width = halo_ref.shape[1]
    local_rows = width * count
    wide[:, :width] = halo_ref[...].astype(F32)
    for index, block in enumerate(blocks):
        start = pl.multiple_of((place_ref[index] + 1) * width, LANES)
        wide[:, pl.ds(start, width)] = block[...].astype(F32)
    padded = wide[...]
    convolved = jnp.zeros((padded.shape[0], local_rows), F32)
    taps = conv_ref[...].T
    for offset in range(taps.shape[1]):
        moved = pltpu.roll(padded, offset, 1) if offset else padded
        convolved += taps[:, offset : offset + 1] * moved[:, width:]
    value = convolved[2 * FEAT :].astype(BF16)
    value_ref[...] = value
    query = features(convolved[:FEAT], False)
    query_ref[...] = query.T
    key = features(convolved[FEAT : 2 * FEAT], True)
    key_ref[...] = key
    state_ref[:NUM_FEAT, :] = dot_last(key, value)
    total = dot_last(jnp.ones((8, local_rows), BF16), key)
    lanes = state_ref.shape[1]
    rest = NUM_FEAT - lanes
    more = jnp.concatenate([total[:, lanes:], jnp.zeros((8, lanes - rest), F32)], axis=1)
    row = lax.broadcasted_iota(jnp.int32, (8, lanes), 0)
    state_ref[NUM_FEAT:, :] = jnp.where(row == 0, total[:, :lanes], jnp.where(row == 1, more, 0.0))


def inner_kernel(query_ref, key_ref, value_ref, numerator_ref, denominator_ref):
    local_rows = query_ref.shape[0]
    width = value_ref.shape[0]
    step = LANES
    for start in range(0, local_rows, step):
        size = start + step
        scores = jnp.dot(query_ref[start:size, :], key_ref[:, :size], preferred_element_type=F32)
        row = lax.broadcasted_iota(jnp.int32, (step, size), 0) + start
        column = lax.broadcasted_iota(jnp.int32, (step, size), 1)
        scores = jnp.where(row >= column, scores, 0.0)
        numerator_ref[start:size, :] = dot_last(scores.astype(BF16), value_ref[:, :size])
        denominator_ref[start:size, :] = jnp.broadcast_to(
            jnp.sum(scores, axis=1, keepdims=True), (step, width)
        )


def finish_kernel(query_ref, numerator_ref, denominator_ref, *refs):
    states, out_ref = refs[:-1], refs[-1]
    state = states[0][...]
    for other in states[1:]:
        state += other[...]
    width = numerator_ref.shape[1]
    query = query_ref[...]
    rest = state[:NUM_FEAT, :]
    numerator = numerator_ref[...]
    for _ in range(3):
        part = rest.astype(BF16)
        rest = rest - part.astype(F32)
        numerator += jnp.dot(query, part, preferred_element_type=F32)
    totals = jnp.concatenate(
        [state[NUM_FEAT : NUM_FEAT + 1, :], state[NUM_FEAT + 1 : NUM_FEAT + 2, : NUM_FEAT - width]], axis=1
    )
    denominator = denominator_ref[:, :1] + jnp.sum(query.astype(F32) * totals, axis=1, keepdims=True)
    out_ref[...] = (numerator / denominator).astype(BF16)


def per_device(ctx, tp, tokens, projection, conv_weight):
    both = ("ctx", "tp")
    rows, depth = tokens.shape
    row_width = projection.shape[1]
    val_width = row_width - 2 * FEAT
    local_rows = rows * tp
    turns = range(1, tp // 2)
    me = lax.axis_index("ctx")
    head = lax.axis_index("tp")
    weight = projection.T
    piece = depth // PIECES
    share = me & PIECES - 1

    def swap(array, bit):
        return lax.ppermute(array, "ctx", [(i, i ^ bit) for i in range(ctx)])

    side = share.astype(jnp.int32).reshape(1)
    lag = conv_weight.shape[0] - 1
    cut_rows = PIECES * lag
    mine, tail = call(
        pack_kernel,
        [
            jax.ShapeDtypeStruct((row_width + cut_rows, piece), BF16),
            jax.ShapeDtypeStruct((cut_rows, piece), BF16),
        ],
        [side, hbm(weight), hbm(tokens)],
        1,
        [pltpu.VMEM((HALO, depth), BF16), pltpu.SemaphoreType.DMA((2,))],
        space=HBM,
    )
    pieces = []
    for turn in turns:
        first = lax.ppermute(mine, "tp", [((z + 2 * turn) % tp, z) for z in range(tp)])
        tail = jnp.where(head + 2 * turn == tp - 1, first[row_width:], tail)
        first = first[:row_width]
        parts = [first] + [swap(first, bits) for bits in (2, 4, 6)]
        pieces += parts + [swap(part, 1) for part in parts]
    paired = lax.ppermute(tokens, "tp", [(z, z ^ 1) for z in range(tp)])

    pairs = [(c * tp + z, (c + 1) * tp + z) for c in range(ctx - 1) for z in range(1, tp, 2)]
    ahead = lax.ppermute(tail, both, pairs)
    beside = lax.ppermute(ahead, "tp", [(z, z - 1) for z in range(1, tp, 2)])
    tail = ahead + beside

    shape = jax.ShapeDtypeStruct((row_width, rows), BF16)
    work = 2 * rows * depth * row_width
    halo, own = call(own_kernel, [shape] * 2, [tail, tokens, weight], flops=2 * work)
    early = call(early_kernel, [shape] * len(turns), [side, tokens] + pieces, 1, flops=work)
    *late, other = call(
        late_kernel, [shape] * (len(turns) + 1), [side, paired, weight] + pieces, 1, flops=2 * work
    )
    blocks, places = [own, other], [head, head ^ 1]
    for turn, one, two in zip(turns, early, late):
        pairs = [(z, (z + 2 * turn) % tp) for z in range(tp)]
        source = (head + tp - 2 * turn) % tp
        blocks += [lax.ppermute(one, "tp", pairs), lax.ppermute(two, "tp", pairs)]
        places += [source, source ^ 1]
    place = jnp.stack(places).astype(jnp.int32)
    query, key, value, state = call(
        feature_kernel,
        [
            jax.ShapeDtypeStruct((local_rows, NUM_FEAT), BF16),
            jax.ShapeDtypeStruct((NUM_FEAT, local_rows), BF16),
            jax.ShapeDtypeStruct((val_width, local_rows), BF16),
            jax.ShapeDtypeStruct((STATE_ROWS, val_width), F32),
        ],
        [place, conv_weight, halo] + blocks,
        1,
        [pltpu.VMEM((row_width, rows + local_rows), F32)],
    )
    numerator, denominator = call(
        inner_kernel,
        [jax.ShapeDtypeStruct((local_rows, val_width), F32)] * 2,
        [query, key, value],
        flops=2 * local_rows * local_rows * (NUM_FEAT + val_width),
    )
    received = swap(state, 1)
    terms = [jnp.where(me % 2 == 1, received, 0.0)]
    total = state + received
    bit = 2
    while bit < ctx:
        radix = min(4, ctx // bit)
        last = bit * radix >= ctx
        digit = me // bit % radix
        parts = []
        for delta in range(1, radix):
            pairs = [(c, c ^ delta * bit) for c in range(ctx)]
            parts.append(lax.ppermute(total, "ctx", pairs))
            terms.append(jnp.where(digit > digit ^ delta, parts[-1], 0.0))
        if not last:
            total = functools.reduce(jnp.add, parts, total)
        bit *= radix
    return call(
        finish_kernel,
        [jax.ShapeDtypeStruct((local_rows, val_width), BF16)],
        [query, numerator, denominator] + terms,
        flops=6 * local_rows * NUM_FEAT * val_width,
    )[0]


def solution(mesh):
    ctx, tp = mesh.shape["ctx"], mesh.shape["tp"]
    if tp % 2 or tp < 4 or ctx < 8 or ctx & (ctx - 1):
        raise ValueError("unsupported mesh")

    def body(*arrays):
        return per_device(ctx, tp, *arrays)

    return jax.shard_map(
        body,
        mesh=mesh,
        in_specs=(P(("ctx", "tp"), None), P(None, "tp"), P(None, "tp")),
        out_specs=P("ctx", "tp"),
        check_vma=False,
    )
```

```python
import functools
import math

import jax
import jax.numpy as jnp
from jax import lax
from jax.experimental import pallas as pl
from jax.experimental.pallas import tpu as pltpu
from jax.sharding import PartitionSpec as P


FEAT = 16
HALO = 8
PIECES = 8
LANES = 128
QUAD_FEATS = FEAT * (FEAT + 1) // 2
NUM_FEAT = QUAD_FEATS + FEAT + 8
STATE_ROWS = NUM_FEAT + 8
F32 = jnp.float32
BF16 = jnp.bfloat16
HBM = pl.BlockSpec(memory_space=pltpu.HBM)
VMEM = pl.BlockSpec(memory_space=pltpu.VMEM)
SMEM = pl.BlockSpec(memory_space=pltpu.SMEM)
LAST = (((1,), (1,)), ((), ()))


def call(kernel, outs, operands, scalars=0, scratch=(), flops=1 << 20, moved=1 << 20, space=VMEM):
    return pl.pallas_call(
        kernel,
        out_shape=outs,
        in_specs=[SMEM] * scalars + [space] * (len(operands) - scalars),
        out_specs=[VMEM] * len(outs),
        scratch_shapes=list(scratch),
        compiler_params=pltpu.CompilerParams(vmem_limit_bytes=16 << 20),
        cost_estimate=pl.CostEstimate(flops=flops, bytes_accessed=moved, transcendentals=0),
    )(*operands)


def hbm(array):
    return pltpu.with_memory_space_constraint(array, pltpu.HBM)


def dot_last(left, right):
    return lax.dot_general(left, right, LAST, preferred_element_type=F32)


def pack_kernel(share_ref, weight_ref, tokens_ref, sent_ref, last_ref, sems):
    width = sent_ref.shape[1]
    start = pl.multiple_of(share_ref[0] * width, LANES)
    weights = pltpu.make_async_copy(weight_ref.at[:, pl.ds(start, width)], sent_ref, sems.at[0])
    last = pltpu.make_async_copy(
        tokens_ref.at[tokens_ref.shape[0] - HALO :, :], last_ref, sems.at[1]
    )
    weights.start()
    last.start()
    weights.wait()
    last.wait()


def own_kernel(tail_ref, tokens_ref, weight_ref, halo_ref, own_ref):
    weight = weight_ref[...]
    own_ref[...] = dot_last(weight, tokens_ref[...]).astype(BF16)
    padded = jnp.concatenate(
        [jnp.zeros((halo_ref.shape[1] - HALO, tail_ref.shape[1]), BF16), tail_ref[...]], axis=0
    )
    halo_ref[...] = dot_last(weight, padded).astype(BF16)


def gathered(share, tokens_ref, pieces):
    depth = pieces[0].shape[1]
    total = None
    for index, piece in zip((0, 2, 4, 6, 1, 3, 5, 7), pieces):
        start = pl.multiple_of((share ^ index) * depth, depth)
        part = dot_last(piece[...], tokens_ref[:, pl.ds(start, depth)])
        total = part if total is None else total + part
    return total.astype(BF16)


def early_kernel(share_ref, tokens_ref, *refs):
    share = share_ref[0]
    count = len(refs) // (PIECES + 1)
    for turn in range(count):
        refs[PIECES * count + turn][...] = gathered(
            share, tokens_ref, refs[PIECES * turn : PIECES * turn + PIECES]
        )


def late_kernel(share_ref, tokens_ref, weight_ref, *refs):
    share = share_ref[0]
    count = len(refs) // (PIECES + 1)
    for turn in range(count):
        refs[PIECES * count + turn][...] = gathered(
            share, tokens_ref, refs[PIECES * turn : PIECES * turn + PIECES]
        )
    refs[-1][...] = dot_last(weight_ref[...], tokens_ref[...]).astype(BF16)


def features(raw, weighted):
    scale = 1.0 / (math.sqrt(2.0) * math.sqrt(FEAT))
    parts = []
    for shift in range(FEAT // 2 + 1):
        pair = raw * (pltpu.roll(raw, shift, 0) if shift else raw) * scale
        if shift == FEAT // 2:
            pair = pair[: FEAT // 2]
        pair = pair.astype(BF16).astype(F32)
        parts.append(pair * 2.0 if weighted and shift else pair)
    parts.append(raw * FEAT ** (-0.25))
    row = lax.broadcasted_iota(jnp.int32, (8, raw.shape[1]), 0)
    parts.append(jnp.where(row == 0, 1.0, 0.0).astype(F32))
    return jnp.concatenate(parts, axis=0).astype(BF16)


def feature_kernel(place_ref, conv_ref, halo_ref, *refs):
    count = place_ref.shape[0]
    blocks = refs[:count]
    query_ref, key_ref, value_ref, state_ref, wide = refs[count:]
    width = halo_ref.shape[1]
    local_rows = width * count
    wide[:, :width] = halo_ref[...].astype(F32)
    for index, block in enumerate(blocks):
        start = pl.multiple_of((place_ref[index] + 1) * width, LANES)
        wide[:, pl.ds(start, width)] = block[...].astype(F32)
    padded = wide[...]
    convolved = jnp.zeros((padded.shape[0], local_rows), F32)
    taps = conv_ref[...].T
    for offset in range(taps.shape[1]):
        moved = pltpu.roll(padded, offset, 1) if offset else padded
        convolved += taps[:, offset : offset + 1] * moved[:, width:]
    value = convolved[2 * FEAT :].astype(BF16)
    value_ref[...] = value
    query = features(convolved[:FEAT], False)
    query_ref[...] = query.T
    key = features(convolved[FEAT : 2 * FEAT], True)
    key_ref[...] = key
    state_ref[:NUM_FEAT, :] = dot_last(key, value)
    total = dot_last(jnp.ones((8, local_rows), BF16), key)
    lanes = state_ref.shape[1]
    rest = NUM_FEAT - lanes
    more = jnp.concatenate([total[:, lanes:], jnp.zeros((8, lanes - rest), F32)], axis=1)
    row = lax.broadcasted_iota(jnp.int32, (8, lanes), 0)
    state_ref[NUM_FEAT:, :] = jnp.where(row == 0, total[:, :lanes], jnp.where(row == 1, more, 0.0))


def inner_kernel(query_ref, key_ref, value_ref, numerator_ref, denominator_ref):
    local_rows = query_ref.shape[0]
    width = value_ref.shape[0]
    step = LANES
    for start in range(0, local_rows, step):
        size = start + step
        scores = jnp.dot(query_ref[start:size, :], key_ref[:, :size], preferred_element_type=F32)
        row = lax.broadcasted_iota(jnp.int32, (step, size), 0) + start
        column = lax.broadcasted_iota(jnp.int32, (step, size), 1)
        scores = jnp.where(row >= column, scores, 0.0)
        numerator_ref[start:size, :] = dot_last(scores.astype(BF16), value_ref[:, :size])
        denominator_ref[start:size, :] = jnp.broadcast_to(
            jnp.sum(scores, axis=1, keepdims=True), (step, width)
        )


def finish_kernel(query_ref, numerator_ref, denominator_ref, *refs):
    states, out_ref = refs[:-1], refs[-1]
    state = states[0][...]
    for other in states[1:]:
        state += other[...]
    width = numerator_ref.shape[1]
    query = query_ref[...]
    rest = state[:NUM_FEAT, :]
    numerator = numerator_ref[...]
    for _ in range(3):
        part = rest.astype(BF16)
        rest = rest - part.astype(F32)
        numerator += jnp.dot(query, part, preferred_element_type=F32)
    totals = jnp.concatenate(
        [state[NUM_FEAT : NUM_FEAT + 1, :], state[NUM_FEAT + 1 : NUM_FEAT + 2, : NUM_FEAT - width]], axis=1
    )
    denominator = denominator_ref[:, :1] + jnp.sum(query.astype(F32) * totals, axis=1, keepdims=True)
    out_ref[...] = (numerator / denominator).astype(BF16)


def per_device(ctx, tp, tokens, projection, conv_weight):
    both = ("ctx", "tp")
    rows, depth = tokens.shape
    row_width = projection.shape[1]
    val_width = row_width - 2 * FEAT
    local_rows = rows * tp
    turns = range(1, tp // 2)
    me = lax.axis_index("ctx")
    head = lax.axis_index("tp")
    weight = projection.T
    piece = depth // PIECES
    share = me & PIECES - 1

    def swap(array, bit):
        return lax.ppermute(array, "ctx", [(i, i ^ bit) for i in range(ctx)])

    side = share.astype(jnp.int32).reshape(1)
    mine, last_rows = call(
        pack_kernel,
        [
            jax.ShapeDtypeStruct((row_width, piece), BF16),
            jax.ShapeDtypeStruct((HALO, depth), BF16),
        ],
        [side, hbm(weight), hbm(tokens)],
        1,
        [pltpu.SemaphoreType.DMA((2,))],
        space=HBM,
    )
    pieces = []
    for turn in turns:
        first = lax.ppermute(mine, "tp", [((z + 2 * turn) % tp, z) for z in range(tp)])
        parts = [first] + [swap(first, bits) for bits in (2, 4, 6)]
        pieces += parts + [swap(part, 1) for part in parts]
    paired = lax.ppermute(tokens, "tp", [(z, z ^ 1) for z in range(tp)])

    tail = None
    for z in range(tp):
        pairs = [((c - 1) * tp + tp - 1, c * tp + z) for c in range(1, ctx)]
        part = lax.ppermute(last_rows, both, pairs)
        tail = part if tail is None else tail + part

    shape = jax.ShapeDtypeStruct((row_width, rows), BF16)
    work = 2 * rows * depth * row_width
    halo, own = call(own_kernel, [shape] * 2, [tail, tokens, weight], flops=2 * work)
    early = call(early_kernel, [shape] * len(turns), [side, tokens] + pieces, 1, flops=work)
    *late, other = call(
        late_kernel, [shape] * (len(turns) + 1), [side, paired, weight] + pieces, 1, flops=2 * work
    )
    blocks, places = [own, other], [head, head ^ 1]
    for turn, one, two in zip(turns, early, late):
        pairs = [(z, (z + 2 * turn) % tp) for z in range(tp)]
        source = (head + tp - 2 * turn) % tp
        blocks += [lax.ppermute(one, "tp", pairs), lax.ppermute(two, "tp", pairs)]
        places += [source, source ^ 1]
    place = jnp.stack(places).astype(jnp.int32)
    query, key, value, state = call(
        feature_kernel,
        [
            jax.ShapeDtypeStruct((local_rows, NUM_FEAT), BF16),
            jax.ShapeDtypeStruct((NUM_FEAT, local_rows), BF16),
            jax.ShapeDtypeStruct((val_width, local_rows), BF16),
            jax.ShapeDtypeStruct((STATE_ROWS, val_width), F32),
        ],
        [place, conv_weight, halo] + blocks,
        1,
        [pltpu.VMEM((row_width, rows + local_rows), F32)],
    )
    numerator, denominator = call(
        inner_kernel,
        [jax.ShapeDtypeStruct((local_rows, val_width), F32)] * 2,
        [query, key, value],
        flops=2 * local_rows * local_rows * (NUM_FEAT + val_width),
    )
    received = swap(state, 1)
    terms = [jnp.where(me % 2 == 1, received, 0.0)]
    total = state + received
    bit = 2
    while bit < ctx:
        radix = min(4, ctx // bit)
        last = bit * radix >= ctx
        digit = me // bit % radix
        parts = []
        for delta in range(1, radix):
            pairs = [(c, c ^ delta * bit) for c in range(ctx)]
            parts.append(lax.ppermute(total, "ctx", pairs))
            terms.append(jnp.where(digit > digit ^ delta, parts[-1], 0.0))
        if not last:
            total = functools.reduce(jnp.add, parts, total)
        bit *= radix
    return call(
        finish_kernel,
        [jax.ShapeDtypeStruct((local_rows, val_width), BF16)],
        [query, numerator, denominator] + terms,
        flops=6 * local_rows * NUM_FEAT * val_width,
    )[0]


def solution(mesh):
    ctx, tp = mesh.shape["ctx"], mesh.shape["tp"]
    if tp % 2 or tp < 4 or ctx < 8 or ctx & (ctx - 1):
        raise ValueError("unsupported mesh")

    def body(*arrays):
        return per_device(ctx, tp, *arrays)

    return jax.shard_map(
        body,
        mesh=mesh,
        in_specs=(P(("ctx", "tp"), None), P(None, "tp"), P(None, "tp")),
        out_specs=P("ctx", "tp"),
        check_vma=False,
    )
```

```python
import functools
import math

import jax
import jax.numpy as jnp
from jax import lax
from jax.experimental import pallas as pl
from jax.experimental.pallas import tpu as pltpu
from jax.sharding import PartitionSpec as P


FEAT = 16
HALO = 8
PIECES = 8
LANES = 128
QUAD_FEATS = FEAT * (FEAT + 1) // 2
NUM_FEAT = QUAD_FEATS + FEAT + 8
STATE_ROWS = NUM_FEAT + 8
F32 = jnp.float32
BF16 = jnp.bfloat16
HBM = pl.BlockSpec(memory_space=pltpu.HBM)
VMEM = pl.BlockSpec(memory_space=pltpu.VMEM)
SMEM = pl.BlockSpec(memory_space=pltpu.SMEM)
LAST = (((1,), (1,)), ((), ()))


def call(kernel, outs, operands, scalars=0, scratch=(), flops=1 << 20, moved=1 << 20, space=VMEM):
    return pl.pallas_call(
        kernel,
        out_shape=outs,
        in_specs=[SMEM] * scalars + [space] * (len(operands) - scalars),
        out_specs=[VMEM] * len(outs),
        scratch_shapes=list(scratch),
        compiler_params=pltpu.CompilerParams(vmem_limit_bytes=16 << 20),
        cost_estimate=pl.CostEstimate(flops=flops, bytes_accessed=moved, transcendentals=0),
    )(*operands)


def hbm(array):
    return pltpu.with_memory_space_constraint(array, pltpu.HBM)


def dot_last(left, right):
    return lax.dot_general(left, right, LAST, preferred_element_type=F32)


def pack_kernel(share_ref, weight_ref, tokens_ref, sent_ref, tail_ref, last_ref, sems):
    height, width = weight_ref.shape[0], sent_ref.shape[1]
    start = pl.multiple_of(share_ref[0] * width, LANES)
    weight_copy = pltpu.make_async_copy(
        weight_ref.at[:, pl.ds(start, width)], sent_ref.at[:height, :], sems.at[0]
    )
    tokens_copy = pltpu.make_async_copy(
        tokens_ref.at[tokens_ref.shape[0] - HALO :, :], last_ref, sems.at[1]
    )
    tokens_copy.start()
    weight_copy.start()
    tokens_copy.wait()
    lag = tail_ref.shape[0] // PIECES
    rows = last_ref[...].astype(F32)
    cuts = []
    for row in range(HALO - lag, HALO):
        cuts += [rows[row : row + 1, index * width : index * width + width] for index in range(PIECES)]
    tail = jnp.concatenate(cuts, axis=0).astype(BF16)
    sent_ref[height:, :] = tail
    tail_ref[...] = tail
    weight_copy.wait()


def own_kernel(tokens_ref, weight_ref, own_ref):
    own_ref[...] = dot_last(weight_ref[...], tokens_ref[...]).astype(BF16)


def halo_kernel(tail_ref, weight_ref, halo_ref):
    depth = weight_ref.shape[1]
    cuts = tail_ref[...].astype(F32)
    lag = cuts.shape[0] // PIECES
    rows = [jnp.zeros((halo_ref.shape[1] - lag, depth), F32)]
    for row in range(lag):
        first = row * PIECES
        rows.append(
            jnp.concatenate([cuts[first + i : first + i + 1, :] for i in range(PIECES)], axis=1)
        )
    padded = jnp.concatenate(rows, axis=0).astype(BF16)
    halo_ref[...] = dot_last(weight_ref[...], padded).astype(BF16)


def gathered(share, tokens_ref, pieces, height):
    depth = pieces[0].shape[1]
    total = None
    for index, piece in zip((0, 2, 4, 6, 1, 3, 5, 7), pieces):
        start = pl.multiple_of((share ^ index) * depth, depth)
        part = dot_last(piece[:height, :], tokens_ref[:, pl.ds(start, depth)])
        total = part if total is None else total + part
    return total.astype(BF16)


def early_kernel(share_ref, tokens_ref, *refs):
    share = share_ref[0]
    count = len(refs) // (PIECES + 1)
    for turn in range(count):
        refs[PIECES * count + turn][...] = gathered(
            share, tokens_ref, refs[PIECES * turn : PIECES * turn + PIECES], refs[-1].shape[0]
        )


def late_kernel(share_ref, tokens_ref, weight_ref, *refs):
    share = share_ref[0]
    count = len(refs) // (PIECES + 1)
    for turn in range(count):
        refs[PIECES * count + turn][...] = gathered(
            share, tokens_ref, refs[PIECES * turn : PIECES * turn + PIECES], refs[-1].shape[0]
        )
    refs[-1][...] = dot_last(weight_ref[...], tokens_ref[...]).astype(BF16)


def features(raw, weighted):
    scale = 1.0 / (math.sqrt(2.0) * math.sqrt(FEAT))
    parts = []
    for shift in range(FEAT // 2 + 1):
        pair = raw * (pltpu.roll(raw, shift, 0) if shift else raw) * scale
        if shift == FEAT // 2:
            pair = pair[: FEAT // 2]
        pair = pair.astype(BF16).astype(F32)
        parts.append(pair * 2.0 if weighted and shift else pair)
    parts.append(raw * FEAT ** (-0.25))
    row = lax.broadcasted_iota(jnp.int32, (8, raw.shape[1]), 0)
    parts.append(jnp.where(row == 0, 1.0, 0.0).astype(F32))
    return jnp.concatenate(parts, axis=0).astype(BF16)


def feature_kernel(place_ref, conv_ref, halo_ref, *refs):
    count = place_ref.shape[0]
    blocks = refs[:count]
    query_ref, key_ref, value_ref, state_ref, wide = refs[count:]
    width = halo_ref.shape[1]
    local_rows = width * count
    wide[:, :width] = halo_ref[...].astype(F32)
    for index, block in enumerate(blocks):
        start = pl.multiple_of((place_ref[index] + 1) * width, LANES)
        wide[:, pl.ds(start, width)] = block[...].astype(F32)
    padded = wide[...]
    convolved = jnp.zeros((padded.shape[0], local_rows), F32)
    taps = conv_ref[...].T
    for offset in range(taps.shape[1]):
        moved = pltpu.roll(padded, offset, 1) if offset else padded
        convolved += taps[:, offset : offset + 1] * moved[:, width:]
    value = convolved[2 * FEAT :].astype(BF16)
    value_ref[...] = value
    query = features(convolved[:FEAT], False)
    query_ref[...] = query.T
    key = features(convolved[FEAT : 2 * FEAT], True)
    key_ref[...] = key
    state_ref[:NUM_FEAT, :] = dot_last(key, value)
    total = dot_last(jnp.ones((8, local_rows), BF16), key)
    lanes = state_ref.shape[1]
    rest = NUM_FEAT - lanes
    more = jnp.concatenate([total[:, lanes:], jnp.zeros((8, lanes - rest), F32)], axis=1)
    row = lax.broadcasted_iota(jnp.int32, (8, lanes), 0)
    state_ref[NUM_FEAT:, :] = jnp.where(row == 0, total[:, :lanes], jnp.where(row == 1, more, 0.0))


def inner_kernel(query_ref, key_ref, value_ref, numerator_ref, denominator_ref):
    local_rows = query_ref.shape[0]
    width = value_ref.shape[0]
    step = LANES
    for start in range(0, local_rows, step):
        size = start + step
        scores = jnp.dot(query_ref[start:size, :], key_ref[:, :size], preferred_element_type=F32)
        row = lax.broadcasted_iota(jnp.int32, (step, size), 0) + start
        column = lax.broadcasted_iota(jnp.int32, (step, size), 1)
        scores = jnp.where(row >= column, scores, 0.0)
        numerator_ref[start:size, :] = dot_last(scores.astype(BF16), value_ref[:, :size])
        denominator_ref[start:size, :] = jnp.broadcast_to(
            jnp.sum(scores, axis=1, keepdims=True), (step, width)
        )


def finish_kernel(query_ref, numerator_ref, denominator_ref, *refs):
    states, out_ref = refs[:-1], refs[-1]
    state = states[0][...]
    for other in states[1:]:
        state += other[...]
    width = numerator_ref.shape[1]
    query = query_ref[...]
    rest = state[:NUM_FEAT, :]
    numerator = numerator_ref[...]
    for _ in range(3):
        part = rest.astype(BF16)
        rest = rest - part.astype(F32)
        numerator += jnp.dot(query, part, preferred_element_type=F32)
    totals = jnp.concatenate(
        [state[NUM_FEAT : NUM_FEAT + 1, :], state[NUM_FEAT + 1 : NUM_FEAT + 2, : NUM_FEAT - width]], axis=1
    )
    denominator = denominator_ref[:, :1] + jnp.sum(query.astype(F32) * totals, axis=1, keepdims=True)
    out_ref[...] = (numerator / denominator).astype(BF16)


def per_device(ctx, tp, tokens, projection, conv_weight):
    both = ("ctx", "tp")
    rows, depth = tokens.shape
    row_width = projection.shape[1]
    val_width = row_width - 2 * FEAT
    local_rows = rows * tp
    turns = range(1, tp // 2)
    me = lax.axis_index("ctx")
    head = lax.axis_index("tp")
    weight = projection.T
    piece = depth // PIECES
    share = me & PIECES - 1

    def swap(array, bit):
        return lax.ppermute(array, "ctx", [(i, i ^ bit) for i in range(ctx)])

    side = share.astype(jnp.int32).reshape(1)
    cut_rows = PIECES * (conv_weight.shape[0] - 1)
    mine, tail = call(
        pack_kernel,
        [
            jax.ShapeDtypeStruct((row_width + cut_rows, piece), BF16),
            jax.ShapeDtypeStruct((cut_rows, piece), BF16),
        ],
        [side, hbm(weight), hbm(tokens)],
        1,
        [pltpu.VMEM((HALO, depth), BF16), pltpu.SemaphoreType.DMA((2,))],
        space=HBM,
    )
    shape = jax.ShapeDtypeStruct((row_width, rows), BF16)
    work = 2 * rows * depth * row_width
    row = lax.broadcasted_iota(jnp.int32, mine.shape, 0)
    replaced = (row >= row_width) & (head == tp - 1)
    pieces, tails = [], []
    for turn in turns:
        first = lax.ppermute(mine, "tp", [((z + 2 * turn) % tp, z) for z in range(tp)])
        first = jnp.where(replaced, mine, first)
        parts = [first] + [swap(first, bits) for bits in (2, 4, 6)]
        parts += [swap(part, 1) for part in parts]
        pieces += parts
        one, two, three = (part[row_width:] for part in (parts[4], parts[5], parts[7]))
        tails.append(jnp.where(me & 1 == 1, one, jnp.where(me & 2 == 2, two, three)))
    tail = tails[0]
    for turn in turns[1:]:
        tail = jnp.where(head + 2 * turn == tp - 1, tails[turn - 1], tail)
    odd = range(1, tp, 2)
    if ctx > PIECES:
        last = jnp.where(head == tp - 1, mine, first)[row_width:]
        for turn in turns:
            last = jnp.where(head + 2 * turn == tp - 1, pieces[PIECES * turn - PIECES][row_width:], last)
        pairs = [((c - 1) * tp + z, c * tp + z) for c in range(PIECES, ctx, PIECES) for z in odd]
        tail = jnp.where(me % PIECES == 0, lax.ppermute(last, both, pairs), tail)
    else:
        tail = jnp.where(me == 0, jnp.zeros_like(tail), tail)
    beside = lax.ppermute(tail, "tp", [(z, z - 1) for z in odd])
    tail = jnp.where(head % 2 == 1, tail, beside)
    paired = lax.ppermute(tokens, "tp", [(z, z ^ 1) for z in range(tp)])
    own = call(own_kernel, [shape], [tokens, weight], flops=work)[0]
    halo = call(halo_kernel, [shape], [tail, weight], flops=work)[0]
    early = call(early_kernel, [shape] * len(turns), [side, tokens] + pieces, 1, flops=work)
    *late, other = call(
        late_kernel, [shape] * (len(turns) + 1), [side, paired, weight] + pieces, 1, flops=2 * work
    )
    blocks, places = [own, other], [head, head ^ 1]
    for turn, one, two in zip(turns, early, late):
        pairs = [(z, (z + 2 * turn) % tp) for z in range(tp)]
        source = (head + tp - 2 * turn) % tp
        blocks += [lax.ppermute(one, "tp", pairs), lax.ppermute(two, "tp", pairs)]
        places += [source, source ^ 1]
    place = jnp.stack(places).astype(jnp.int32)
    query, key, value, state = call(
        feature_kernel,
        [
            jax.ShapeDtypeStruct((local_rows, NUM_FEAT), BF16),
            jax.ShapeDtypeStruct((NUM_FEAT, local_rows), BF16),
            jax.ShapeDtypeStruct((val_width, local_rows), BF16),
            jax.ShapeDtypeStruct((STATE_ROWS, val_width), F32),
        ],
        [place, conv_weight, halo] + blocks,
        1,
        [pltpu.VMEM((row_width, rows + local_rows), F32)],
    )
    numerator, denominator = call(
        inner_kernel,
        [jax.ShapeDtypeStruct((local_rows, val_width), F32)] * 2,
        [query, key, value],
        flops=2 * local_rows * local_rows * (NUM_FEAT + val_width),
    )
    received = swap(state, 1)
    terms = [jnp.where(me % 2 == 1, received, 0.0)]
    total = state + received
    bit = 2
    while bit < ctx:
        radix = min(4, ctx // bit)
        last = bit * radix >= ctx
        digit = me // bit % radix
        parts = []
        for delta in range(1, radix):
            pairs = [(c, c ^ delta * bit) for c in range(ctx)]
            parts.append(lax.ppermute(total, "ctx", pairs))
            terms.append(jnp.where(digit > digit ^ delta, parts[-1], 0.0))
        if not last:
            total = functools.reduce(jnp.add, parts, total)
        bit *= radix
    return call(
        finish_kernel,
        [jax.ShapeDtypeStruct((local_rows, val_width), BF16)],
        [query, numerator, denominator] + terms,
        flops=6 * local_rows * NUM_FEAT * val_width,
    )[0]


def solution(mesh):
    ctx, tp = mesh.shape["ctx"], mesh.shape["tp"]
    if tp % 2 or tp < 4 or ctx < 8 or ctx & (ctx - 1):
        raise ValueError("unsupported mesh")

    def body(*arrays):
        return per_device(ctx, tp, *arrays)

    return jax.shard_map(
        body,
        mesh=mesh,
        in_specs=(P(("ctx", "tp"), None), P(None, "tp"), P(None, "tp")),
        out_specs=P("ctx", "tp"),
        check_vma=False,
    )
```

```python
import functools
import math

import jax
import jax.numpy as jnp
from jax import lax
from jax.experimental import pallas as pl
from jax.experimental.pallas import tpu as pltpu
from jax.sharding import PartitionSpec as P


FEAT = 16
HALO = 8
PIECES = 8
LANES = 128
QUAD_FEATS = FEAT * (FEAT + 1) // 2
NUM_FEAT = QUAD_FEATS + FEAT + 8
STATE_ROWS = NUM_FEAT + 8
F32 = jnp.float32
BF16 = jnp.bfloat16
HBM = pl.BlockSpec(memory_space=pltpu.HBM)
VMEM = pl.BlockSpec(memory_space=pltpu.VMEM)
SMEM = pl.BlockSpec(memory_space=pltpu.SMEM)
LAST = (((1,), (1,)), ((), ()))


def call(kernel, outs, operands, scalars=0, scratch=(), flops=1 << 20, moved=1 << 20, space=VMEM):
    return pl.pallas_call(
        kernel,
        out_shape=outs,
        in_specs=[SMEM] * scalars + [space] * (len(operands) - scalars),
        out_specs=[VMEM] * len(outs),
        scratch_shapes=list(scratch),
        compiler_params=pltpu.CompilerParams(vmem_limit_bytes=16 << 20),
        cost_estimate=pl.CostEstimate(flops=flops, bytes_accessed=moved, transcendentals=0),
    )(*operands)


def hbm(array):
    return pltpu.with_memory_space_constraint(array, pltpu.HBM)


def dot_last(left, right):
    return lax.dot_general(left, right, LAST, preferred_element_type=F32)


def pack_kernel(share_ref, weight_ref, tokens_ref, sent_ref, last_ref, sems):
    width = sent_ref.shape[1]
    start = pl.multiple_of(share_ref[0] * width, LANES)
    weights = pltpu.make_async_copy(weight_ref.at[:, pl.ds(start, width)], sent_ref, sems.at[0])
    last = pltpu.make_async_copy(
        tokens_ref.at[tokens_ref.shape[0] - HALO :, :], last_ref, sems.at[1]
    )
    weights.start()
    last.start()
    weights.wait()
    last.wait()


def own_kernel(tail_ref, tokens_ref, weight_ref, halo_ref, own_ref):
    weight = weight_ref[...]
    own_ref[...] = dot_last(weight, tokens_ref[...]).astype(BF16)
    padded = jnp.concatenate(
        [jnp.zeros((halo_ref.shape[1] - HALO, tail_ref.shape[1]), BF16), tail_ref[...]], axis=0
    )
    halo_ref[...] = dot_last(weight, padded).astype(BF16)


def second_kernel(share_ref, tokens_ref, paired_ref, weight_ref, *refs):
    share = share_ref[0]
    count = (len(refs) - 1) // (PIECES + 1)
    height, rows = refs[-1].shape
    for turn in range(count):
        total = None
        for index, piece in zip((0, 2, 4, 6, 1, 3, 5, 7), refs[PIECES * turn : PIECES * turn + PIECES]):
            depth = piece.shape[1]
            start = pl.multiple_of((share ^ index) * depth, depth)
            both = jnp.concatenate(
                [tokens_ref[:, pl.ds(start, depth)], paired_ref[:, pl.ds(start, depth)]], axis=0
            )
            part = dot_last(piece[...], both)
            total = part if total is None else total + part
        out_ref = refs[PIECES * count + turn]
        out_ref[:height, :] = total[:, :rows].astype(BF16)
        out_ref[height:, :] = total[:, rows:].astype(BF16)
    refs[-1][...] = dot_last(weight_ref[...], paired_ref[...]).astype(BF16)


def features(raw, weighted):
    scale = 1.0 / (math.sqrt(2.0) * math.sqrt(FEAT))
    parts = []
    for shift in range(FEAT // 2 + 1):
        pair = raw * (pltpu.roll(raw, shift, 0) if shift else raw) * scale
        if shift == FEAT // 2:
            pair = pair[: FEAT // 2]
        pair = pair.astype(BF16).astype(F32)
        parts.append(pair * 2.0 if weighted and shift else pair)
    parts.append(raw * FEAT ** (-0.25))
    row = lax.broadcasted_iota(jnp.int32, (8, raw.shape[1]), 0)
    parts.append(jnp.where(row == 0, 1.0, 0.0).astype(F32))
    return jnp.concatenate(parts, axis=0).astype(BF16)


def feature_kernel(place_ref, conv_ref, halo_ref, *refs):
    count = place_ref.shape[0]
    query_ref, key_ref, value_ref, state_ref, wide = refs[-5:]
    width = halo_ref.shape[1]
    height = wide.shape[0]
    blocks = [refs[0][...], refs[1][...]]
    for message in refs[2:-5]:
        blocks += [message[:height, :], message[height:, :]]
    local_rows = width * count
    wide[:, :width] = halo_ref[...].astype(F32)
    for index, block in enumerate(blocks):
        start = pl.multiple_of((place_ref[index] + 1) * width, LANES)
        wide[:, pl.ds(start, width)] = block.astype(F32)
    padded = wide[...]
    convolved = jnp.zeros((padded.shape[0], local_rows), F32)
    taps = conv_ref[...].T
    for offset in range(taps.shape[1]):
        moved = pltpu.roll(padded, offset, 1) if offset else padded
        convolved += taps[:, offset : offset + 1] * moved[:, width:]
    value = convolved[2 * FEAT :].astype(BF16)
    value_ref[...] = value
    query = features(convolved[:FEAT], False)
    query_ref[...] = query.T
    key = features(convolved[FEAT : 2 * FEAT], True)
    key_ref[...] = key
    state_ref[:NUM_FEAT, :] = dot_last(key, value)
    total = dot_last(jnp.ones((8, local_rows), BF16), key)
    lanes = state_ref.shape[1]
    rest = NUM_FEAT - lanes
    more = jnp.concatenate([total[:, lanes:], jnp.zeros((8, lanes - rest), F32)], axis=1)
    row = lax.broadcasted_iota(jnp.int32, (8, lanes), 0)
    state_ref[NUM_FEAT:, :] = jnp.where(row == 0, total[:, :lanes], jnp.where(row == 1, more, 0.0))


def inner_kernel(query_ref, key_ref, value_ref, numerator_ref, denominator_ref):
    local_rows = query_ref.shape[0]
    width = value_ref.shape[0]
    step = LANES
    for start in range(0, local_rows, step):
        size = start + step
        scores = jnp.dot(query_ref[start:size, :], key_ref[:, :size], preferred_element_type=F32)
        row = lax.broadcasted_iota(jnp.int32, (step, size), 0) + start
        column = lax.broadcasted_iota(jnp.int32, (step, size), 1)
        scores = jnp.where(row >= column, scores, 0.0)
        numerator_ref[start:size, :] = dot_last(scores.astype(BF16), value_ref[:, :size])
        denominator_ref[start:size, :] = jnp.broadcast_to(
            jnp.sum(scores, axis=1, keepdims=True), (step, width)
        )


def finish_kernel(query_ref, numerator_ref, denominator_ref, *refs):
    states, out_ref = refs[:-1], refs[-1]
    state = states[0][...]
    for other in states[1:]:
        state += other[...]
    width = numerator_ref.shape[1]
    query = query_ref[...]
    rest = state[:NUM_FEAT, :]
    numerator = numerator_ref[...]
    for _ in range(3):
        part = rest.astype(BF16)
        rest = rest - part.astype(F32)
        numerator += jnp.dot(query, part, preferred_element_type=F32)
    totals = jnp.concatenate(
        [state[NUM_FEAT : NUM_FEAT + 1, :], state[NUM_FEAT + 1 : NUM_FEAT + 2, : NUM_FEAT - width]], axis=1
    )
    denominator = denominator_ref[:, :1] + jnp.sum(query.astype(F32) * totals, axis=1, keepdims=True)
    out_ref[...] = (numerator / denominator).astype(BF16)


def per_device(ctx, tp, tokens, projection, conv_weight):
    both = ("ctx", "tp")
    rows, depth = tokens.shape
    row_width = projection.shape[1]
    val_width = row_width - 2 * FEAT
    local_rows = rows * tp
    turns = range(1, tp // 2)
    me = lax.axis_index("ctx")
    head = lax.axis_index("tp")
    weight = projection.T
    piece = depth // PIECES
    share = me & PIECES - 1

    def swap(array, bit):
        return lax.ppermute(array, "ctx", [(i, i ^ bit) for i in range(ctx)])

    side = share.astype(jnp.int32).reshape(1)
    mine, last_rows = call(
        pack_kernel,
        [
            jax.ShapeDtypeStruct((row_width, piece), BF16),
            jax.ShapeDtypeStruct((HALO, depth), BF16),
        ],
        [side, hbm(weight), hbm(tokens)],
        1,
        [pltpu.SemaphoreType.DMA((2,))],
        space=HBM,
    )
    pieces = []
    for turn in turns:
        first = lax.ppermute(mine, "tp", [((z + 2 * turn) % tp, z) for z in range(tp)])
        parts = [first] + [swap(first, bits) for bits in (2, 4, 6)]
        pieces += parts + [swap(part, 1) for part in parts]
    paired = lax.ppermute(tokens, "tp", [(z, z ^ 1) for z in range(tp)])

    tail = None
    for z in range(tp):
        pairs = [((c - 1) * tp + tp - 1, c * tp + z) for c in range(1, ctx)]
        part = lax.ppermute(last_rows, both, pairs)
        tail = part if tail is None else tail + part

    shape = jax.ShapeDtypeStruct((row_width, rows), BF16)
    work = 2 * rows * depth * row_width
    halo, own = call(own_kernel, [shape] * 2, [tail, tokens, weight], flops=2 * work)
    pair_shape = jax.ShapeDtypeStruct((2 * row_width, rows), BF16)
    *messages, other = call(
        second_kernel,
        [pair_shape] * len(turns) + [shape],
        [side, tokens, paired, weight] + pieces,
        1,
        flops=3 * work,
    )
    blocks, places = [own, other], [head, head ^ 1]
    for turn, message in zip(turns, messages):
        blocks.append(lax.ppermute(message, "tp", [(z, (z + 2 * turn) % tp) for z in range(tp)]))
        source = (head + tp - 2 * turn) % tp
        places += [source, source ^ 1]
    place = jnp.stack(places).astype(jnp.int32)
    query, key, value, state = call(
        feature_kernel,
        [
            jax.ShapeDtypeStruct((local_rows, NUM_FEAT), BF16),
            jax.ShapeDtypeStruct((NUM_FEAT, local_rows), BF16),
            jax.ShapeDtypeStruct((val_width, local_rows), BF16),
            jax.ShapeDtypeStruct((STATE_ROWS, val_width), F32),
        ],
        [place, conv_weight, halo] + blocks,
        1,
        [pltpu.VMEM((row_width, rows + local_rows), F32)],
    )
    numerator, denominator = call(
        inner_kernel,
        [jax.ShapeDtypeStruct((local_rows, val_width), F32)] * 2,
        [query, key, value],
        flops=2 * local_rows * local_rows * (NUM_FEAT + val_width),
    )
    received = swap(state, 1)
    terms = [jnp.where(me % 2 == 1, received, 0.0)]
    total = state + received
    bit = 2
    while bit < ctx:
        radix = min(4, ctx // bit)
        last = bit * radix >= ctx
        digit = me // bit % radix
        parts = []
        for delta in range(1, radix):
            pairs = [(c, c ^ delta * bit) for c in range(ctx)]
            parts.append(lax.ppermute(total, "ctx", pairs))
            terms.append(jnp.where(digit > digit ^ delta, parts[-1], 0.0))
        if not last:
            total = functools.reduce(jnp.add, parts, total)
        bit *= radix
    return call(
        finish_kernel,
        [jax.ShapeDtypeStruct((local_rows, val_width), BF16)],
        [query, numerator, denominator] + terms,
        flops=6 * local_rows * NUM_FEAT * val_width,
    )[0]


def solution(mesh):
    ctx, tp = mesh.shape["ctx"], mesh.shape["tp"]
    if tp % 2 or tp < 4 or ctx < 8 or ctx & (ctx - 1):
        raise ValueError("unsupported mesh")

    def body(*arrays):
        return per_device(ctx, tp, *arrays)

    return jax.shard_map(
        body,
        mesh=mesh,
        in_specs=(P(("ctx", "tp"), None), P(None, "tp"), P(None, "tp")),
        out_specs=P("ctx", "tp"),
        check_vma=False,
    )
```

```python
import functools
import math

import jax
import jax.numpy as jnp
from jax import lax
from jax.experimental import pallas as pl
from jax.experimental.pallas import tpu as pltpu
from jax.sharding import PartitionSpec as P


FEAT = 16
HALO = 8
PIECES = 8
LANES = 128
QUAD_FEATS = FEAT * (FEAT + 1) // 2
NUM_FEAT = QUAD_FEATS + FEAT + 8
HALF = (NUM_FEAT + 16) // 2
F32 = jnp.float32
BF16 = jnp.bfloat16
HBM = pl.BlockSpec(memory_space=pltpu.HBM)
VMEM = pl.BlockSpec(memory_space=pltpu.VMEM)
SMEM = pl.BlockSpec(memory_space=pltpu.SMEM)
LAST = (((1,), (1,)), ((), ()))


def call(kernel, outs, operands, scalars=0, scratch=(), flops=1 << 20, moved=1 << 20, space=VMEM):
    return pl.pallas_call(
        kernel,
        out_shape=outs,
        in_specs=[SMEM] * scalars + [space] * (len(operands) - scalars),
        out_specs=[VMEM] * len(outs),
        scratch_shapes=list(scratch),
        compiler_params=pltpu.CompilerParams(vmem_limit_bytes=16 << 20),
        cost_estimate=pl.CostEstimate(flops=flops, bytes_accessed=moved, transcendentals=0),
    )(*operands)


def hbm(array):
    return pltpu.with_memory_space_constraint(array, pltpu.HBM)


def dot_last(left, right):
    return lax.dot_general(left, right, LAST, preferred_element_type=F32)


def pack_kernel(share_ref, weight_ref, tokens_ref, sent_ref, last_ref, sems):
    width = sent_ref.shape[1]
    start = pl.multiple_of(share_ref[0] * width, LANES)
    weights = pltpu.make_async_copy(weight_ref.at[:, pl.ds(start, width)], sent_ref, sems.at[0])
    last = pltpu.make_async_copy(
        tokens_ref.at[tokens_ref.shape[0] - HALO :, :], last_ref, sems.at[1]
    )
    weights.start()
    last.start()
    weights.wait()
    last.wait()


def own_kernel(tail_ref, tokens_ref, weight_ref, halo_ref, own_ref):
    weight = weight_ref[...]
    own_ref[...] = dot_last(weight, tokens_ref[...]).astype(BF16)
    padded = jnp.concatenate(
        [jnp.zeros((halo_ref.shape[1] - HALO, tail_ref.shape[1]), BF16), tail_ref[...]], axis=0
    )
    halo_ref[...] = dot_last(weight, padded).astype(BF16)


def gathered(share, tokens_ref, pieces):
    depth = pieces[0].shape[1]
    total = None
    for index, piece in zip((0, 2, 4, 6, 1, 3, 5, 7), pieces):
        start = pl.multiple_of((share ^ index) * depth, depth)
        part = dot_last(piece[...], tokens_ref[:, pl.ds(start, depth)])
        total = part if total is None else total + part
    return total.astype(BF16)


def early_kernel(share_ref, tokens_ref, *refs):
    share = share_ref[0]
    count = len(refs) // (PIECES + 1)
    for turn in range(count):
        refs[PIECES * count + turn][...] = gathered(
            share, tokens_ref, refs[PIECES * turn : PIECES * turn + PIECES]
        )


def late_kernel(share_ref, tokens_ref, weight_ref, *refs):
    share = share_ref[0]
    count = len(refs) // (PIECES + 1)
    for turn in range(count):
        refs[PIECES * count + turn][...] = gathered(
            share, tokens_ref, refs[PIECES * turn : PIECES * turn + PIECES]
        )
    refs[-1][...] = dot_last(weight_ref[...], tokens_ref[...]).astype(BF16)


def features(raw, weighted):
    scale = 1.0 / (math.sqrt(2.0) * math.sqrt(FEAT))
    parts = []
    for shift in range(FEAT // 2 + 1):
        pair = raw * (pltpu.roll(raw, shift, 0) if shift else raw) * scale
        if shift == FEAT // 2:
            pair = pair[: FEAT // 2]
        pair = pair.astype(BF16).astype(F32)
        parts.append(pair * 2.0 if weighted and shift else pair)
    parts.append(raw * FEAT ** (-0.25))
    row = lax.broadcasted_iota(jnp.int32, (8, raw.shape[1]), 0)
    parts.append(jnp.where(row == 0, 1.0, 0.0).astype(F32))
    return jnp.concatenate(parts, axis=0).astype(BF16)


def feature_kernel(place_ref, side_ref, conv_ref, halo_ref, *refs):
    count = place_ref.shape[0]
    blocks = refs[:count]
    query_ref, key_ref, value_ref, kept_ref, sent_ref, wide, state_ref = refs[count:]
    width = halo_ref.shape[1]
    local_rows = width * count
    wide[:, :width] = halo_ref[...].astype(F32)
    for index, block in enumerate(blocks):
        start = pl.multiple_of((place_ref[index] + 1) * width, LANES)
        wide[:, pl.ds(start, width)] = block[...].astype(F32)
    padded = wide[...]
    convolved = jnp.zeros((padded.shape[0], local_rows), F32)
    taps = conv_ref[...].T
    for offset in range(taps.shape[1]):
        moved = pltpu.roll(padded, offset, 1) if offset else padded
        convolved += taps[:, offset : offset + 1] * moved[:, width:]
    value = convolved[2 * FEAT :].astype(BF16)
    value_ref[...] = value
    query = features(convolved[:FEAT], False)
    query_ref[...] = query.T
    key = features(convolved[FEAT : 2 * FEAT], True)
    key_ref[...] = key
    state_ref[:NUM_FEAT, :] = dot_last(key, value)
    total = dot_last(jnp.ones((8, local_rows), BF16), key)
    lanes = state_ref.shape[1]
    rest = NUM_FEAT - lanes
    more = jnp.concatenate([total[:, lanes:], jnp.zeros((8, lanes - rest), F32)], axis=1)
    row = lax.broadcasted_iota(jnp.int32, (8, lanes), 0)
    rows = jnp.where(row == 0, total[:, :lanes], jnp.where(row == 1, more, 0.0))
    state_ref[NUM_FEAT : NUM_FEAT + 8, :] = rows
    state_ref[NUM_FEAT + 8 :, :] = jnp.zeros((2 * HALF - NUM_FEAT - 8, lanes), F32)
    core = side_ref[0] % 2
    kept_ref[...] = state_ref[pl.ds(pl.multiple_of(core * HALF, 8), HALF), :]
    sent_ref[...] = state_ref[pl.ds(pl.multiple_of(HALF - core * HALF, 8), HALF), :]


def inner_kernel(query_ref, key_ref, value_ref, numerator_ref, denominator_ref):
    local_rows = query_ref.shape[0]
    width = value_ref.shape[0]
    step = LANES
    for start in range(0, local_rows, step):
        size = start + step
        scores = jnp.dot(query_ref[start:size, :], key_ref[:, :size], preferred_element_type=F32)
        row = lax.broadcasted_iota(jnp.int32, (step, size), 0) + start
        column = lax.broadcasted_iota(jnp.int32, (step, size), 1)
        scores = jnp.where(row >= column, scores, 0.0)
        numerator_ref[start:size, :] = dot_last(scores.astype(BF16), value_ref[:, :size])
        denominator_ref[start:size, :] = jnp.broadcast_to(
            jnp.sum(scores, axis=1, keepdims=True), (step, width)
        )


def finish_kernel(side_ref, query_ref, numerator_ref, denominator_ref, kept_ref, other_ref, out_ref, state_ref):
    core = side_ref[0] % 2
    state_ref[pl.ds(pl.multiple_of(core * HALF, 8), HALF), :] = kept_ref[...]
    state_ref[pl.ds(pl.multiple_of(HALF - core * HALF, 8), HALF), :] = other_ref[...]
    state = state_ref[...]
    width = numerator_ref.shape[1]
    query = query_ref[...]
    rest = state[:NUM_FEAT, :]
    numerator = numerator_ref[...]
    for _ in range(3):
        part = rest.astype(BF16)
        rest = rest - part.astype(F32)
        numerator += jnp.dot(query, part, preferred_element_type=F32)
    totals = jnp.concatenate(
        [state[NUM_FEAT : NUM_FEAT + 1, :], state[NUM_FEAT + 1 : NUM_FEAT + 2, : NUM_FEAT - width]], axis=1
    )
    denominator = denominator_ref[:, :1] + jnp.sum(query.astype(F32) * totals, axis=1, keepdims=True)
    out_ref[...] = (numerator / denominator).astype(BF16)


def per_device(ctx, tp, tokens, projection, conv_weight):
    both = ("ctx", "tp")
    rows, depth = tokens.shape
    row_width = projection.shape[1]
    val_width = row_width - 2 * FEAT
    local_rows = rows * tp
    turns = range(1, tp // 2)
    me = lax.axis_index("ctx")
    head = lax.axis_index("tp")
    weight = projection.T
    piece = depth // PIECES
    share = me & PIECES - 1

    def swap(array, bit):
        return lax.ppermute(array, "ctx", [(i, i ^ bit) for i in range(ctx)])

    side = share.astype(jnp.int32).reshape(1)
    mine, last_rows = call(
        pack_kernel,
        [
            jax.ShapeDtypeStruct((row_width, piece), BF16),
            jax.ShapeDtypeStruct((HALO, depth), BF16),
        ],
        [side, hbm(weight), hbm(tokens)],
        1,
        [pltpu.SemaphoreType.DMA((2,))],
        space=HBM,
    )
    pieces = []
    for turn in turns:
        first = lax.ppermute(mine, "tp", [((z + 2 * turn) % tp, z) for z in range(tp)])
        parts = [first] + [swap(first, bits) for bits in (2, 4, 6)]
        pieces += parts + [swap(part, 1) for part in parts]
    paired = lax.ppermute(tokens, "tp", [(z, z ^ 1) for z in range(tp)])

    tail = None
    for z in range(tp):
        pairs = [((c - 1) * tp + tp - 1, c * tp + z) for c in range(1, ctx)]
        part = lax.ppermute(last_rows, both, pairs)
        tail = part if tail is None else tail + part

    shape = jax.ShapeDtypeStruct((row_width, rows), BF16)
    work = 2 * rows * depth * row_width
    halo, own = call(own_kernel, [shape] * 2, [tail, tokens, weight], flops=2 * work)
    early = call(early_kernel, [shape] * len(turns), [side, tokens] + pieces, 1, flops=work)
    *late, other = call(
        late_kernel, [shape] * (len(turns) + 1), [side, paired, weight] + pieces, 1, flops=2 * work
    )
    blocks, places = [own, other], [head, head ^ 1]
    for turn, one, two in zip(turns, early, late):
        pairs = [(z, (z + 2 * turn) % tp) for z in range(tp)]
        source = (head + tp - 2 * turn) % tp
        blocks += [lax.ppermute(one, "tp", pairs), lax.ppermute(two, "tp", pairs)]
        places += [source, source ^ 1]
    place = jnp.stack(places).astype(jnp.int32)
    query, key, value, mine, theirs = call(
        feature_kernel,
        [
            jax.ShapeDtypeStruct((local_rows, NUM_FEAT), BF16),
            jax.ShapeDtypeStruct((NUM_FEAT, local_rows), BF16),
            jax.ShapeDtypeStruct((val_width, local_rows), BF16),
            jax.ShapeDtypeStruct((HALF, val_width), F32),
            jax.ShapeDtypeStruct((HALF, val_width), F32),
        ],
        [place, side, conv_weight, halo] + blocks,
        2,
        [pltpu.VMEM((row_width, rows + local_rows), F32), pltpu.VMEM((2 * HALF, val_width), F32)],
    )
    numerator, denominator = call(
        inner_kernel,
        [jax.ShapeDtypeStruct((local_rows, val_width), F32)] * 2,
        [query, key, value],
        flops=2 * local_rows * local_rows * (NUM_FEAT + val_width),
    )
    core = me % 2
    received = swap(theirs, 1)
    total = mine + received
    earlier = jnp.zeros_like(total)
    bit = 2
    while bit < ctx:
        radix = min(4, ctx // bit)
        last = bit * radix >= ctx
        digit = me // bit % radix
        parts = []
        for delta in range(1, radix):
            pairs = [(c, c ^ delta * bit) for c in range(ctx)]
            parts.append(lax.ppermute(total, "ctx", pairs))
            earlier = earlier + jnp.where(digit > digit ^ delta, parts[-1], 0.0)
        if not last:
            total = functools.reduce(jnp.add, parts, total)
        bit *= radix
    other = swap(earlier + jnp.where(core == 0, mine, 0.0), 1)
    kept = earlier + jnp.where(core == 1, received, 0.0)
    return call(
        finish_kernel,
        [jax.ShapeDtypeStruct((local_rows, val_width), BF16)],
        [side, query, numerator, denominator, kept, other],
        1,
        [pltpu.VMEM((2 * HALF, val_width), F32)],
        flops=6 * local_rows * NUM_FEAT * val_width,
    )[0]


def solution(mesh):
    ctx, tp = mesh.shape["ctx"], mesh.shape["tp"]
    if tp % 2 or tp < 4 or ctx < 8 or ctx & (ctx - 1):
        raise ValueError("unsupported mesh")

    def body(*arrays):
        return per_device(ctx, tp, *arrays)

    return jax.shard_map(
        body,
        mesh=mesh,
        in_specs=(P(("ctx", "tp"), None), P(None, "tp"), P(None, "tp")),
        out_specs=P("ctx", "tp"),
        check_vma=False,
    )
```

```python
import functools
import math

import jax
import jax.numpy as jnp
from jax import lax
from jax.experimental import pallas as pl
from jax.experimental.pallas import tpu as pltpu
from jax.sharding import PartitionSpec as P


FEAT = 16
HALO = 8
PIECES = 8
LANES = 128
QUAD_FEATS = FEAT * (FEAT + 1) // 2
NUM_FEAT = QUAD_FEATS + FEAT + 8
STATE_ROWS = NUM_FEAT + 8
F32 = jnp.float32
BF16 = jnp.bfloat16
HBM = pl.BlockSpec(memory_space=pltpu.HBM)
VMEM = pl.BlockSpec(memory_space=pltpu.VMEM)
SMEM = pl.BlockSpec(memory_space=pltpu.SMEM)
LAST = (((1,), (1,)), ((), ()))


def call(kernel, outs, operands, scalars=0, scratch=(), flops=1 << 20, moved=1 << 20, space=VMEM):
    return pl.pallas_call(
        kernel,
        out_shape=outs,
        in_specs=[SMEM] * scalars + [space] * (len(operands) - scalars),
        out_specs=[VMEM] * len(outs),
        scratch_shapes=list(scratch),
        compiler_params=pltpu.CompilerParams(vmem_limit_bytes=16 << 20),
        cost_estimate=pl.CostEstimate(flops=flops, bytes_accessed=moved, transcendentals=0),
    )(*operands)


def hbm(array):
    return pltpu.with_memory_space_constraint(array, pltpu.HBM)


def dot_last(left, right):
    return lax.dot_general(left, right, LAST, preferred_element_type=F32)


def pack_kernel(share_ref, weight_ref, tokens_ref, sent_ref, last_ref, sems):
    width = sent_ref.shape[1]
    start = pl.multiple_of(share_ref[0] * width, LANES)
    weights = pltpu.make_async_copy(weight_ref.at[:, pl.ds(start, width)], sent_ref, sems.at[0])
    last = pltpu.make_async_copy(
        tokens_ref.at[tokens_ref.shape[0] - HALO :, :], last_ref, sems.at[1]
    )
    weights.start()
    last.start()
    weights.wait()
    last.wait()


def own_kernel(tail_ref, tokens_ref, weight_ref, halo_ref, own_ref):
    weight = weight_ref[...]
    own_ref[...] = dot_last(weight, tokens_ref[...]).astype(BF16)
    padded = jnp.concatenate(
        [jnp.zeros((halo_ref.shape[1] - HALO, tail_ref.shape[1]), BF16), tail_ref[...]], axis=0
    )
    halo_ref[...] = dot_last(weight, padded).astype(BF16)


def gathered(share, tokens_ref, pieces):
    depth = pieces[0].shape[1]
    total = None
    for index, piece in zip((0, 2, 4, 6, 1, 3, 5, 7), pieces):
        start = pl.multiple_of((share ^ index) * depth, depth)
        part = dot_last(piece[...], tokens_ref[:, pl.ds(start, depth)])
        total = part if total is None else total + part
    return total.astype(BF16)


def early_kernel(share_ref, tokens_ref, *refs):
    share = share_ref[0]
    count = len(refs) // (PIECES + 1)
    for turn in range(count):
        refs[PIECES * count + turn][...] = gathered(
            share, tokens_ref, refs[PIECES * turn : PIECES * turn + PIECES]
        )


def late_kernel(share_ref, tokens_ref, weight_ref, *refs):
    share = share_ref[0]
    count = len(refs) // (PIECES + 1)
    for turn in range(count):
        refs[PIECES * count + turn][...] = gathered(
            share, tokens_ref, refs[PIECES * turn : PIECES * turn + PIECES]
        )
    refs[-1][...] = dot_last(weight_ref[...], tokens_ref[...]).astype(BF16)


def features(raw, weighted):
    scale = 1.0 / (math.sqrt(2.0) * math.sqrt(FEAT))
    parts = []
    for shift in range(FEAT // 2 + 1):
        pair = raw * (pltpu.roll(raw, shift, 0) if shift else raw) * scale
        if shift == FEAT // 2:
            pair = pair[: FEAT // 2]
        pair = pair.astype(BF16).astype(F32)
        parts.append(pair * 2.0 if weighted and shift else pair)
    parts.append(raw * FEAT ** (-0.25))
    row = lax.broadcasted_iota(jnp.int32, (8, raw.shape[1]), 0)
    parts.append(jnp.where(row == 0, 1.0, 0.0).astype(F32))
    return jnp.concatenate(parts, axis=0).astype(BF16)


def feature_kernel(place_ref, conv_ref, halo_ref, *refs):
    count = place_ref.shape[0]
    blocks = refs[:count]
    query_ref, key_ref, value_ref, state_ref, wide = refs[count:]
    width = halo_ref.shape[1]
    local_rows = width * count
    wide[:, :width] = halo_ref[...].astype(F32)
    for index, block in enumerate(blocks):
        start = pl.multiple_of((place_ref[index] + 1) * width, LANES)
        wide[:, pl.ds(start, width)] = block[...].astype(F32)
    padded = wide[...]
    convolved = jnp.zeros((padded.shape[0], local_rows), F32)
    taps = conv_ref[...].T
    for offset in range(taps.shape[1]):
        moved = pltpu.roll(padded, offset, 1) if offset else padded
        convolved += taps[:, offset : offset + 1] * moved[:, width:]
    value = convolved[2 * FEAT :].astype(BF16)
    value_ref[...] = value
    query = features(convolved[:FEAT], False)
    query_ref[...] = query.T
    key = features(convolved[FEAT : 2 * FEAT], True)
    key_ref[...] = key
    state_ref[:NUM_FEAT, :] = dot_last(key, value)
    total = dot_last(jnp.ones((8, local_rows), BF16), key)
    lanes = state_ref.shape[1]
    rest = NUM_FEAT - lanes
    more = jnp.concatenate([total[:, lanes:], jnp.zeros((8, lanes - rest), F32)], axis=1)
    row = lax.broadcasted_iota(jnp.int32, (8, lanes), 0)
    state_ref[NUM_FEAT:, :] = jnp.where(row == 0, total[:, :lanes], jnp.where(row == 1, more, 0.0))


def inner_kernel(query_ref, key_ref, value_ref, numerator_ref, denominator_ref):
    local_rows = query_ref.shape[0]
    width = value_ref.shape[0]
    step = LANES
    for start in range(0, local_rows, step):
        size = start + step
        scores = jnp.dot(query_ref[start:size, :], key_ref[:, :size], preferred_element_type=F32)
        row = lax.broadcasted_iota(jnp.int32, (step, size), 0) + start
        column = lax.broadcasted_iota(jnp.int32, (step, size), 1)
        scores = jnp.where(row >= column, scores, 0.0)
        numerator_ref[start:size, :] = dot_last(scores.astype(BF16), value_ref[:, :size])
        denominator_ref[start:size, :] = jnp.broadcast_to(
            jnp.sum(scores, axis=1, keepdims=True), (step, width)
        )


def finish_kernel(query_ref, numerator_ref, denominator_ref, *refs):
    states, out_ref = refs[:-1], refs[-1]
    state = states[0][...]
    for other in states[1:]:
        state += other[...]
    width = numerator_ref.shape[1]
    query = query_ref[...]
    rest = state[:NUM_FEAT, :]
    numerator = numerator_ref[...]
    for _ in range(3):
        part = rest.astype(BF16)
        rest = rest - part.astype(F32)
        numerator += jnp.dot(query, part, preferred_element_type=F32)
    totals = jnp.concatenate(
        [state[NUM_FEAT : NUM_FEAT + 1, :], state[NUM_FEAT + 1 : NUM_FEAT + 2, : NUM_FEAT - width]], axis=1
    )
    denominator = denominator_ref[:, :1] + jnp.sum(query.astype(F32) * totals, axis=1, keepdims=True)
    out_ref[...] = (numerator / denominator).astype(BF16)


def per_device(ctx, tp, tokens, projection, conv_weight):
    both = ("ctx", "tp")
    rows, depth = tokens.shape
    row_width = projection.shape[1]
    val_width = row_width - 2 * FEAT
    local_rows = rows * tp
    turns = range(1, tp // 2)
    me = lax.axis_index("ctx")
    head = lax.axis_index("tp")
    weight = projection.T
    piece = depth // PIECES
    share = me & PIECES - 1

    def swap(array, bit):
        return lax.ppermute(array, "ctx", [(i, i ^ bit) for i in range(ctx)])

    side = share.astype(jnp.int32).reshape(1)
    mine, last_rows = call(
        pack_kernel,
        [
            jax.ShapeDtypeStruct((row_width, piece), BF16),
            jax.ShapeDtypeStruct((HALO, depth), BF16),
        ],
        [side, hbm(weight), hbm(tokens)],
        1,
        [pltpu.SemaphoreType.DMA((2,))],
        space=HBM,
    )
    pieces = []
    for turn in turns:
        first = lax.ppermute(mine, "tp", [((z + 2 * turn) % tp, z) for z in range(tp)])
        parts = [first] + [swap(first, bits) for bits in (2, 4, 6)]
        pieces += parts + [swap(part, 1) for part in parts]
    paired = lax.ppermute(tokens, "tp", [(z, z ^ 1) for z in range(tp)])

    pairs = [((c - 1) * tp + tp - 1, c * tp + tp - 1) for c in range(1, ctx)]
    ahead = lax.ppermute(last_rows, both, pairs)
    tail = ahead
    for z in range(tp - 1):
        pairs = [(c * tp + tp - 1, c * tp + z) for c in range(1, ctx)]
        tail = tail + lax.ppermute(ahead, both, pairs)

    shape = jax.ShapeDtypeStruct((row_width, rows), BF16)
    work = 2 * rows * depth * row_width
    halo, own = call(own_kernel, [shape] * 2, [tail, tokens, weight], flops=2 * work)
    early = call(early_kernel, [shape] * len(turns), [side, tokens] + pieces, 1, flops=work)
    *late, other = call(
        late_kernel, [shape] * (len(turns) + 1), [side, paired, weight] + pieces, 1, flops=2 * work
    )
    blocks, places = [own, other], [head, head ^ 1]
    for turn, one, two in zip(turns, early, late):
        pairs = [(z, (z + 2 * turn) % tp) for z in range(tp)]
        source = (head + tp - 2 * turn) % tp
        blocks += [lax.ppermute(one, "tp", pairs), lax.ppermute(two, "tp", pairs)]
        places += [source, source ^ 1]
    place = jnp.stack(places).astype(jnp.int32)
    query, key, value, state = call(
        feature_kernel,
        [
            jax.ShapeDtypeStruct((local_rows, NUM_FEAT), BF16),
            jax.ShapeDtypeStruct((NUM_FEAT, local_rows), BF16),
            jax.ShapeDtypeStruct((val_width, local_rows), BF16),
            jax.ShapeDtypeStruct((STATE_ROWS, val_width), F32),
        ],
        [place, conv_weight, halo] + blocks,
        1,
        [pltpu.VMEM((row_width, rows + local_rows), F32)],
    )
    numerator, denominator = call(
        inner_kernel,
        [jax.ShapeDtypeStruct((local_rows, val_width), F32)] * 2,
        [query, key, value],
        flops=2 * local_rows * local_rows * (NUM_FEAT + val_width),
    )
    received = swap(state, 1)
    terms = [jnp.where(me % 2 == 1, received, 0.0)]
    total = state + received
    bit = 2
    while bit < ctx:
        radix = min(4, ctx // bit)
        last = bit * radix >= ctx
        digit = me // bit % radix
        parts = []
        for delta in range(1, radix):
            pairs = [(c, c ^ delta * bit) for c in range(ctx)]
            parts.append(lax.ppermute(total, "ctx", pairs))
            terms.append(jnp.where(digit > digit ^ delta, parts[-1], 0.0))
        if not last:
            total = functools.reduce(jnp.add, parts, total)
        bit *= radix
    return call(
        finish_kernel,
        [jax.ShapeDtypeStruct((local_rows, val_width), BF16)],
        [query, numerator, denominator] + terms,
        flops=6 * local_rows * NUM_FEAT * val_width,
    )[0]


def solution(mesh):
    ctx, tp = mesh.shape["ctx"], mesh.shape["tp"]
    if tp % 2 or tp < 4 or ctx < 8 or ctx & (ctx - 1):
        raise ValueError("unsupported mesh")

    def body(*arrays):
        return per_device(ctx, tp, *arrays)

    return jax.shard_map(
        body,
        mesh=mesh,
        in_specs=(P(("ctx", "tp"), None), P(None, "tp"), P(None, "tp")),
        out_specs=P("ctx", "tp"),
        check_vma=False,
    )
```

```python
import functools
import math

import jax
import jax.numpy as jnp
from jax import lax
from jax.experimental import pallas as pl
from jax.experimental.pallas import tpu as pltpu
from jax.sharding import PartitionSpec as P


FEAT = 16
HALO = 8
PIECES = 8
LANES = 128
QUAD_FEATS = FEAT * (FEAT + 1) // 2
NUM_FEAT = QUAD_FEATS + FEAT + 8
STATE_ROWS = NUM_FEAT + 8
F32 = jnp.float32
BF16 = jnp.bfloat16
HBM = pl.BlockSpec(memory_space=pltpu.HBM)
VMEM = pl.BlockSpec(memory_space=pltpu.VMEM)
SMEM = pl.BlockSpec(memory_space=pltpu.SMEM)
LAST = (((1,), (1,)), ((), ()))


def call(kernel, outs, operands, scalars=0, scratch=(), flops=1 << 20, moved=1 << 20, space=VMEM):
    return pl.pallas_call(
        kernel,
        out_shape=outs,
        in_specs=[SMEM] * scalars + [space] * (len(operands) - scalars),
        out_specs=[VMEM] * len(outs),
        scratch_shapes=list(scratch),
        compiler_params=pltpu.CompilerParams(vmem_limit_bytes=16 << 20),
        cost_estimate=pl.CostEstimate(flops=flops, bytes_accessed=moved, transcendentals=0),
    )(*operands)


def hbm(array):
    return pltpu.with_memory_space_constraint(array, pltpu.HBM)


def dot_last(left, right):
    return lax.dot_general(left, right, LAST, preferred_element_type=F32)


def pack_kernel(share_ref, weight_ref, tokens_ref, sent_ref, last_ref, sems):
    width = sent_ref.shape[1]
    start = pl.multiple_of(share_ref[0] * width, LANES)
    weights = pltpu.make_async_copy(weight_ref.at[:, pl.ds(start, width)], sent_ref, sems.at[0])
    last = pltpu.make_async_copy(
        tokens_ref.at[tokens_ref.shape[0] - HALO :, :], last_ref, sems.at[1]
    )
    weights.start()
    last.start()
    weights.wait()
    last.wait()


def own_kernel(tail_ref, tokens_ref, weight_ref, halo_ref, own_ref):
    weight = weight_ref[...]
    own_ref[...] = dot_last(weight, tokens_ref[...]).astype(BF16)
    padded = jnp.concatenate(
        [jnp.zeros((halo_ref.shape[1] - HALO, tail_ref.shape[1]), BF16), tail_ref[...]], axis=0
    )
    halo_ref[...] = dot_last(weight, padded).astype(BF16)


def gathered(share, tokens_ref, pieces):
    depth = pieces[0].shape[1]
    total = None
    for index, piece in zip((0, 2, 4, 6, 1, 3, 5, 7), pieces):
        start = pl.multiple_of((share ^ index) * depth, depth)
        part = dot_last(piece[...], tokens_ref[:, pl.ds(start, depth)])
        total = part if total is None else total + part
    return total.astype(BF16)


def early_kernel(share_ref, tokens_ref, *refs):
    share = share_ref[0]
    count = len(refs) // (PIECES + 1)
    for turn in range(count):
        refs[PIECES * count + turn][...] = gathered(
            share, tokens_ref, refs[PIECES * turn : PIECES * turn + PIECES]
        )


def late_kernel(share_ref, tokens_ref, weight_ref, *refs):
    share = share_ref[0]
    count = len(refs) // (PIECES + 1)
    for turn in range(count):
        refs[PIECES * count + turn][...] = gathered(
            share, tokens_ref, refs[PIECES * turn : PIECES * turn + PIECES]
        )
    refs[-1][...] = dot_last(weight_ref[...], tokens_ref[...]).astype(BF16)


def features(raw, weighted):
    scale = 1.0 / (math.sqrt(2.0) * math.sqrt(FEAT))
    parts = []
    for shift in range(FEAT // 2 + 1):
        pair = raw * (pltpu.roll(raw, shift, 0) if shift else raw) * scale
        if shift == FEAT // 2:
            pair = pair[: FEAT // 2]
        pair = pair.astype(BF16).astype(F32)
        parts.append(pair * 2.0 if weighted and shift else pair)
    parts.append(raw * FEAT ** (-0.25))
    row = lax.broadcasted_iota(jnp.int32, (8, raw.shape[1]), 0)
    parts.append(jnp.where(row == 0, 1.0, 0.0).astype(F32))
    return jnp.concatenate(parts, axis=0).astype(BF16)


def feature_kernel(place_ref, conv_ref, halo_ref, *refs):
    count = place_ref.shape[0]
    blocks = refs[:count]
    query_ref, key_ref, value_ref, state_ref, wide = refs[count:]
    width = halo_ref.shape[1]
    local_rows = width * count
    wide[:, :width] = halo_ref[...].astype(F32)
    for index, block in enumerate(blocks):
        start = pl.multiple_of((place_ref[index] + 1) * width, LANES)
        wide[:, pl.ds(start, width)] = block[...].astype(F32)
    padded = wide[...]
    convolved = jnp.zeros((padded.shape[0], local_rows), F32)
    taps = conv_ref[...].T
    for offset in range(taps.shape[1]):
        moved = pltpu.roll(padded, offset, 1) if offset else padded
        convolved += taps[:, offset : offset + 1] * moved[:, width:]
    value = convolved[2 * FEAT :].astype(BF16)
    value_ref[...] = value
    query_ref[...] = convolved[:FEAT]
    key = features(convolved[FEAT : 2 * FEAT], True)
    key_ref[...] = key
    state_ref[:NUM_FEAT, :] = dot_last(key, value)
    total = dot_last(jnp.ones((8, local_rows), BF16), key)
    lanes = state_ref.shape[1]
    rest = NUM_FEAT - lanes
    more = jnp.concatenate([total[:, lanes:], jnp.zeros((8, lanes - rest), F32)], axis=1)
    row = lax.broadcasted_iota(jnp.int32, (8, lanes), 0)
    state_ref[NUM_FEAT:, :] = jnp.where(row == 0, total[:, :lanes], jnp.where(row == 1, more, 0.0))


def inner_kernel(raw_ref, key_ref, value_ref, query_ref, numerator_ref, denominator_ref):
    query_ref[...] = features(raw_ref[...], False).T
    local_rows = query_ref.shape[0]
    width = value_ref.shape[0]
    step = LANES
    for start in range(0, local_rows, step):
        size = start + step
        scores = jnp.dot(query_ref[start:size, :], key_ref[:, :size], preferred_element_type=F32)
        row = lax.broadcasted_iota(jnp.int32, (step, size), 0) + start
        column = lax.broadcasted_iota(jnp.int32, (step, size), 1)
        scores = jnp.where(row >= column, scores, 0.0)
        numerator_ref[start:size, :] = dot_last(scores.astype(BF16), value_ref[:, :size])
        denominator_ref[start:size, :] = jnp.broadcast_to(
            jnp.sum(scores, axis=1, keepdims=True), (step, width)
        )


def finish_kernel(query_ref, numerator_ref, denominator_ref, *refs):
    states, out_ref = refs[:-1], refs[-1]
    state = states[0][...]
    for other in states[1:]:
        state += other[...]
    width = numerator_ref.shape[1]
    query = query_ref[...]
    rest = state[:NUM_FEAT, :]
    numerator = numerator_ref[...]
    for _ in range(3):
        part = rest.astype(BF16)
        rest = rest - part.astype(F32)
        numerator += jnp.dot(query, part, preferred_element_type=F32)
    totals = jnp.concatenate(
        [state[NUM_FEAT : NUM_FEAT + 1, :], state[NUM_FEAT + 1 : NUM_FEAT + 2, : NUM_FEAT - width]], axis=1
    )
    denominator = denominator_ref[:, :1] + jnp.sum(query.astype(F32) * totals, axis=1, keepdims=True)
    out_ref[...] = (numerator / denominator).astype(BF16)


def per_device(ctx, tp, tokens, projection, conv_weight):
    both = ("ctx", "tp")
    rows, depth = tokens.shape
    row_width = projection.shape[1]
    val_width = row_width - 2 * FEAT
    local_rows = rows * tp
    turns = range(1, tp // 2)
    me = lax.axis_index("ctx")
    head = lax.axis_index("tp")
    weight = projection.T
    piece = depth // PIECES
    share = me & PIECES - 1

    def swap(array, bit):
        return lax.ppermute(array, "ctx", [(i, i ^ bit) for i in range(ctx)])

    side = share.astype(jnp.int32).reshape(1)
    mine, last_rows = call(
        pack_kernel,
        [
            jax.ShapeDtypeStruct((row_width, piece), BF16),
            jax.ShapeDtypeStruct((HALO, depth), BF16),
        ],
        [side, hbm(weight), hbm(tokens)],
        1,
        [pltpu.SemaphoreType.DMA((2,))],
        space=HBM,
    )
    pieces = []
    for turn in turns:
        first = lax.ppermute(mine, "tp", [((z + 2 * turn) % tp, z) for z in range(tp)])
        parts = [first] + [swap(first, bits) for bits in (2, 4, 6)]
        pieces += parts + [swap(part, 1) for part in parts]
    paired = lax.ppermute(tokens, "tp", [(z, z ^ 1) for z in range(tp)])

    tail = None
    for z in range(tp):
        pairs = [((c - 1) * tp + tp - 1, c * tp + z) for c in range(1, ctx)]
        part = lax.ppermute(last_rows, both, pairs)
        tail = part if tail is None else tail + part

    shape = jax.ShapeDtypeStruct((row_width, rows), BF16)
    work = 2 * rows * depth * row_width
    halo, own = call(own_kernel, [shape] * 2, [tail, tokens, weight], flops=2 * work)
    early = call(early_kernel, [shape] * len(turns), [side, tokens] + pieces, 1, flops=work)
    *late, other = call(
        late_kernel, [shape] * (len(turns) + 1), [side, paired, weight] + pieces, 1, flops=2 * work
    )
    blocks, places = [own, other], [head, head ^ 1]
    for turn, one, two in zip(turns, early, late):
        pairs = [(z, (z + 2 * turn) % tp) for z in range(tp)]
        source = (head + tp - 2 * turn) % tp
        blocks += [lax.ppermute(one, "tp", pairs), lax.ppermute(two, "tp", pairs)]
        places += [source, source ^ 1]
    place = jnp.stack(places).astype(jnp.int32)
    raw, key, value, state = call(
        feature_kernel,
        [
            jax.ShapeDtypeStruct((FEAT, local_rows), F32),
            jax.ShapeDtypeStruct((NUM_FEAT, local_rows), BF16),
            jax.ShapeDtypeStruct((val_width, local_rows), BF16),
            jax.ShapeDtypeStruct((STATE_ROWS, val_width), F32),
        ],
        [place, conv_weight, halo] + blocks,
        1,
        [pltpu.VMEM((row_width, rows + local_rows), F32)],
    )
    query, numerator, denominator = call(
        inner_kernel,
        [jax.ShapeDtypeStruct((local_rows, NUM_FEAT), BF16)]
        + [jax.ShapeDtypeStruct((local_rows, val_width), F32)] * 2,
        [raw, key, value],
        flops=2 * local_rows * local_rows * (NUM_FEAT + val_width),
    )
    received = swap(state, 1)
    terms = [jnp.where(me % 2 == 1, received, 0.0)]
    total = state + received
    bit = 2
    while bit < ctx:
        radix = min(4, ctx // bit)
        last = bit * radix >= ctx
        digit = me // bit % radix
        parts = []
        for delta in range(1, radix):
            pairs = [(c, c ^ delta * bit) for c in range(ctx)]
            parts.append(lax.ppermute(total, "ctx", pairs))
            terms.append(jnp.where(digit > digit ^ delta, parts[-1], 0.0))
        if not last:
            total = functools.reduce(jnp.add, parts, total)
        bit *= radix
    return call(
        finish_kernel,
        [jax.ShapeDtypeStruct((local_rows, val_width), BF16)],
        [query, numerator, denominator] + terms,
        flops=6 * local_rows * NUM_FEAT * val_width,
    )[0]


def solution(mesh):
    ctx, tp = mesh.shape["ctx"], mesh.shape["tp"]
    if tp % 2 or tp < 4 or ctx < 8 or ctx & (ctx - 1):
        raise ValueError("unsupported mesh")

    def body(*arrays):
        return per_device(ctx, tp, *arrays)

    return jax.shard_map(
        body,
        mesh=mesh,
        in_specs=(P(("ctx", "tp"), None), P(None, "tp"), P(None, "tp")),
        out_specs=P("ctx", "tp"),
        check_vma=False,
    )
```

```python
import functools
import math

import jax
import jax.numpy as jnp
from jax import lax
from jax.experimental import pallas as pl
from jax.experimental.pallas import tpu as pltpu
from jax.sharding import PartitionSpec as P


FEAT = 16
HALO = 8
PIECES = 8
LANES = 128
QUAD_FEATS = FEAT * (FEAT + 1) // 2
NUM_FEAT = QUAD_FEATS + FEAT + 8
STATE_ROWS = NUM_FEAT + 8
F32 = jnp.float32
BF16 = jnp.bfloat16
HBM = pl.BlockSpec(memory_space=pltpu.HBM)
VMEM = pl.BlockSpec(memory_space=pltpu.VMEM)
LAST = (((1,), (1,)), ((), ()))


def call(kernel, outs, operands, scratch=(), flops=1 << 20, moved=1 << 20, space=VMEM):
    return pl.pallas_call(
        kernel,
        out_shape=outs,
        in_specs=[space] * len(operands),
        out_specs=[VMEM] * len(outs),
        scratch_shapes=list(scratch),
        compiler_params=pltpu.CompilerParams(vmem_limit_bytes=16 << 20),
        cost_estimate=pl.CostEstimate(flops=flops, bytes_accessed=moved, transcendentals=0),
    )(*operands)


def hbm(array):
    return pltpu.with_memory_space_constraint(array, pltpu.HBM)


def dot_last(left, right):
    return lax.dot_general(left, right, LAST, preferred_element_type=F32)


def own_share():
    return lax.axis_index("ctx") & PIECES - 1


def pack_kernel(weight_ref, tokens_ref, sent_ref, last_ref, sems):
    width = sent_ref.shape[1]
    start = pl.multiple_of(own_share() * width, LANES)
    weights = pltpu.make_async_copy(weight_ref.at[:, pl.ds(start, width)], sent_ref, sems.at[0])
    last = pltpu.make_async_copy(
        tokens_ref.at[tokens_ref.shape[0] - HALO :, :], last_ref, sems.at[1]
    )
    weights.start()
    last.start()
    weights.wait()
    last.wait()


def own_kernel(tail_ref, tokens_ref, paired_ref, weight_ref, halo_ref, own_ref, other_ref):
    weight = weight_ref[...]
    own_ref[...] = dot_last(weight, tokens_ref[...]).astype(BF16)
    other_ref[...] = dot_last(weight, paired_ref[...]).astype(BF16)
    padded = jnp.concatenate(
        [jnp.zeros((halo_ref.shape[1] - HALO, tail_ref.shape[1]), BF16), tail_ref[...]], axis=0
    )
    halo_ref[...] = dot_last(weight, padded).astype(BF16)


def gathered(share, tokens_ref, pieces):
    depth = pieces[0].shape[1]
    total = None
    for index, piece in zip((0, 2, 4, 6, 1, 3, 5, 7), pieces):
        start = pl.multiple_of((share ^ index) * depth, depth)
        part = dot_last(piece[...], tokens_ref[:, pl.ds(start, depth)])
        total = part if total is None else total + part
    return total.astype(BF16)


def other_heads_kernel(tokens_ref, *refs):
    share = own_share()
    count = len(refs) // (PIECES + 1)
    for turn in range(count):
        refs[PIECES * count + turn][...] = gathered(
            share, tokens_ref, refs[PIECES * turn : PIECES * turn + PIECES]
        )


def features(raw, weighted):
    scale = 1.0 / (math.sqrt(2.0) * math.sqrt(FEAT))
    parts = []
    for shift in range(FEAT // 2 + 1):
        pair = raw * (pltpu.roll(raw, shift, 0) if shift else raw) * scale
        if shift == FEAT // 2:
            pair = pair[: FEAT // 2]
        pair = pair.astype(BF16).astype(F32)
        parts.append(pair * 2.0 if weighted and shift else pair)
    parts.append(raw * FEAT ** (-0.25))
    row = lax.broadcasted_iota(jnp.int32, (8, raw.shape[1]), 0)
    parts.append(jnp.where(row == 0, 1.0, 0.0).astype(F32))
    return jnp.concatenate(parts, axis=0).astype(BF16)


def feature_kernel(conv_ref, halo_ref, *refs):
    count = len(refs) - 5
    head = lax.axis_index("tp")
    places = []
    for turn in range(count // 2):
        source = (head + count - 2 * turn) % count
        places += [source, source ^ 1]
    blocks = refs[:count]
    query_ref, key_ref, value_ref, state_ref, wide = refs[count:]
    width = halo_ref.shape[1]
    local_rows = width * count
    wide[:, :width] = halo_ref[...].astype(F32)
    for index, block in enumerate(blocks):
        start = pl.multiple_of((places[index] + 1) * width, LANES)
        wide[:, pl.ds(start, width)] = block[...].astype(F32)
    padded = wide[...]
    convolved = jnp.zeros((padded.shape[0], local_rows), F32)
    taps = conv_ref[...].T
    for offset in range(taps.shape[1]):
        moved = pltpu.roll(padded, offset, 1) if offset else padded
        convolved += taps[:, offset : offset + 1] * moved[:, width:]
    value = convolved[2 * FEAT :].astype(BF16)
    value_ref[...] = value
    query_ref[...] = convolved[:FEAT]
    key = features(convolved[FEAT : 2 * FEAT], True)
    key_ref[...] = key
    state_ref[:NUM_FEAT, :] = dot_last(key, value)
    total = dot_last(jnp.ones((8, local_rows), BF16), key)
    lanes = state_ref.shape[1]
    rest = NUM_FEAT - lanes
    more = jnp.concatenate([total[:, lanes:], jnp.zeros((8, lanes - rest), F32)], axis=1)
    row = lax.broadcasted_iota(jnp.int32, (8, lanes), 0)
    state_ref[NUM_FEAT:, :] = jnp.where(row == 0, total[:, :lanes], jnp.where(row == 1, more, 0.0))


def inner_kernel(raw_ref, key_ref, value_ref, query_ref, numerator_ref, denominator_ref):
    query_ref[...] = features(raw_ref[...], False).T
    local_rows = query_ref.shape[0]
    width = value_ref.shape[0]
    step = LANES
    for start in range(0, local_rows, step):
        size = start + step
        scores = jnp.dot(query_ref[start:size, :], key_ref[:, :size], preferred_element_type=F32)
        row = lax.broadcasted_iota(jnp.int32, (step, size), 0) + start
        column = lax.broadcasted_iota(jnp.int32, (step, size), 1)
        scores = jnp.where(row >= column, scores, 0.0)
        numerator_ref[start:size, :] = dot_last(scores.astype(BF16), value_ref[:, :size])
        denominator_ref[start:size, :] = jnp.broadcast_to(
            jnp.sum(scores, axis=1, keepdims=True), (step, width)
        )


def finish_kernel(query_ref, numerator_ref, denominator_ref, *refs):
    states, out_ref = refs[:-1], refs[-1]
    state = states[0][...]
    for other in states[1:]:
        state += other[...]
    width = numerator_ref.shape[1]
    query = query_ref[...]
    rest = state[:NUM_FEAT, :]
    parts = []
    for _ in range(3):
        parts.append(rest.astype(BF16))
        rest = rest - parts[-1].astype(F32)
    product = jnp.dot(query, jnp.concatenate(parts, axis=1), preferred_element_type=F32)
    numerator = numerator_ref[...]
    for start in range(0, 3 * width, width):
        numerator += product[:, start : start + width]
    totals = jnp.concatenate(
        [state[NUM_FEAT : NUM_FEAT + 1, :], state[NUM_FEAT + 1 : NUM_FEAT + 2, : NUM_FEAT - width]], axis=1
    )
    denominator = denominator_ref[:, :1] + jnp.sum(query.astype(F32) * totals, axis=1, keepdims=True)
    out_ref[...] = (numerator / denominator).astype(BF16)


def per_device(ctx, tp, tokens, projection, conv_weight):
    both = ("ctx", "tp")
    rows, depth = tokens.shape
    row_width = projection.shape[1]
    val_width = row_width - 2 * FEAT
    local_rows = rows * tp
    turns = range(1, tp // 2)
    me = lax.axis_index("ctx")
    weight = projection.T
    piece = depth // PIECES

    def swap(array, bit):
        return lax.ppermute(array, "ctx", [(i, i ^ bit) for i in range(ctx)])

    mine, last_rows = call(
        pack_kernel,
        [
            jax.ShapeDtypeStruct((row_width, piece), BF16),
            jax.ShapeDtypeStruct((HALO, depth), BF16),
        ],
        [hbm(weight), hbm(tokens)],
        [pltpu.SemaphoreType.DMA((2,))],
        space=HBM,
    )
    pieces = []
    for turn in turns:
        first = lax.ppermute(mine, "tp", [((z + 2 * turn) % tp, z) for z in range(tp)])
        parts = [first] + [swap(first, bits) for bits in (2, 4, 6)]
        pieces += parts + [swap(part, 1) for part in parts]
    paired = lax.ppermute(tokens, "tp", [(z, z ^ 1) for z in range(tp)])

    pairs = [((c - 1) * tp + tp - 1, c * tp + tp - 1) for c in range(1, ctx)]
    ahead = lax.ppermute(last_rows, both, pairs)
    tail = ahead
    for z in range(tp - 1):
        pairs = [(c * tp + tp - 1, c * tp + z) for c in range(1, ctx)]
        tail = tail + lax.ppermute(ahead, both, pairs)

    shape = jax.ShapeDtypeStruct((row_width, rows), BF16)
    work = 2 * rows * depth * row_width
    halo, own, other = call(own_kernel, [shape] * 3, [tail, tokens, paired, weight], flops=3 * work)
    early = call(other_heads_kernel, [shape] * len(turns), [tokens] + pieces, flops=work)
    late = call(other_heads_kernel, [shape] * len(turns), [paired] + pieces, flops=work)
    blocks = [own, other]
    for turn, one, two in zip(turns, early, late):
        pairs = [(z, (z + 2 * turn) % tp) for z in range(tp)]
        blocks += [lax.ppermute(one, "tp", pairs), lax.ppermute(two, "tp", pairs)]
    raw, key, value, state = call(
        feature_kernel,
        [
            jax.ShapeDtypeStruct((FEAT, local_rows), F32),
            jax.ShapeDtypeStruct((NUM_FEAT, local_rows), BF16),
            jax.ShapeDtypeStruct((val_width, local_rows), BF16),
            jax.ShapeDtypeStruct((STATE_ROWS, val_width), F32),
        ],
        [conv_weight, halo] + blocks,
        [pltpu.VMEM((row_width, rows + local_rows), F32)],
    )
    query, numerator, denominator = call(
        inner_kernel,
        [jax.ShapeDtypeStruct((local_rows, NUM_FEAT), BF16)]
        + [jax.ShapeDtypeStruct((local_rows, val_width), F32)] * 2,
        [raw, key, value],
        flops=2 * local_rows * local_rows * (NUM_FEAT + val_width),
    )
    received = swap(state, 1)
    terms = [jnp.where(me % 2 == 1, received, 0.0)]
    total = state + received
    bit = 2
    while bit < ctx:
        radix = min(4, ctx // bit)
        last = bit * radix >= ctx
        digit = me // bit % radix
        parts = []
        for delta in range(1, radix):
            pairs = [(c, c ^ delta * bit) for c in range(ctx)]
            parts.append(lax.ppermute(total, "ctx", pairs))
            terms.append(jnp.where(digit > digit ^ delta, parts[-1], 0.0))
        if not last:
            total = functools.reduce(jnp.add, parts, total)
        bit *= radix
    return call(
        finish_kernel,
        [jax.ShapeDtypeStruct((local_rows, val_width), BF16)],
        [query, numerator, denominator] + terms,
        flops=6 * local_rows * NUM_FEAT * val_width,
    )[0]


def solution(mesh):
    ctx, tp = mesh.shape["ctx"], mesh.shape["tp"]
    if tp % 2 or tp < 4 or ctx < 8 or ctx & (ctx - 1):
        raise ValueError("unsupported mesh")

    def body(*arrays):
        return per_device(ctx, tp, *arrays)

    return jax.shard_map(
        body,
        mesh=mesh,
        in_specs=(P(("ctx", "tp"), None), P(None, "tp"), P(None, "tp")),
        out_specs=P("ctx", "tp"),
        check_vma=False,
    )
```

```python
import functools
import math

import jax
import jax.numpy as jnp
from jax import lax
from jax.experimental import pallas as pl
from jax.experimental.pallas import tpu as pltpu
from jax.sharding import PartitionSpec as P


FEAT = 16
HALO = 8
PIECES = 8
LANES = 128
QUAD_FEATS = FEAT * (FEAT + 1) // 2
NUM_FEAT = QUAD_FEATS + FEAT + 8
HALF = NUM_FEAT // 2
F32 = jnp.float32
BF16 = jnp.bfloat16
HBM = pl.BlockSpec(memory_space=pltpu.HBM)
VMEM = pl.BlockSpec(memory_space=pltpu.VMEM)
LAST = (((1,), (1,)), ((), ()))


def call(kernel, outs, operands, scratch=(), flops=1 << 20, moved=1 << 20, space=VMEM):
    return pl.pallas_call(
        kernel,
        out_shape=outs,
        in_specs=[space] * len(operands),
        out_specs=[VMEM] * len(outs),
        scratch_shapes=list(scratch),
        compiler_params=pltpu.CompilerParams(vmem_limit_bytes=16 << 20),
        cost_estimate=pl.CostEstimate(flops=flops, bytes_accessed=moved, transcendentals=0),
    )(*operands)


def hbm(array):
    return pltpu.with_memory_space_constraint(array, pltpu.HBM)


def dot_last(left, right):
    return lax.dot_general(left, right, LAST, preferred_element_type=F32)


def own_share():
    return lax.axis_index("ctx") & PIECES - 1


def pack_kernel(weight_ref, tokens_ref, sent_ref, last_ref, sems):
    width = sent_ref.shape[1]
    start = pl.multiple_of(own_share() * width, LANES)
    weights = pltpu.make_async_copy(weight_ref.at[:, pl.ds(start, width)], sent_ref, sems.at[0])
    last = pltpu.make_async_copy(
        tokens_ref.at[tokens_ref.shape[0] - HALO :, :], last_ref, sems.at[1]
    )
    weights.start()
    last.start()
    weights.wait()
    last.wait()


def own_kernel(tail_ref, tokens_ref, paired_ref, weight_ref, halo_ref, own_ref, other_ref):
    weight = weight_ref[...]
    own_ref[...] = dot_last(weight, tokens_ref[...]).astype(BF16)
    other_ref[...] = dot_last(weight, paired_ref[...]).astype(BF16)
    padded = jnp.concatenate(
        [jnp.zeros((halo_ref.shape[1] - HALO, tail_ref.shape[1]), BF16), tail_ref[...]], axis=0
    )
    halo_ref[...] = dot_last(weight, padded).astype(BF16)


def gathered(share, tokens_ref, pieces):
    depth = pieces[0].shape[1]
    total = None
    for index, piece in zip((0, 2, 4, 6, 1, 3, 5, 7), pieces):
        start = pl.multiple_of((share ^ index) * depth, depth)
        part = dot_last(piece[...], tokens_ref[:, pl.ds(start, depth)])
        total = part if total is None else total + part
    return total.astype(BF16)


def other_heads_kernel(tokens_ref, *refs):
    share = own_share()
    count = len(refs) // (PIECES + 1)
    for turn in range(count):
        refs[PIECES * count + turn][...] = gathered(
            share, tokens_ref, refs[PIECES * turn : PIECES * turn + PIECES]
        )


def features(raw, weighted):
    scale = 1.0 / (math.sqrt(2.0) * math.sqrt(FEAT))
    parts = []
    for shift in range(FEAT // 2 + 1):
        pair = raw * (pltpu.roll(raw, shift, 0) if shift else raw) * scale
        if shift == FEAT // 2:
            pair = pair[: FEAT // 2]
        pair = pair.astype(BF16).astype(F32)
        parts.append(pair * 2.0 if weighted and shift else pair)
    parts.append(raw * FEAT ** (-0.25))
    row = lax.broadcasted_iota(jnp.int32, (8, raw.shape[1]), 0)
    parts.append(jnp.where(row == 0, 1.0, 0.0).astype(F32))
    return jnp.concatenate(parts, axis=0).astype(BF16)


def feature_kernel(conv_ref, halo_ref, *refs):
    count = len(refs) - 7
    head = lax.axis_index("tp")
    places = []
    for turn in range(count // 2):
        source = (head + count - 2 * turn) % count
        places += [source, source ^ 1]
    blocks = refs[:count]
    query_ref, key_ref, value_ref, kept_ref, sent_ref, wide, state_ref = refs[count:]
    width = halo_ref.shape[1]
    local_rows = width * count
    wide[:, :width] = halo_ref[...].astype(F32)
    for index, block in enumerate(blocks):
        start = pl.multiple_of((places[index] + 1) * width, LANES)
        wide[:, pl.ds(start, width)] = block[...].astype(F32)
    padded = wide[...]
    convolved = jnp.zeros((padded.shape[0], local_rows), F32)
    taps = conv_ref[...].T
    for offset in range(taps.shape[1]):
        moved = pltpu.roll(padded, offset, 1) if offset else padded
        convolved += taps[:, offset : offset + 1] * moved[:, width:]
    value = convolved[2 * FEAT :].astype(BF16)
    value_ref[...] = value
    query_ref[...] = convolved[:FEAT]
    key = features(convolved[FEAT : 2 * FEAT], True)
    key_ref[...] = key
    state_ref[...] = dot_last(key, value)
    total = dot_last(jnp.ones((8, local_rows), BF16), key)
    lanes = state_ref.shape[1]
    rest = NUM_FEAT - lanes
    more = jnp.concatenate([total[:, lanes:], jnp.zeros((8, lanes - rest), F32)], axis=1)
    row = lax.broadcasted_iota(jnp.int32, (8, lanes), 0)
    tail = state_ref[NUM_FEAT - 8 :, :]
    state_ref[NUM_FEAT - 8 :, :] = jnp.where(row == 1, total[:, :lanes], jnp.where(row == 2, more, tail))
    core = lax.axis_index("ctx") & 1
    kept_ref[...] = state_ref[pl.ds(pl.multiple_of(core * HALF, 8), HALF), :]
    sent_ref[...] = state_ref[pl.ds(pl.multiple_of(HALF - core * HALF, 8), HALF), :]


def inner_kernel(raw_ref, key_ref, value_ref, query_ref, numerator_ref, denominator_ref):
    query_ref[...] = features(raw_ref[...], False).T
    local_rows = query_ref.shape[0]
    width = value_ref.shape[0]
    step = LANES
    for start in range(0, local_rows, step):
        size = start + step
        scores = jnp.dot(query_ref[start:size, :], key_ref[:, :size], preferred_element_type=F32)
        row = lax.broadcasted_iota(jnp.int32, (step, size), 0) + start
        column = lax.broadcasted_iota(jnp.int32, (step, size), 1)
        scores = jnp.where(row >= column, scores, 0.0)
        numerator_ref[start:size, :] = dot_last(scores.astype(BF16), value_ref[:, :size])
        denominator_ref[start:size, :] = jnp.broadcast_to(
            jnp.sum(scores, axis=1, keepdims=True), (step, width)
        )


def finish_kernel(query_ref, numerator_ref, denominator_ref, kept_ref, other_ref, out_ref, state_ref):
    core = lax.axis_index("ctx") & 1
    state_ref[pl.ds(pl.multiple_of(core * HALF, 8), HALF), :] = kept_ref[...]
    state_ref[pl.ds(pl.multiple_of(HALF - core * HALF, 8), HALF), :] = other_ref[...]
    state = state_ref[...]
    width = numerator_ref.shape[1]
    query = query_ref[...]
    rest = state
    parts = []
    for _ in range(3):
        parts.append(rest.astype(BF16))
        rest = rest - parts[-1].astype(F32)
    product = jnp.dot(query, jnp.concatenate(parts, axis=1), preferred_element_type=F32)
    numerator = numerator_ref[...]
    for start in range(0, 3 * width, width):
        numerator += product[:, start : start + width]
    totals = jnp.concatenate(
        [state[NUM_FEAT - 7 : NUM_FEAT - 6, :], state[NUM_FEAT - 6 : NUM_FEAT - 5, : NUM_FEAT - width]], axis=1
    )
    denominator = denominator_ref[:, :1] + jnp.sum(query.astype(F32) * totals, axis=1, keepdims=True)
    out_ref[...] = (numerator / denominator).astype(BF16)


def per_device(ctx, tp, tokens, projection, conv_weight):
    both = ("ctx", "tp")
    rows, depth = tokens.shape
    row_width = projection.shape[1]
    val_width = row_width - 2 * FEAT
    local_rows = rows * tp
    turns = range(1, tp // 2)
    me = lax.axis_index("ctx")
    weight = projection.T
    piece = depth // PIECES

    def swap(array, bit):
        return lax.ppermute(array, "ctx", [(i, i ^ bit) for i in range(ctx)])

    mine, last_rows = call(
        pack_kernel,
        [
            jax.ShapeDtypeStruct((row_width, piece), BF16),
            jax.ShapeDtypeStruct((HALO, depth), BF16),
        ],
        [hbm(weight), hbm(tokens)],
        [pltpu.SemaphoreType.DMA((2,))],
        space=HBM,
    )
    pieces = []
    for turn in turns:
        first = lax.ppermute(mine, "tp", [((z + 2 * turn) % tp, z) for z in range(tp)])
        parts = [first] + [swap(first, bits) for bits in (2, 4, 6)]
        pieces += parts + [swap(part, 1) for part in parts]
    paired = lax.ppermute(tokens, "tp", [(z, z ^ 1) for z in range(tp)])

    tail = None
    for z in range(tp):
        pairs = [((c - 1) * tp + tp - 1, c * tp + z) for c in range(1, ctx)]
        part = lax.ppermute(last_rows, both, pairs)
        tail = part if tail is None else tail + part

    shape = jax.ShapeDtypeStruct((row_width, rows), BF16)
    work = 2 * rows * depth * row_width
    halo, own, other = call(own_kernel, [shape] * 3, [tail, tokens, paired, weight], flops=3 * work)
    early = call(other_heads_kernel, [shape] * len(turns), [tokens] + pieces, flops=work)
    late = call(other_heads_kernel, [shape] * len(turns), [paired] + pieces, flops=work)
    blocks = [own, other]
    for turn, one, two in zip(turns, early, late):
        pairs = [(z, (z + 2 * turn) % tp) for z in range(tp)]
        blocks += [lax.ppermute(one, "tp", pairs), lax.ppermute(two, "tp", pairs)]
    raw, key, value, mine, theirs = call(
        feature_kernel,
        [
            jax.ShapeDtypeStruct((FEAT, local_rows), F32),
            jax.ShapeDtypeStruct((NUM_FEAT, local_rows), BF16),
            jax.ShapeDtypeStruct((val_width, local_rows), BF16),
            jax.ShapeDtypeStruct((HALF, val_width), F32),
            jax.ShapeDtypeStruct((HALF, val_width), F32),
        ],
        [conv_weight, halo] + blocks,
        [pltpu.VMEM((row_width, rows + local_rows), F32), pltpu.VMEM((NUM_FEAT, val_width), F32)],
    )
    query, numerator, denominator = call(
        inner_kernel,
        [jax.ShapeDtypeStruct((local_rows, NUM_FEAT), BF16)]
        + [jax.ShapeDtypeStruct((local_rows, val_width), F32)] * 2,
        [raw, key, value],
        flops=2 * local_rows * local_rows * (NUM_FEAT + val_width),
    )
    received = swap(theirs, 1)
    total = mine + received
    earlier = jnp.zeros_like(total)
    bit = 2
    while bit < ctx:
        radix = min(4, ctx // bit)
        last = bit * radix >= ctx
        digit = me // bit % radix
        parts = []
        for delta in range(1, radix):
            pairs = [(c, c ^ delta * bit) for c in range(ctx)]
            parts.append(lax.ppermute(total, "ctx", pairs))
            earlier = earlier + jnp.where(digit > digit ^ delta, parts[-1], 0.0)
        if not last:
            total = functools.reduce(jnp.add, parts, total)
        bit *= radix
    first = me % 2 == 0
    other = swap(earlier + jnp.where(first, mine, 0.0), 1)
    kept = earlier + jnp.where(first, 0.0, received)
    return call(
        finish_kernel,
        [jax.ShapeDtypeStruct((local_rows, val_width), BF16)],
        [query, numerator, denominator, kept, other],
        [pltpu.VMEM((NUM_FEAT, val_width), F32)],
        flops=6 * local_rows * NUM_FEAT * val_width,
    )[0]


def solution(mesh):
    ctx, tp = mesh.shape["ctx"], mesh.shape["tp"]
    if tp % 2 or tp < 4 or ctx < 8 or ctx & (ctx - 1):
        raise ValueError("unsupported mesh")

    def body(*arrays):
        return per_device(ctx, tp, *arrays)

    return jax.shard_map(
        body,
        mesh=mesh,
        in_specs=(P(("ctx", "tp"), None), P(None, "tp"), P(None, "tp")),
        out_specs=P("ctx", "tp"),
        check_vma=False,
    )
```

```python
import functools
import math

import jax
import jax.numpy as jnp
from jax import lax
from jax.experimental import pallas as pl
from jax.experimental.pallas import tpu as pltpu
from jax.sharding import PartitionSpec as P


FEAT = 16
HALO = 8
PIECES = 8
LANES = 128
QUAD_FEATS = FEAT * (FEAT + 1) // 2
NUM_FEAT = QUAD_FEATS + FEAT + 8
STATE_ROWS = NUM_FEAT + 8
F32 = jnp.float32
BF16 = jnp.bfloat16
HBM = pl.BlockSpec(memory_space=pltpu.HBM)
VMEM = pl.BlockSpec(memory_space=pltpu.VMEM)
LAST = (((1,), (1,)), ((), ()))


def call(kernel, outs, operands, scratch=(), flops=1 << 20, moved=1 << 20, space=VMEM):
    return pl.pallas_call(
        kernel,
        out_shape=outs,
        in_specs=[space] * len(operands),
        out_specs=[VMEM] * len(outs),
        scratch_shapes=list(scratch),
        compiler_params=pltpu.CompilerParams(vmem_limit_bytes=16 << 20),
        cost_estimate=pl.CostEstimate(flops=flops, bytes_accessed=moved, transcendentals=0),
    )(*operands)


def hbm(array):
    return pltpu.with_memory_space_constraint(array, pltpu.HBM)


def dot_last(left, right):
    return lax.dot_general(left, right, LAST, preferred_element_type=F32)


def own_share():
    return lax.axis_index("ctx") & PIECES - 1


def pack_kernel(weight_ref, tokens_ref, sent_ref, last_ref, sems):
    width = sent_ref.shape[1]
    start = pl.multiple_of(own_share() * width, LANES)
    weights = pltpu.make_async_copy(weight_ref.at[:, pl.ds(start, width)], sent_ref, sems.at[0])
    last = pltpu.make_async_copy(
        tokens_ref.at[tokens_ref.shape[0] - HALO :, :], last_ref, sems.at[1]
    )
    weights.start()
    last.start()
    weights.wait()
    last.wait()


def own_kernel(tail_ref, tokens_ref, paired_ref, weight_ref, halo_ref, own_ref, other_ref):
    weight = weight_ref[...]
    own_ref[...] = dot_last(weight, tokens_ref[...]).astype(BF16)
    other_ref[...] = dot_last(weight, paired_ref[...]).astype(BF16)
    padded = jnp.concatenate(
        [jnp.zeros((halo_ref.shape[1] - HALO, tail_ref.shape[1]), BF16), tail_ref[...]], axis=0
    )
    halo_ref[...] = dot_last(weight, padded).astype(BF16)


def gathered(share, tokens_ref, pieces):
    depth = pieces[0].shape[1]
    total = None
    for index, piece in zip((0, 2, 4, 6, 1, 3, 5, 7), pieces):
        start = pl.multiple_of((share ^ index) * depth, depth)
        part = dot_last(piece[...], tokens_ref[:, pl.ds(start, depth)])
        total = part if total is None else total + part
    return total.astype(BF16)


def other_heads_kernel(tokens_ref, *refs):
    share = own_share()
    count = len(refs) // (PIECES + 1)
    for turn in range(count):
        refs[PIECES * count + turn][...] = gathered(
            share, tokens_ref, refs[PIECES * turn : PIECES * turn + PIECES]
        )


def features(raw, weighted):
    scale = 1.0 / (math.sqrt(2.0) * math.sqrt(FEAT))
    parts = []
    for shift in range(FEAT // 2 + 1):
        pair = raw * (pltpu.roll(raw, shift, 0) if shift else raw) * scale
        if shift == FEAT // 2:
            pair = pair[: FEAT // 2]
        pair = pair.astype(BF16).astype(F32)
        parts.append(pair * 2.0 if weighted and shift else pair)
    parts.append(raw * FEAT ** (-0.25))
    row = lax.broadcasted_iota(jnp.int32, (8, raw.shape[1]), 0)
    parts.append(jnp.where(row == 0, 1.0, 0.0).astype(F32))
    return jnp.concatenate(parts, axis=0).astype(BF16)


def feature_kernel(conv_ref, halo_ref, *refs):
    count = len(refs) - 5
    head = lax.axis_index("tp")
    places = []
    for turn in range(count // 2):
        source = (head + count - 2 * turn) % count
        places += [source, source ^ 1]
    blocks = refs[:count]
    query_ref, key_ref, value_ref, state_ref, wide = refs[count:]
    width = halo_ref.shape[1]
    local_rows = width * count
    wide[:, :width] = halo_ref[...].astype(F32)
    for index, block in enumerate(blocks):
        start = pl.multiple_of((places[index] + 1) * width, LANES)
        wide[:, pl.ds(start, width)] = block[...].astype(F32)
    padded = wide[...]
    convolved = jnp.zeros((padded.shape[0], local_rows), F32)
    taps = conv_ref[...].T
    for offset in range(taps.shape[1]):
        moved = pltpu.roll(padded, offset, 1) if offset else padded
        convolved += taps[:, offset : offset + 1] * moved[:, width:]
    value = convolved[2 * FEAT :].astype(BF16)
    value_ref[...] = value
    query_ref[...] = convolved[:FEAT]
    key = features(convolved[FEAT : 2 * FEAT], True)
    key_ref[...] = key
    state_ref[:NUM_FEAT, :] = dot_last(key, value)
    total = dot_last(jnp.ones((8, local_rows), BF16), key)
    lanes = state_ref.shape[1]
    rest = NUM_FEAT - lanes
    more = jnp.concatenate([total[:, lanes:], jnp.zeros((8, lanes - rest), F32)], axis=1)
    row = lax.broadcasted_iota(jnp.int32, (8, lanes), 0)
    state_ref[NUM_FEAT:, :] = jnp.where(row == 0, total[:, :lanes], jnp.where(row == 1, more, 0.0))


def inner_kernel(raw_ref, key_ref, value_ref, query_ref, numerator_ref, denominator_ref):
    query_ref[...] = features(raw_ref[...], False).T
    local_rows = query_ref.shape[0]
    width = value_ref.shape[0]
    step = LANES
    for start in range(0, local_rows, step):
        size = start + step
        scores = jnp.dot(query_ref[start:size, :], key_ref[:, :size], preferred_element_type=F32)
        row = lax.broadcasted_iota(jnp.int32, (step, size), 0) + start
        column = lax.broadcasted_iota(jnp.int32, (step, size), 1)
        scores = jnp.where(row >= column, scores, 0.0)
        numerator_ref[start:size, :] = dot_last(scores.astype(BF16), value_ref[:, :size])
        denominator_ref[start:size, :] = jnp.broadcast_to(
            jnp.sum(scores, axis=1, keepdims=True), (step, width)
        )


def finish_kernel(query_ref, numerator_ref, denominator_ref, *refs):
    states, out_ref = refs[:-1], refs[-1]
    state = states[0][...]
    for other in states[1:]:
        state += other[...]
    width = numerator_ref.shape[1]
    query = query_ref[...]
    rest = state[:NUM_FEAT, :]
    parts = []
    for _ in range(3):
        parts.append(rest.astype(BF16))
        rest = rest - parts[-1].astype(F32)
    product = jnp.dot(query, jnp.concatenate(parts, axis=1), preferred_element_type=F32)
    numerator = numerator_ref[...]
    for start in range(0, 3 * width, width):
        numerator += product[:, start : start + width]
    totals = jnp.concatenate(
        [state[NUM_FEAT : NUM_FEAT + 1, :], state[NUM_FEAT + 1 : NUM_FEAT + 2, : NUM_FEAT - width]], axis=1
    )
    denominator = denominator_ref[:, :1] + jnp.sum(query.astype(F32) * totals, axis=1, keepdims=True)
    out_ref[...] = (numerator / denominator).astype(BF16)


def per_device(ctx, tp, tokens, projection, conv_weight):
    both = ("ctx", "tp")
    rows, depth = tokens.shape
    row_width = projection.shape[1]
    val_width = row_width - 2 * FEAT
    local_rows = rows * tp
    turns = range(1, tp // 2)
    me = lax.axis_index("ctx")
    weight = projection.T
    piece = depth // PIECES

    def swap(array, bit):
        return lax.ppermute(array, "ctx", [(i, i ^ bit) for i in range(ctx)])

    mine, last_rows = call(
        pack_kernel,
        [
            jax.ShapeDtypeStruct((row_width, piece), BF16),
            jax.ShapeDtypeStruct((HALO, depth), BF16),
        ],
        [hbm(weight), hbm(tokens)],
        [pltpu.SemaphoreType.DMA((2,))],
        space=HBM,
    )
    pieces = []
    for turn in turns:
        first = lax.ppermute(mine, "tp", [((z + 2 * turn) % tp, z) for z in range(tp)])
        parts = [first] + [swap(first, bits) for bits in (2, 4, 6)]
        pieces += parts + [swap(part, 1) for part in parts]
    paired = lax.ppermute(tokens, "tp", [(z, z ^ 1) for z in range(tp)])

    tail = None
    for z in range(tp):
        pairs = [((c - 1) * tp + tp - 1, c * tp + z) for c in range(1, ctx)]
        part = lax.ppermute(last_rows, both, pairs)
        tail = part if tail is None else tail + part

    shape = jax.ShapeDtypeStruct((row_width, rows), BF16)
    work = 2 * rows * depth * row_width
    halo, own, other = call(own_kernel, [shape] * 3, [tail, tokens, paired, weight], flops=3 * work)
    early = call(other_heads_kernel, [shape] * len(turns), [tokens] + pieces, flops=work)
    late = call(other_heads_kernel, [shape] * len(turns), [paired] + pieces, flops=work)
    blocks = [own, other]
    for turn, one, two in zip(turns, early, late):
        pairs = [(z, (z + 2 * turn) % tp) for z in range(tp)]
        blocks += [lax.ppermute(one, "tp", pairs), lax.ppermute(two, "tp", pairs)]
    raw, key, value, state = call(
        feature_kernel,
        [
            jax.ShapeDtypeStruct((FEAT, local_rows), F32),
            jax.ShapeDtypeStruct((NUM_FEAT, local_rows), BF16),
            jax.ShapeDtypeStruct((val_width, local_rows), BF16),
            jax.ShapeDtypeStruct((STATE_ROWS, val_width), F32),
        ],
        [conv_weight, halo] + blocks,
        [pltpu.VMEM((row_width, rows + local_rows), F32)],
    )
    query, numerator, denominator = call(
        inner_kernel,
        [jax.ShapeDtypeStruct((local_rows, NUM_FEAT), BF16)]
        + [jax.ShapeDtypeStruct((local_rows, val_width), F32)] * 2,
        [raw, key, value],
        flops=2 * local_rows * local_rows * (NUM_FEAT + val_width),
    )
    received = swap(state, 1)
    terms = [jnp.where(me % 2 == 1, received, 0.0)]
    total = state + received
    bit = 2
    while bit < ctx:
        radix = min(4, ctx // bit)
        last = bit * radix >= ctx
        digit = me // bit % radix
        parts = []
        for delta in range(1, radix):
            pairs = [(c, c ^ delta * bit) for c in range(ctx)]
            parts.append(lax.ppermute(total, "ctx", pairs))
            terms.append(jnp.where(digit > digit ^ delta, parts[-1], 0.0))
        if not last:
            total = functools.reduce(jnp.add, parts, total)
        bit *= radix
    return call(
        finish_kernel,
        [jax.ShapeDtypeStruct((local_rows, val_width), BF16)],
        [query, numerator, denominator] + terms,
        flops=6 * local_rows * NUM_FEAT * val_width,
    )[0]


def solution(mesh):
    ctx, tp = mesh.shape["ctx"], mesh.shape["tp"]
    if tp % 2 or tp < 4 or ctx < 8 or ctx & (ctx - 1):
        raise ValueError("unsupported mesh")

    def body(*arrays):
        return per_device(ctx, tp, *arrays)

    return jax.shard_map(
        body,
        mesh=mesh,
        in_specs=(P(("ctx", "tp"), None), P(None, "tp"), P(None, "tp")),
        out_specs=P("ctx", "tp"),
        check_vma=False,
    )
```

```python
import functools
import math

import jax
import jax.numpy as jnp
from jax import lax
from jax.experimental import pallas as pl
from jax.experimental.pallas import tpu as pltpu
from jax.sharding import PartitionSpec as P


FEAT = 16
HALO = 8
PIECES = 8
LANES = 128
QUAD_FEATS = FEAT * (FEAT + 1) // 2
NUM_FEAT = QUAD_FEATS + FEAT + 8
STATE_ROWS = NUM_FEAT + 8
F32 = jnp.float32
BF16 = jnp.bfloat16
HBM = pl.BlockSpec(memory_space=pltpu.HBM)
VMEM = pl.BlockSpec(memory_space=pltpu.VMEM)
LAST = (((1,), (1,)), ((), ()))


def call(kernel, outs, operands, scratch=(), flops=1 << 20, moved=1 << 20, space=VMEM):
    return pl.pallas_call(
        kernel,
        out_shape=outs,
        in_specs=[space] * len(operands),
        out_specs=[VMEM] * len(outs),
        scratch_shapes=list(scratch),
        compiler_params=pltpu.CompilerParams(vmem_limit_bytes=16 << 20),
        cost_estimate=pl.CostEstimate(flops=flops, bytes_accessed=moved, transcendentals=0),
    )(*operands)


def hbm(array):
    return pltpu.with_memory_space_constraint(array, pltpu.HBM)


def dot_last(left, right):
    return lax.dot_general(left, right, LAST, preferred_element_type=F32)


def own_share():
    return lax.axis_index("ctx") & PIECES - 1


def pack_kernel(weight_ref, tokens_ref, sent_ref, last_ref, sems):
    width = sent_ref.shape[1]
    start = pl.multiple_of(own_share() * width, LANES)
    weights = pltpu.make_async_copy(weight_ref.at[:, pl.ds(start, width)], sent_ref, sems.at[0])
    last = pltpu.make_async_copy(
        tokens_ref.at[tokens_ref.shape[0] - HALO :, :], last_ref, sems.at[1]
    )
    weights.start()
    last.start()
    weights.wait()
    last.wait()


def own_kernel(tail_ref, tokens_ref, weight_ref, halo_ref, own_ref):
    weight = weight_ref[...]
    own_ref[...] = dot_last(weight, tokens_ref[...]).astype(BF16)
    padded = jnp.concatenate(
        [jnp.zeros((halo_ref.shape[1] - HALO, tail_ref.shape[1]), BF16), tail_ref[...]], axis=0
    )
    halo_ref[...] = dot_last(weight, padded).astype(BF16)


def gathered(share, tokens_ref, pieces):
    depth = pieces[0].shape[1]
    total = None
    for index, piece in zip((0, 2, 4, 6, 1, 3, 5, 7), pieces):
        start = pl.multiple_of((share ^ index) * depth, depth)
        part = dot_last(piece[...], tokens_ref[:, pl.ds(start, depth)])
        total = part if total is None else total + part
    return total.astype(BF16)


def early_kernel(tokens_ref, *refs):
    share = own_share()
    count = len(refs) // (PIECES + 1)
    for turn in range(count):
        refs[PIECES * count + turn][...] = gathered(
            share, tokens_ref, refs[PIECES * turn : PIECES * turn + PIECES]
        )


def late_kernel(tokens_ref, weight_ref, *refs):
    share = own_share()
    count = len(refs) // (PIECES + 1)
    for turn in range(count):
        refs[PIECES * count + turn][...] = gathered(
            share, tokens_ref, refs[PIECES * turn : PIECES * turn + PIECES]
        )
    refs[-1][...] = dot_last(weight_ref[...], tokens_ref[...]).astype(BF16)


def features(raw, weighted):
    scale = 1.0 / (math.sqrt(2.0) * math.sqrt(FEAT))
    parts = []
    for shift in range(FEAT // 2 + 1):
        pair = raw * (pltpu.roll(raw, shift, 0) if shift else raw) * scale
        if shift == FEAT // 2:
            pair = pair[: FEAT // 2]
        pair = pair.astype(BF16).astype(F32)
        parts.append(pair * 2.0 if weighted and shift else pair)
    parts.append(raw * FEAT ** (-0.25))
    row = lax.broadcasted_iota(jnp.int32, (8, raw.shape[1]), 0)
    parts.append(jnp.where(row == 0, 1.0, 0.0).astype(F32))
    return jnp.concatenate(parts, axis=0).astype(BF16)


def feature_kernel(conv_ref, halo_ref, *refs):
    count = len(refs) - 5
    head = lax.axis_index("tp")
    places = []
    for turn in range(count // 2):
        source = (head + count - 2 * turn) % count
        places += [source, source ^ 1]
    blocks = refs[:count]
    query_ref, key_ref, value_ref, state_ref, wide = refs[count:]
    width = halo_ref.shape[1]
    local_rows = width * count
    wide[:, :width] = halo_ref[...].astype(F32)
    for index, block in enumerate(blocks):
        start = pl.multiple_of((places[index] + 1) * width, LANES)
        wide[:, pl.ds(start, width)] = block[...].astype(F32)
    padded = wide[...]
    convolved = jnp.zeros((padded.shape[0], local_rows), F32)
    taps = conv_ref[...].T
    for offset in range(taps.shape[1]):
        moved = pltpu.roll(padded, offset, 1) if offset else padded
        convolved += taps[:, offset : offset + 1] * moved[:, width:]
    value = convolved[2 * FEAT :].astype(BF16)
    value_ref[...] = value
    query_ref[...] = convolved[:FEAT]
    key = features(convolved[FEAT : 2 * FEAT], True)
    key_ref[...] = key
    state_ref[:NUM_FEAT, :] = dot_last(key, value)
    total = dot_last(jnp.ones((8, local_rows), BF16), key)
    lanes = state_ref.shape[1]
    rest = NUM_FEAT - lanes
    more = jnp.concatenate([total[:, lanes:], jnp.zeros((8, lanes - rest), F32)], axis=1)
    row = lax.broadcasted_iota(jnp.int32, (8, lanes), 0)
    state_ref[NUM_FEAT:, :] = jnp.where(row == 0, total[:, :lanes], jnp.where(row == 1, more, 0.0))


def inner_kernel(raw_ref, key_ref, value_ref, query_ref, numerator_ref, denominator_ref):
    query_ref[...] = features(raw_ref[...], False).T
    local_rows = query_ref.shape[0]
    width = value_ref.shape[0]
    step = LANES
    for start in range(0, local_rows, step):
        size = start + step
        scores = jnp.dot(query_ref[start:size, :], key_ref[:, :size], preferred_element_type=F32)
        row = lax.broadcasted_iota(jnp.int32, (step, size), 0) + start
        column = lax.broadcasted_iota(jnp.int32, (step, size), 1)
        scores = jnp.where(row >= column, scores, 0.0)
        numerator_ref[start:size, :] = dot_last(scores.astype(BF16), value_ref[:, :size])
        denominator_ref[start:size, :] = jnp.broadcast_to(
            jnp.sum(scores, axis=1, keepdims=True), (step, width)
        )


def finish_kernel(query_ref, numerator_ref, denominator_ref, *refs):
    states, out_ref = refs[:-1], refs[-1]
    state = states[0][...]
    for other in states[1:]:
        state += other[...]
    width = numerator_ref.shape[1]
    query = query_ref[...]
    rest = state[:NUM_FEAT, :]
    parts = []
    for _ in range(3):
        parts.append(rest.astype(BF16))
        rest = rest - parts[-1].astype(F32)
    product = jnp.dot(query, jnp.concatenate(parts, axis=1), preferred_element_type=F32)
    numerator = numerator_ref[...]
    for start in range(0, 3 * width, width):
        numerator += product[:, start : start + width]
    totals = jnp.concatenate(
        [state[NUM_FEAT : NUM_FEAT + 1, :], state[NUM_FEAT + 1 : NUM_FEAT + 2, : NUM_FEAT - width]], axis=1
    )
    denominator = denominator_ref[:, :1] + jnp.sum(query.astype(F32) * totals, axis=1, keepdims=True)
    out_ref[...] = (numerator / denominator).astype(BF16)


def per_device(ctx, tp, tokens, projection, conv_weight):
    both = ("ctx", "tp")
    rows, depth = tokens.shape
    row_width = projection.shape[1]
    val_width = row_width - 2 * FEAT
    local_rows = rows * tp
    turns = range(1, tp // 2)
    me = lax.axis_index("ctx")
    weight = projection.T
    piece = depth // PIECES

    def swap(array, bit):
        return lax.ppermute(array, "ctx", [(i, i ^ bit) for i in range(ctx)])

    mine, last_rows = call(
        pack_kernel,
        [
            jax.ShapeDtypeStruct((row_width, piece), BF16),
            jax.ShapeDtypeStruct((HALO, depth), BF16),
        ],
        [hbm(weight), hbm(tokens)],
        [pltpu.SemaphoreType.DMA((2,))],
        space=HBM,
    )
    pieces = []
    for turn in turns:
        first = lax.ppermute(mine, "tp", [((z + 2 * turn) % tp, z) for z in range(tp)])
        parts = [first] + [swap(first, bits) for bits in (2, 4, 6)]
        pieces += parts + [swap(part, 1) for part in parts]
    paired = lax.ppermute(tokens, "tp", [(z, z ^ 1) for z in range(tp)])

    tail = None
    for z in range(tp):
        pairs = [((c - 1) * tp + tp - 1, c * tp + z) for c in range(1, ctx)]
        part = lax.ppermute(last_rows, both, pairs)
        tail = part if tail is None else tail + part

    shape = jax.ShapeDtypeStruct((row_width, rows), BF16)
    work = 2 * rows * depth * row_width
    halo, own = call(own_kernel, [shape] * 2, [tail, tokens, weight], flops=2 * work)
    early = call(early_kernel, [shape] * len(turns), [tokens] + pieces, flops=work)
    *late, other = call(
        late_kernel, [shape] * (len(turns) + 1), [paired, weight] + pieces, flops=2 * work
    )
    blocks = [own, other]
    for turn, one, two in zip(turns, early, late):
        pairs = [(z, (z + 2 * turn) % tp) for z in range(tp)]
        blocks += [lax.ppermute(one, "tp", pairs), lax.ppermute(two, "tp", pairs)]
    raw, key, value, state = call(
        feature_kernel,
        [
            jax.ShapeDtypeStruct((FEAT, local_rows), F32),
            jax.ShapeDtypeStruct((NUM_FEAT, local_rows), BF16),
            jax.ShapeDtypeStruct((val_width, local_rows), BF16),
            jax.ShapeDtypeStruct((STATE_ROWS, val_width), F32),
        ],
        [conv_weight, halo] + blocks,
        [pltpu.VMEM((row_width, rows + local_rows), F32)],
    )
    query, numerator, denominator = call(
        inner_kernel,
        [jax.ShapeDtypeStruct((local_rows, NUM_FEAT), BF16)]
        + [jax.ShapeDtypeStruct((local_rows, val_width), F32)] * 2,
        [raw, key, value],
        flops=2 * local_rows * local_rows * (NUM_FEAT + val_width),
    )
    received = swap(state, 1)
    terms = [jnp.where(me % 2 == 1, received, 0.0)]
    total = state + received
    bit = 2
    while bit < ctx:
        radix = 2
        last = bit * radix >= ctx
        digit = me // bit % radix
        parts = []
        for delta in range(1, radix):
            pairs = [(c, c ^ delta * bit) for c in range(ctx)]
            parts.append(lax.ppermute(total, "ctx", pairs))
            terms.append(jnp.where(digit > digit ^ delta, parts[-1], 0.0))
        if not last:
            total = functools.reduce(jnp.add, parts, total)
        bit *= radix
    return call(
        finish_kernel,
        [jax.ShapeDtypeStruct((local_rows, val_width), BF16)],
        [query, numerator, denominator] + terms,
        flops=6 * local_rows * NUM_FEAT * val_width,
    )[0]


def solution(mesh):
    ctx, tp = mesh.shape["ctx"], mesh.shape["tp"]
    if tp % 2 or tp < 4 or ctx < 8 or ctx & (ctx - 1):
        raise ValueError("unsupported mesh")

    def body(*arrays):
        return per_device(ctx, tp, *arrays)

    return jax.shard_map(
        body,
        mesh=mesh,
        in_specs=(P(("ctx", "tp"), None), P(None, "tp"), P(None, "tp")),
        out_specs=P("ctx", "tp"),
        check_vma=False,
    )
```

```python
import functools
import math

import jax
import jax.numpy as jnp
from jax import lax
from jax.experimental import pallas as pl
from jax.experimental.pallas import tpu as pltpu
from jax.sharding import PartitionSpec as P


FEAT = 16
HALO = 8
PIECES = 8
LANES = 128
QUAD_FEATS = FEAT * (FEAT + 1) // 2
NUM_FEAT = QUAD_FEATS + FEAT + 8
F32 = jnp.float32
BF16 = jnp.bfloat16
HBM = pl.BlockSpec(memory_space=pltpu.HBM)
VMEM = pl.BlockSpec(memory_space=pltpu.VMEM)
LAST = (((1,), (1,)), ((), ()))


def call(kernel, outs, operands, scratch=(), flops=1 << 20, moved=1 << 20, space=VMEM):
    return pl.pallas_call(
        kernel,
        out_shape=outs,
        in_specs=[space] * len(operands),
        out_specs=[VMEM] * len(outs),
        scratch_shapes=list(scratch),
        compiler_params=pltpu.CompilerParams(vmem_limit_bytes=16 << 20),
        cost_estimate=pl.CostEstimate(flops=flops, bytes_accessed=moved, transcendentals=0),
    )(*operands)


def hbm(array):
    return pltpu.with_memory_space_constraint(array, pltpu.HBM)


def dot_last(left, right):
    return lax.dot_general(left, right, LAST, preferred_element_type=F32)


def own_share():
    return lax.axis_index("ctx") & PIECES - 1


def pack_kernel(weight_ref, tokens_ref, sent_ref, last_ref, sems):
    width = sent_ref.shape[1]
    start = pl.multiple_of(own_share() * width, LANES)
    weights = pltpu.make_async_copy(weight_ref.at[:, pl.ds(start, width)], sent_ref, sems.at[0])
    last = pltpu.make_async_copy(
        tokens_ref.at[tokens_ref.shape[0] - HALO :, :], last_ref, sems.at[1]
    )
    weights.start()
    last.start()
    weights.wait()
    last.wait()


def own_kernel(tail_ref, tokens_ref, weight_ref, halo_ref, own_ref):
    weight = weight_ref[...]
    own_ref[...] = dot_last(weight, tokens_ref[...]).astype(BF16)
    padded = jnp.concatenate(
        [jnp.zeros((halo_ref.shape[1] - HALO, tail_ref.shape[1]), BF16), tail_ref[...]], axis=0
    )
    halo_ref[...] = dot_last(weight, padded).astype(BF16)


def gathered(share, tokens_ref, pieces):
    depth = pieces[0].shape[1]
    total = None
    for index, piece in zip((0, 2, 4, 6, 1, 3, 5, 7), pieces):
        start = pl.multiple_of((share ^ index) * depth, depth)
        part = dot_last(piece[...], tokens_ref[:, pl.ds(start, depth)])
        total = part if total is None else total + part
    return total.astype(BF16)


def early_kernel(tokens_ref, *refs):
    share = own_share()
    count = len(refs) // (PIECES + 1)
    for turn in range(count):
        refs[PIECES * count + turn][...] = gathered(
            share, tokens_ref, refs[PIECES * turn : PIECES * turn + PIECES]
        )


def late_kernel(tokens_ref, weight_ref, *refs):
    share = own_share()
    count = len(refs) // (PIECES + 1)
    for turn in range(count):
        refs[PIECES * count + turn][...] = gathered(
            share, tokens_ref, refs[PIECES * turn : PIECES * turn + PIECES]
        )
    refs[-1][...] = dot_last(weight_ref[...], tokens_ref[...]).astype(BF16)


def features(raw, weighted):
    scale = 1.0 / (math.sqrt(2.0) * math.sqrt(FEAT))
    parts = []
    for shift in range(FEAT // 2 + 1):
        pair = raw * (pltpu.roll(raw, shift, 0) if shift else raw) * scale
        if shift == FEAT // 2:
            pair = pair[: FEAT // 2]
        pair = pair.astype(BF16).astype(F32)
        parts.append(pair * 2.0 if weighted and shift else pair)
    parts.append(raw * FEAT ** (-0.25))
    row = lax.broadcasted_iota(jnp.int32, (8, raw.shape[1]), 0)
    parts.append(jnp.where(row == 0, 1.0, 0.0).astype(F32))
    return jnp.concatenate(parts, axis=0).astype(BF16)


def feature_kernel(conv_ref, halo_ref, *refs):
    count = len(refs) - 5
    head = lax.axis_index("tp")
    places = []
    for turn in range(count // 2):
        source = (head + count - 2 * turn) % count
        places += [source, source ^ 1]
    blocks = refs[:count]
    query_ref, key_ref, value_ref, state_ref, wide = refs[count:]
    width = halo_ref.shape[1]
    local_rows = width * count
    wide[:, :width] = halo_ref[...].astype(F32)
    for index, block in enumerate(blocks):
        start = pl.multiple_of((places[index] + 1) * width, LANES)
        wide[:, pl.ds(start, width)] = block[...].astype(F32)
    padded = wide[...]
    convolved = jnp.zeros((padded.shape[0], local_rows), F32)
    taps = conv_ref[...].T
    for offset in range(taps.shape[1]):
        moved = pltpu.roll(padded, offset, 1) if offset else padded
        convolved += taps[:, offset : offset + 1] * moved[:, width:]
    value = convolved[2 * FEAT :].astype(BF16)
    value_ref[...] = value
    query_ref[...] = convolved[:FEAT]
    key = features(convolved[FEAT : 2 * FEAT], True)
    key_ref[...] = key
    state_ref[...] = dot_last(key, value)
    total = dot_last(jnp.ones((8, local_rows), BF16), key)
    lanes = state_ref.shape[1]
    rest = NUM_FEAT - lanes
    more = jnp.concatenate([total[:, lanes:], jnp.zeros((8, lanes - rest), F32)], axis=1)
    row = lax.broadcasted_iota(jnp.int32, (8, lanes), 0)
    tail = state_ref[NUM_FEAT - 8 :, :]
    state_ref[NUM_FEAT - 8 :, :] = jnp.where(row == 1, total[:, :lanes], jnp.where(row == 2, more, tail))


def inner_kernel(raw_ref, key_ref, value_ref, query_ref, numerator_ref, denominator_ref):
    query_ref[...] = features(raw_ref[...], False).T
    local_rows = query_ref.shape[0]
    width = value_ref.shape[0]
    step = LANES
    for start in range(0, local_rows, step):
        size = start + step
        scores = jnp.dot(query_ref[start:size, :], key_ref[:, :size], preferred_element_type=F32)
        row = lax.broadcasted_iota(jnp.int32, (step, size), 0) + start
        column = lax.broadcasted_iota(jnp.int32, (step, size), 1)
        scores = jnp.where(row >= column, scores, 0.0)
        numerator_ref[start:size, :] = dot_last(scores.astype(BF16), value_ref[:, :size])
        denominator_ref[start:size, :] = jnp.broadcast_to(
            jnp.sum(scores, axis=1, keepdims=True), (step, width)
        )


def finish_kernel(query_ref, numerator_ref, denominator_ref, *refs):
    states, out_ref = refs[:-1], refs[-1]
    state = states[0][...]
    for other in states[1:]:
        state += other[...]
    width = numerator_ref.shape[1]
    query = query_ref[...]
    rest = state
    parts = []
    for _ in range(3):
        parts.append(rest.astype(BF16))
        rest = rest - parts[-1].astype(F32)
    product = jnp.dot(query, jnp.concatenate(parts, axis=1), preferred_element_type=F32)
    numerator = numerator_ref[...]
    for start in range(0, 3 * width, width):
        numerator += product[:, start : start + width]
    totals = jnp.concatenate(
        [state[NUM_FEAT - 7 : NUM_FEAT - 6, :], state[NUM_FEAT - 6 : NUM_FEAT - 5, : NUM_FEAT - width]], axis=1
    )
    denominator = denominator_ref[:, :1] + jnp.sum(query.astype(F32) * totals, axis=1, keepdims=True)
    out_ref[...] = (numerator / denominator).astype(BF16)


def per_device(ctx, tp, tokens, projection, conv_weight):
    both = ("ctx", "tp")
    rows, depth = tokens.shape
    row_width = projection.shape[1]
    val_width = row_width - 2 * FEAT
    local_rows = rows * tp
    turns = range(1, tp // 2)
    me = lax.axis_index("ctx")
    weight = projection.T
    piece = depth // PIECES

    def swap(array, bit):
        return lax.ppermute(array, "ctx", [(i, i ^ bit) for i in range(ctx)])

    mine, last_rows = call(
        pack_kernel,
        [
            jax.ShapeDtypeStruct((row_width, piece), BF16),
            jax.ShapeDtypeStruct((HALO, depth), BF16),
        ],
        [hbm(weight), hbm(tokens)],
        [pltpu.SemaphoreType.DMA((2,))],
        space=HBM,
    )
    pieces = []
    for turn in turns:
        first = lax.ppermute(mine, "tp", [((z + 2 * turn) % tp, z) for z in range(tp)])
        parts = [first] + [swap(first, bits) for bits in (2, 4, 6)]
        pieces += parts + [swap(part, 1) for part in parts]
    paired = lax.ppermute(tokens, "tp", [(z, z ^ 1) for z in range(tp)])

    tail = None
    for z in range(tp):
        pairs = [((c - 1) * tp + tp - 1, c * tp + z) for c in range(1, ctx)]
        part = lax.ppermute(last_rows, both, pairs)
        tail = part if tail is None else tail + part

    shape = jax.ShapeDtypeStruct((row_width, rows), BF16)
    work = 2 * rows * depth * row_width
    halo, own = call(own_kernel, [shape] * 2, [tail, tokens, weight], flops=2 * work)
    early = call(early_kernel, [shape] * len(turns), [tokens] + pieces, flops=work)
    *late, other = call(
        late_kernel, [shape] * (len(turns) + 1), [paired, weight] + pieces, flops=2 * work
    )
    blocks = [own, other]
    for turn, one, two in zip(turns, early, late):
        pairs = [(z, (z + 2 * turn) % tp) for z in range(tp)]
        blocks += [lax.ppermute(one, "tp", pairs), lax.ppermute(two, "tp", pairs)]
    raw, key, value, state = call(
        feature_kernel,
        [
            jax.ShapeDtypeStruct((FEAT, local_rows), F32),
            jax.ShapeDtypeStruct((NUM_FEAT, local_rows), BF16),
            jax.ShapeDtypeStruct((val_width, local_rows), BF16),
            jax.ShapeDtypeStruct((NUM_FEAT, val_width), F32),
        ],
        [conv_weight, halo] + blocks,
        [pltpu.VMEM((row_width, rows + local_rows), F32)],
    )
    query, numerator, denominator = call(
        inner_kernel,
        [jax.ShapeDtypeStruct((local_rows, NUM_FEAT), BF16)]
        + [jax.ShapeDtypeStruct((local_rows, val_width), F32)] * 2,
        [raw, key, value],
        flops=2 * local_rows * local_rows * (NUM_FEAT + val_width),
    )
    received = swap(state, 1)
    terms = [jnp.where(me % 2 == 1, received, 0.0)]
    total = state + received
    bit = 2
    while bit < ctx:
        radix = min(4, ctx // bit)
        last = bit * radix >= ctx
        digit = me // bit % radix
        parts = []
        for delta in range(1, radix):
            pairs = [(c, c ^ delta * bit) for c in range(ctx)]
            parts.append(lax.ppermute(total, "ctx", pairs))
            terms.append(jnp.where(digit > digit ^ delta, parts[-1], 0.0))
        if not last:
            total = functools.reduce(jnp.add, parts, total)
        bit *= radix
    return call(
        finish_kernel,
        [jax.ShapeDtypeStruct((local_rows, val_width), BF16)],
        [query, numerator, denominator] + terms,
        flops=6 * local_rows * NUM_FEAT * val_width,
    )[0]


def solution(mesh):
    ctx, tp = mesh.shape["ctx"], mesh.shape["tp"]
    if tp % 2 or tp < 4 or ctx < 8 or ctx & (ctx - 1):
        raise ValueError("unsupported mesh")

    def body(*arrays):
        return per_device(ctx, tp, *arrays)

    return jax.shard_map(
        body,
        mesh=mesh,
        in_specs=(P(("ctx", "tp"), None), P(None, "tp"), P(None, "tp")),
        out_specs=P("ctx", "tp"),
        check_vma=False,
    )
```

```python
import functools
import math

import jax
import jax.numpy as jnp
from jax import lax
from jax.experimental import pallas as pl
from jax.experimental.pallas import tpu as pltpu
from jax.sharding import PartitionSpec as P


FEAT = 16
HALO = 8
PIECES = 8
LANES = 128
QUAD_FEATS = FEAT * (FEAT + 1) // 2
NUM_FEAT = QUAD_FEATS + FEAT + 8
F32 = jnp.float32
BF16 = jnp.bfloat16
HBM = pl.BlockSpec(memory_space=pltpu.HBM)
VMEM = pl.BlockSpec(memory_space=pltpu.VMEM)
LAST = (((1,), (1,)), ((), ()))


def call(kernel, outs, operands, scratch=(), flops=1 << 20, moved=1 << 20, space=VMEM):
    return pl.pallas_call(
        kernel,
        out_shape=outs,
        in_specs=[space] * len(operands),
        out_specs=[VMEM] * len(outs),
        scratch_shapes=list(scratch),
        compiler_params=pltpu.CompilerParams(vmem_limit_bytes=16 << 20),
        cost_estimate=pl.CostEstimate(flops=flops, bytes_accessed=moved, transcendentals=0),
    )(*operands)


def hbm(array):
    return pltpu.with_memory_space_constraint(array, pltpu.HBM)


def dot_last(left, right):
    return lax.dot_general(left, right, LAST, preferred_element_type=F32)


def own_share():
    return lax.axis_index("ctx") & PIECES - 1


def pack_kernel(weight_ref, tokens_ref, sent_ref, last_ref, sems):
    width = sent_ref.shape[1]
    start = pl.multiple_of(own_share() * width, LANES)
    weights = pltpu.make_async_copy(weight_ref.at[:, pl.ds(start, width)], sent_ref, sems.at[0])
    last = pltpu.make_async_copy(
        tokens_ref.at[tokens_ref.shape[0] - HALO :, :], last_ref, sems.at[1]
    )
    weights.start()
    last.start()
    weights.wait()
    last.wait()


def own_kernel(tail_ref, tokens_ref, paired_ref, weight_ref, halo_ref, own_ref, other_ref):
    weight = weight_ref[...]
    own_ref[...] = dot_last(weight, tokens_ref[...]).astype(BF16)
    other_ref[...] = dot_last(weight, paired_ref[...]).astype(BF16)
    padded = jnp.concatenate(
        [jnp.zeros((halo_ref.shape[1] - HALO, tail_ref.shape[1]), BF16), tail_ref[...]], axis=0
    )
    halo_ref[...] = dot_last(weight, padded).astype(BF16)


def gathered(share, tokens_ref, pieces):
    depth = pieces[0].shape[1]
    total = None
    for index, piece in zip((0, 2, 4, 6, 1, 3, 5, 7), pieces):
        start = pl.multiple_of((share ^ index) * depth, depth)
        part = dot_last(piece[...], tokens_ref[:, pl.ds(start, depth)])
        total = part if total is None else total + part
    return total.astype(BF16)


def other_heads_kernel(tokens_ref, *refs):
    share = own_share()
    count = len(refs) // (PIECES + 1)
    for turn in range(count):
        refs[PIECES * count + turn][...] = gathered(
            share, tokens_ref, refs[PIECES * turn : PIECES * turn + PIECES]
        )


def features(raw, weighted):
    scale = 1.0 / (math.sqrt(2.0) * math.sqrt(FEAT))
    parts = []
    for shift in range(FEAT // 2 + 1):
        pair = raw * (pltpu.roll(raw, shift, 0) if shift else raw) * scale
        if shift == FEAT // 2:
            pair = pair[: FEAT // 2]
        pair = pair.astype(BF16).astype(F32)
        parts.append(pair * 2.0 if weighted and shift else pair)
    parts.append(raw * FEAT ** (-0.25))
    row = lax.broadcasted_iota(jnp.int32, (8, raw.shape[1]), 0)
    parts.append(jnp.where(row == 0, 1.0, 0.0).astype(F32))
    return jnp.concatenate(parts, axis=0).astype(BF16)


def feature_kernel(conv_ref, halo_ref, *refs):
    count = len(refs) - 5
    head = lax.axis_index("tp")
    places = []
    for turn in range(count // 2):
        source = (head + count - 2 * turn) % count
        places += [source, source ^ 1]
    blocks = refs[:count]
    query_ref, key_ref, value_ref, state_ref, wide = refs[count:]
    width = halo_ref.shape[1]
    local_rows = width * count
    wide[:, :width] = halo_ref[...].astype(F32)
    for index, block in enumerate(blocks):
        start = pl.multiple_of((places[index] + 1) * width, LANES)
        wide[:, pl.ds(start, width)] = block[...].astype(F32)
    padded = wide[...]
    convolved = jnp.zeros((padded.shape[0], local_rows), F32)
    taps = conv_ref[...].T
    for offset in range(taps.shape[1]):
        moved = pltpu.roll(padded, offset, 1) if offset else padded
        convolved += taps[:, offset : offset + 1] * moved[:, width:]
    value = convolved[2 * FEAT :].astype(BF16)
    value_ref[...] = value
    query_ref[...] = convolved[:FEAT]
    key = features(convolved[FEAT : 2 * FEAT], True)
    key_ref[...] = key
    state_ref[...] = dot_last(key, value)
    total = dot_last(jnp.ones((8, local_rows), BF16), key)
    lanes = state_ref.shape[1]
    rest = NUM_FEAT - lanes
    more = jnp.concatenate([total[:, lanes:], jnp.zeros((8, lanes - rest), F32)], axis=1)
    row = lax.broadcasted_iota(jnp.int32, (8, lanes), 0)
    tail = state_ref[NUM_FEAT - 8 :, :]
    state_ref[NUM_FEAT - 8 :, :] = jnp.where(row == 1, total[:, :lanes], jnp.where(row == 2, more, tail))


def inner_kernel(raw_ref, key_ref, value_ref, query_ref, numerator_ref, denominator_ref):
    query_ref[...] = features(raw_ref[...], False).T
    local_rows = query_ref.shape[0]
    width = value_ref.shape[0]
    step = LANES
    for start in range(0, local_rows, step):
        size = start + step
        scores = jnp.dot(query_ref[start:size, :], key_ref[:, :size], preferred_element_type=F32)
        row = lax.broadcasted_iota(jnp.int32, (step, size), 0) + start
        column = lax.broadcasted_iota(jnp.int32, (step, size), 1)
        scores = jnp.where(row >= column, scores, 0.0)
        numerator_ref[start:size, :] = dot_last(scores.astype(BF16), value_ref[:, :size])
        denominator_ref[start:size, :] = jnp.broadcast_to(
            jnp.sum(scores, axis=1, keepdims=True), (step, width)
        )


def finish_kernel(query_ref, numerator_ref, denominator_ref, *refs):
    states, out_ref = refs[:-1], refs[-1]
    state = states[0][...]
    for other in states[1:]:
        state += other[...]
    width = numerator_ref.shape[1]
    query = query_ref[...]
    rest = state
    parts = []
    for _ in range(3):
        parts.append(rest.astype(BF16))
        rest = rest - parts[-1].astype(F32)
    product = jnp.dot(query, jnp.concatenate(parts, axis=1), preferred_element_type=F32)
    numerator = numerator_ref[...]
    for start in range(0, 3 * width, width):
        numerator += product[:, start : start + width]
    totals = jnp.concatenate(
        [state[NUM_FEAT - 7 : NUM_FEAT - 6, :], state[NUM_FEAT - 6 : NUM_FEAT - 5, : NUM_FEAT - width]], axis=1
    )
    denominator = denominator_ref[:, :1] + jnp.sum(query.astype(F32) * totals, axis=1, keepdims=True)
    out_ref[...] = (numerator / denominator).astype(BF16)


def per_device(ctx, tp, tokens, projection, conv_weight):
    both = ("ctx", "tp")
    rows, depth = tokens.shape
    row_width = projection.shape[1]
    val_width = row_width - 2 * FEAT
    local_rows = rows * tp
    turns = range(1, tp // 2)
    me = lax.axis_index("ctx")
    weight = projection.T
    piece = depth // PIECES

    def swap(array, bit):
        return lax.ppermute(array, "ctx", [(i, i ^ bit) for i in range(ctx)])

    mine, last_rows = call(
        pack_kernel,
        [
            jax.ShapeDtypeStruct((row_width, piece), BF16),
            jax.ShapeDtypeStruct((HALO, depth), BF16),
        ],
        [hbm(weight), hbm(tokens)],
        [pltpu.SemaphoreType.DMA((2,))],
        space=HBM,
    )
    pieces = []
    for turn in turns:
        first = lax.ppermute(mine, "tp", [((z + 2 * turn) % tp, z) for z in range(tp)])
        parts = [first] + [swap(first, bits) for bits in (2, 4, 6)]
        pieces += parts + [swap(part, 1) for part in parts]
    paired = lax.ppermute(tokens, "tp", [(z, z ^ 1) for z in range(tp)])

    tail = None
    for z in range(tp):
        pairs = [((c - 1) * tp + tp - 1, c * tp + z) for c in range(1, ctx)]
        part = lax.ppermute(last_rows, both, pairs)
        tail = part if tail is None else tail + part

    shape = jax.ShapeDtypeStruct((row_width, rows), BF16)
    work = 2 * rows * depth * row_width
    halo, own, other = call(own_kernel, [shape] * 3, [tail, tokens, paired, weight], flops=3 * work)
    early = call(other_heads_kernel, [shape] * len(turns), [tokens] + pieces, flops=work)
    late = call(other_heads_kernel, [shape] * len(turns), [paired] + pieces, flops=work)
    blocks = [own, other]
    for turn, one, two in zip(turns, early, late):
        pairs = [(z, (z + 2 * turn) % tp) for z in range(tp)]
        blocks += [lax.ppermute(one, "tp", pairs), lax.ppermute(two, "tp", pairs)]
    raw, key, value, state = call(
        feature_kernel,
        [
            jax.ShapeDtypeStruct((FEAT, local_rows), F32),
            jax.ShapeDtypeStruct((NUM_FEAT, local_rows), BF16),
            jax.ShapeDtypeStruct((val_width, local_rows), BF16),
            jax.ShapeDtypeStruct((NUM_FEAT, val_width), F32),
        ],
        [conv_weight, halo] + blocks,
        [pltpu.VMEM((row_width, rows + local_rows), F32)],
    )
    query, numerator, denominator = call(
        inner_kernel,
        [jax.ShapeDtypeStruct((local_rows, NUM_FEAT), BF16)]
        + [jax.ShapeDtypeStruct((local_rows, val_width), F32)] * 2,
        [raw, key, value],
        flops=2 * local_rows * local_rows * (NUM_FEAT + val_width),
    )
    received = swap(state, 1)
    terms = [jnp.where(me % 2 == 1, received, 0.0)]
    total = state + received
    bit = 2
    while bit < ctx:
        radix = min(4, ctx // bit)
        last = bit * radix >= ctx
        digit = me // bit % radix
        parts = []
        for delta in range(1, radix):
            pairs = [(c, c ^ delta * bit) for c in range(ctx)]
            parts.append(lax.ppermute(total, "ctx", pairs))
            terms.append(jnp.where(digit > digit ^ delta, parts[-1], 0.0))
        if not last:
            total = functools.reduce(jnp.add, parts, total)
        bit *= radix
    return call(
        finish_kernel,
        [jax.ShapeDtypeStruct((local_rows, val_width), BF16)],
        [query, numerator, denominator] + terms,
        flops=6 * local_rows * NUM_FEAT * val_width,
    )[0]


def solution(mesh):
    ctx, tp = mesh.shape["ctx"], mesh.shape["tp"]
    if tp % 2 or tp < 4 or ctx < 8 or ctx & (ctx - 1):
        raise ValueError("unsupported mesh")

    def body(*arrays):
        return per_device(ctx, tp, *arrays)

    return jax.shard_map(
        body,
        mesh=mesh,
        in_specs=(P(("ctx", "tp"), None), P(None, "tp"), P(None, "tp")),
        out_specs=P("ctx", "tp"),
        check_vma=False,
    )
```
